256 devices in a mesh: seg: 4 (over y), rank: 64 (over z, x, core).
Axes of the slice: x: 4, y: 4, z: 8, core: 2. Of those that a mesh axis runs over, the one named last changes fastest.
Arguments:
- parent_nodes: float32 [655360, 375], P(('seg', 'rank')), as said below
- marks: int32 [256, 256], P(('seg', 'rank')), may hold values from 0 to 2559, as said below
- child_owner: int32 [524288, 1], P(('seg', 'rank')), may hold values from 0 to 255; in each aligned block of 2048 rows (0 to 2047, 2048 to 4095, ...) at most 16 rows name the same one
- face_link: int32 [1048576, 6], P(('seg', 'rank')), may hold values from 0 to 12287
Outputs:
- node_mass: float32 [125, 1048576], P(None, ('seg', 'rank'))
- face_mass: float32 [150, 1048576], P(None, ('seg', 'rank'))
The draws below stay inside these ranges and needn't reach their ends.
Inputs may be any that keep to these rules, and one draw needn't show every extreme that they name: `marks`: each row holds distinct local parent indices of its device. `child_owner`: among the children of one device no owner is named more than 16 times, a bound that some block reaches. `face_link`: the first 4096 values name slots of the previous owner along rank, the next 4096 own slots, the last 4096 slots of the next owner. `parent_nodes`: nodes of a slightly perturbed cube of side 3 to 6 around a point of the box from -8 to 8.
All inputs are finite; a program needn't handle non-finite values.
Results may differ from the reference program's by a relative error of at most 0.0003.
Values sent between devices are 32-bit elements; how exact they have to be, the bound alone decides.
No kernel may reach another device: no remote copies, remote signals or barrier semaphores. Data moves between devices by JAX's collectives and lax.ppermute only.
A program may use at most 192 MiB of HBM per device.

```python
import math
import jax
import jax.numpy as jnp
import numpy as np
from jax import lax

ELEM_DEV = 2560
MARKED = 256
KIDS = 2048
CAP = 16
SLOTS = 4096
ELEMS = 655360
KIDS_ALL = 524288
SLOTS_ALL = 1048576
N_SEG = 4
N_RANK = 64


def draw_parent_nodes(key, part):
    points = np.array([-1.0, -math.sqrt(3.0 / 7.0), 0.0, math.sqrt(3.0 / 7.0), 1.0])
    lattice = np.zeros((3, 125))
    for i in range(5):
        for j in range(5):
            for k in range(5):
                lattice[0, i * 25 + j * 5 + k] = points[i]
                lattice[1, i * 25 + j * 5 + k] = points[j]
                lattice[2, i * 25 + j * 5 + k] = points[k]
    first_key, second_key, third_key = jax.random.split(key, 3)
    centre = jax.random.uniform(first_key, (ELEMS, 3, 1), jnp.float32, -8.0, 8.0)
    side = jnp.exp(jax.random.uniform(second_key, (ELEMS, 1, 1), jnp.float32, math.log(3.0), math.log(6.0)))
    jitter = 0.03 * jax.random.normal(third_key, (ELEMS, 3, 125), jnp.float32)
    nodes = centre + side * (0.5 * jnp.asarray(lattice, jnp.float32)[None] + jitter)
    return nodes.reshape(ELEMS, 375).astype(jnp.float32)


def draw_marks(key, part):
    devices = ELEMS // ELEM_DEV
    keys = jax.random.split(jax.random.fold_in(key, 17), devices)
    chosen = jax.vmap(lambda k: jax.random.permutation(k, ELEM_DEV)[:MARKED])(keys)
    return chosen.astype(jnp.int32)


def set_ends(values, own_key, smallest, high):
    shape = values.shape
    place = [jax.random.randint(jax.random.fold_in(own_key, axis), (), 0, shape[axis]) for axis in range(len(shape))]
    values = values.at[tuple(place)].set(smallest)
    longest = shape.index(max(shape))
    place[longest] = (place[longest] + 1) % shape[longest]
    return values.at[tuple(place)].set(high)


def routed_block(rng, own, number, rows, count, top, limit, skew):
    order = jax.random.permutation(rng, count)
    heavy_load, usual = portions_of(count, rows * top, limit, skew, True), portions_of(count, rows * top, limit, skew, False)
    places = jnp.arange(count)

    def named(sizes, rotation):
        used = int((sizes > 0).sum())
        fixed = max(1, used // 4)
        shifted = fixed + (places - fixed + rotation * (used - fixed)) % max(1, count - fixed)
        return jnp.zeros((count,), jnp.int32).at[order[jnp.where(places < fixed, places, shifted)]].set(jnp.asarray(sizes, jnp.int32))

    sizes = jnp.where(number % 4 == 0, named(heavy_load, number // 4), named(usual, number - number // 4 - 1))
    mixed = jax.random.permutation(jax.random.fold_in(own, 3), count)
    donor, receiver = mixed[0:count // 2 * 2:2], mixed[1:count // 2 * 2:2]
    room = jnp.minimum(sizes[donor] - 1, limit - sizes[receiver]) // 2
    room = jnp.where((donor == order[0]) | (receiver == order[0]) | (sizes[receiver] == 0), 0, jnp.maximum(room, 0))
    shifted = jax.random.randint(jax.random.fold_in(own, 4), (count // 2,), 0, 1 << 20) % (room + 1)
    sizes = sizes.at[donor].add(-shifted).at[receiver].add(shifted)
    labels = jnp.searchsorted(jnp.cumsum(sizes), jnp.arange(rows * top), side="right").astype(jnp.int32)
    table = labels.reshape(top, rows).T
    table = table[jax.random.permutation(jax.random.fold_in(own, 1), rows)]
    rotation = jax.random.randint(jax.random.fold_in(own, 2), (rows, 1), 0, top)
    return jnp.take_along_axis(table, (jnp.arange(top)[None, :] + rotation) % top, axis=1)


def portions_of(count, total, bound, slope, full):
    weights = [(1 << 20) // math.isqrt(grade ** slope) + 1 for grade in range(1, count + 1)]
    largest = bound if full else min(bound, max(-(-total // count), total * weights[0] // sum(weights)))
    least = 1 if total - largest >= count - 1 else 0
    holding, rest = [largest] + [least] * (count - 1), total - largest - least * (count - 1)
    while rest > 0:
        candidates = [i for i in range(1, count) if holding[i] < largest] or [i for i in range(1, count) if holding[i] < bound]
        whole, left = sum([weights[i] for i in candidates]), rest
        for i in candidates:
            addition = min(bound - holding[i], max(1, left * weights[i] // whole), rest)
            holding[i] = holding[i] + addition
            rest = rest - addition
    return np.array(holding)


def setup_inputs(seed: int = 0) -> dict:
    key_of = jax.random.split(jax.random.key(seed), 5)
    parent_nodes = draw_parent_nodes(jax.random.fold_in(key_of[4], 71), 0)
    marks = draw_marks(jax.random.fold_in(key_of[4], 71), 0)
    child_owner_keys = jax.random.split(jax.random.fold_in(key_of[2], 1), KIDS_ALL // KIDS)
    child_owner_turns = jax.random.permutation(jax.random.fold_in(key_of[2], 3), KIDS_ALL // KIDS)
    child_owner = jax.vmap(lambda own, number: routed_block(jax.random.fold_in(key_of[2], 2), own, number, KIDS, N_SEG * N_RANK, 1, CAP, 2))(child_owner_keys, child_owner_turns).reshape((KIDS_ALL, 1))
    face_link = set_ends(jax.random.randint(key_of[3], (SLOTS_ALL, 6), 0, 3 * SLOTS), jax.random.fold_in(key_of[3], 1), 0, (3 * SLOTS) - 1).astype(jnp.int32)
    return {"parent_nodes": parent_nodes, "marks": marks, "child_owner": child_owner, "face_link": face_link}


def gll_tables():
    points = np.array([-1.0, -math.sqrt(3.0 / 7.0), 0.0, math.sqrt(3.0 / 7.0), 1.0])
    weights = np.array([0.1, 49.0 / 90.0, 32.0 / 45.0, 49.0 / 90.0, 0.1])
    barycentric = np.array([1.0 / np.prod([points[j] - points[m] for m in range(5) if m != j]) for j in range(5)])
    slopes = np.zeros((5, 5))
    for i in range(5):
        for j in range(5):
            if i != j:
                slopes[i, j] = barycentric[j] / barycentric[i] / (points[i] - points[j])
        slopes[i, i] = -np.sum(slopes[i])

    def lagrange_at(where):
        table = np.ones((5, 5))
        for a in range(5):
            for j in range(5):
                for m in range(5):
                    if m != j:
                        table[a, j] *= (where[a] - points[m]) / (points[j] - points[m])
        return table

    def blend(value, side):
        return (1.0 - value) / 2.0 if side == 0 else (1.0 + value) / 2.0

    def flat(i, j, k):
        return i * 25 + j * 5 + k
    ends = (0, 4)
    gordon = np.zeros((125, 125))
    for i in range(5):
        for j in range(5):
            for k in range(5):
                r, s, t = (points[i], points[j], points[k])
                target = flat(i, j, k)
                for a in range(2):
                    gordon[target, flat(ends[a], j, k)] += blend(r, a)
                    gordon[target, flat(i, ends[a], k)] += blend(s, a)
                    gordon[target, flat(i, j, ends[a])] += blend(t, a)
                    for b in range(2):
                        gordon[target, flat(ends[a], ends[b], k)] -= blend(r, a) * blend(s, b)
                        gordon[target, flat(ends[a], j, ends[b])] -= blend(r, a) * blend(t, b)
                        gordon[target, flat(i, ends[a], ends[b])] -= blend(s, a) * blend(t, b)
                        for c in range(2):
                            gordon[target, flat(ends[a], ends[b], ends[c])] += blend(r, a) * blend(s, b) * blend(t, c)
    children = np.zeros((8, 125, 125))
    for octant in range(8):
        shifts = [2 * (octant >> 2 & 1) - 1, 2 * (octant >> 1 & 1) - 1, 2 * (octant & 1) - 1]
        tables = [lagrange_at((points + shifts[q]) / 2.0) for q in range(3)]
        children[octant] = np.kron(np.kron(tables[0], tables[1]), tables[2]) @ gordon
    identity = np.eye(5)
    derivs = [np.kron(np.kron(slopes, identity), identity), np.kron(np.kron(identity, slopes), identity), np.kron(np.kron(identity, identity), slopes)]
    deriv_table = np.concatenate([derivs[q].T for q in range(3)], axis=1)
    mass_weights = np.kron(np.kron(weights, weights), weights)
    face_weights = np.kron(weights, weights)
    face_nodes = []
    for side in (0, 4):
        face_nodes.append([flat(side, j, k) for j in range(5) for k in range(5)])
    face_nodes = [face_nodes[0], face_nodes[1]]
    for side in (0, 4):
        face_nodes.append([flat(i, side, k) for i in range(5) for k in range(5)])
    for side in (0, 4):
        face_nodes.append([flat(i, j, side) for i in range(5) for j in range(5)])
    tangents = [(1, 2), (1, 2), (0, 2), (0, 2), (0, 1), (0, 1)]
    boundary = [flat(i, j, k) for i in range(5) for j in range(5) for k in range(5) if i in ends or j in ends or k in ends]
    children_map = children.transpose(2, 0, 1).reshape(125, 1000)
    return (children_map, deriv_table, mass_weights, face_weights, np.array(face_nodes), tangents, np.array(boundary))

def geometry(coords, tables):
    children_map, deriv_table, mass_weights, face_weights, face_nodes, tangents, boundary = tables
    width = coords.shape[0]
    deriv = jnp.dot(coords.reshape(width * 3, 125), jnp.asarray(deriv_table, jnp.float32), precision=lax.Precision.HIGHEST, preferred_element_type=jnp.float32).reshape(width, 3, 3, 125)
    jac = [[deriv[:, c, d, :] for d in range(3)] for c in range(3)]
    determinant = jac[0][0] * (jac[1][1] * jac[2][2] - jac[1][2] * jac[2][1]) - jac[0][1] * (jac[1][0] * jac[2][2] - jac[1][2] * jac[2][0]) + jac[0][2] * (jac[1][0] * jac[2][1] - jac[1][1] * jac[2][0])
    mass = determinant * jnp.asarray(mass_weights, jnp.float32)
    areas = []
    for face in range(6):
        first, second = tangents[face]
        nodes = face_nodes[face]
        along = deriv[:, :, first, :][:, :, nodes]
        across = deriv[:, :, second, :][:, :, nodes]
        normal_x = along[:, 1] * across[:, 2] - along[:, 2] * across[:, 1]
        normal_y = along[:, 2] * across[:, 0] - along[:, 0] * across[:, 2]
        normal_z = along[:, 0] * across[:, 1] - along[:, 1] * across[:, 0]
        length = jnp.sqrt(normal_x * normal_x + normal_y * normal_y + normal_z * normal_z)
        areas.append(length * jnp.asarray(face_weights, jnp.float32))
    return (mass, jnp.stack(areas, axis=1).reshape(width, 150))

def reference(parent_nodes, marks, child_owner, face_link):
    tables = gll_tables()
    devices = N_SEG * N_RANK
    children_map = jnp.asarray(tables[0], jnp.float32)
    rows = (jnp.arange(devices, dtype=jnp.int32)[:, None] * ELEM_DEV + marks).reshape(-1)
    picked = parent_nodes[rows].reshape(devices * MARKED * 3, 125)
    made = jnp.dot(picked, children_map, precision=lax.Precision.HIGHEST, preferred_element_type=jnp.float32)
    made = made.reshape(devices * MARKED, 3, 8, 125).transpose(0, 2, 1, 3).reshape(devices * KIDS, 375)
    owners = child_owner[:, 0].reshape(devices, KIDS)

    def rank_slots(row):
        onehot = (row[:, None] == jnp.arange(devices, dtype=jnp.int32)[None, :]).astype(jnp.int32)
        return lax.optimization_barrier(jnp.sum(jnp.cumsum(onehot, axis=0) * onehot, axis=1)) - 1
    positions = lax.map(rank_slots, owners)
    sources = jnp.arange(devices, dtype=jnp.int32)[:, None]
    target = (owners * SLOTS + sources * CAP + positions).reshape(-1)
    received = jnp.zeros((devices * SLOTS, 375), jnp.float32).at[target].set(made)
    mass, faces = lax.map(lambda block: geometry(block, tables), received.reshape(devices, SLOTS, 375))
    faces_flat = faces.reshape(devices * SLOTS * 6, 25)
    links = face_link.reshape(N_SEG, N_RANK, SLOTS, 6)
    rank_pos = jnp.arange(N_RANK, dtype=jnp.int32)[None, :, None, None]
    seg_pos = jnp.arange(N_SEG, dtype=jnp.int32)[:, None, None, None]
    source_rank = rank_pos + links // SLOTS - 1
    valid = (source_rank >= 0) & (source_rank < N_RANK)
    owner_of = seg_pos * N_RANK + jnp.clip(source_rank, 0, N_RANK - 1)
    faces_idx = jnp.arange(6, dtype=jnp.int32)
    opposite = faces_idx // 2 * 2 + 1 - faces_idx % 2
    index = ((owner_of * SLOTS + links % SLOTS) * 6 + opposite[None, None, None, :]).reshape(-1)
    fetched = faces_flat[index].reshape(devices * SLOTS, 6, 25)
    fetched = jnp.where(valid.reshape(devices * SLOTS, 6, 1), fetched, jnp.zeros_like(fetched))
    face_total = faces.reshape(devices * SLOTS, 6, 25) + fetched
    return (mass.reshape(devices * SLOTS, 125).T, face_total.reshape(devices * SLOTS, 150).T)
```

```python
import functools
import math

import jax
import jax.numpy as jnp
import numpy as np
from jax import lax
from jax.experimental import pallas as pl
from jax.experimental.pallas import tpu as pltpu
from jax.sharding import PartitionSpec as P

F32 = jnp.float32
BF16 = jnp.bfloat16
GROUPS = 8
FACE_ROWS = 19
FACE_PAD = 24
MASS_ROWS = 16
FACES = GROUPS * FACE_PAD
MASS = GROUPS * MASS_ROWS
CHUNK = 36


def shifted(array, axis, by):
    count = lax.axis_size(axis)
    pairs = [(i, i + by) for i in range(count) if 0 <= i + by < count]
    return lax.ppermute(array, axis, pairs)


def gll_tables():
    points = np.array([-1.0, -math.sqrt(3.0 / 7.0), 0.0, math.sqrt(3.0 / 7.0), 1.0])
    weights = np.array([0.1, 49.0 / 90.0, 32.0 / 45.0, 49.0 / 90.0, 0.1])
    barycentric = np.array(
        [1.0 / np.prod([points[j] - points[m] for m in range(5) if m != j]) for j in range(5)]
    )
    slopes = np.zeros((5, 5))
    for i in range(5):
        for j in range(5):
            if i != j:
                slopes[i, j] = barycentric[j] / barycentric[i] / (points[i] - points[j])
        slopes[i, i] = -np.sum(slopes[i])

    def lagrange_at(where):
        table = np.ones((5, 5))
        for a in range(5):
            for j in range(5):
                for m in range(5):
                    if m != j:
                        table[a, j] *= (where[a] - points[m]) / (points[j] - points[m])
        return table

    def blend(value, side):
        return (1.0 - value) / 2.0 if side == 0 else (1.0 + value) / 2.0

    def flat(i, j, k):
        return i * 25 + j * 5 + k

    ends = (0, 4)
    gordon = np.zeros((125, 125))
    for i in range(5):
        for j in range(5):
            for k in range(5):
                r, s, t = (points[i], points[j], points[k])
                target = flat(i, j, k)
                for a in range(2):
                    gordon[target, flat(ends[a], j, k)] += blend(r, a)
                    gordon[target, flat(i, ends[a], k)] += blend(s, a)
                    gordon[target, flat(i, j, ends[a])] += blend(t, a)
                    for b in range(2):
                        gordon[target, flat(ends[a], ends[b], k)] -= blend(r, a) * blend(s, b)
                        gordon[target, flat(ends[a], j, ends[b])] -= blend(r, a) * blend(t, b)
                        gordon[target, flat(i, ends[a], ends[b])] -= blend(s, a) * blend(t, b)
                        for c in range(2):
                            gordon[target, flat(ends[a], ends[b], ends[c])] += (
                                blend(r, a) * blend(s, b) * blend(t, c)
                            )
    children = np.zeros((8, 125, 125))
    for octant in range(8):
        shifts = [2 * (octant >> 2 & 1) - 1, 2 * (octant >> 1 & 1) - 1, 2 * (octant & 1) - 1]
        tables = [lagrange_at((points + shifts[q]) / 2.0) for q in range(3)]
        children[octant] = np.kron(np.kron(tables[0], tables[1]), tables[2]) @ gordon
    identity = np.eye(5)
    derivs = [
        np.kron(np.kron(slopes, identity), identity),
        np.kron(np.kron(identity, slopes), identity),
        np.kron(np.kron(identity, identity), slopes),
    ]
    deriv_table = np.concatenate([derivs[q].T for q in range(3)], axis=1)
    mass_weights = np.kron(np.kron(weights, weights), weights)
    face_weights = np.kron(weights, weights)
    tangents = [(1, 2), (1, 2), (0, 2), (0, 2), (0, 1), (0, 1)]
    boundary = [
        flat(i, j, k)
        for i in range(5)
        for j in range(5)
        for k in range(5)
        if i in ends or j in ends or k in ends
    ]
    children_map = children.transpose(2, 0, 1).reshape(125, 1000)
    return (children_map, deriv_table, mass_weights, face_weights, tangents, np.array(boundary))


def split(value, parts):
    pieces = []
    for _ in range(parts):
        piece = value.astype(BF16)
        pieces.append(piece)
        value = value - piece.astype(F32)
    return pieces


def flipped(blocks):
    lanes = lax.broadcasted_iota(jnp.int32, blocks[0].shape, 1) // (128 // GROUPS)
    blocks = list(blocks)
    for bit in (1, 2, 4):
        low = (lanes & bit) == 0
        step = bit * (128 // GROUPS)
        for i in range(GROUPS):
            if i & bit == 0:
                a, c = blocks[i], blocks[i | bit]
                blocks[i] = jnp.where(low, a, pltpu.roll(c, step, 1))
                blocks[i | bit] = jnp.where(low, pltpu.roll(a, 128 - step, 1), c)
    return blocks


def face_order():
    return [25 * f + p for f in range(6) for p in range(24)] + [25 * f + 24 for f in range(6)]


def constants():
    children_map, deriv_table, mass_weights, face_weights, tangents, _ = gll_tables()
    child = np.zeros((8, 128, 128))
    child[:, :125, :125] = children_map.reshape(125, 8, 125).transpose(1, 2, 0)
    derivs = deriv_table.reshape(125, 3, 125).transpose(1, 2, 0)
    grid = np.arange(125).reshape(5, 5, 5)
    rows = np.zeros((2 * FACES + 3 * MASS, 128))
    face_scale = np.zeros((FACES, 1))
    for face in range(6):
        nodes = np.take(grid, 0 if face % 2 == 0 else 4, axis=face // 2).reshape(-1)
        for p in range(25):
            n = 24 * face + p if p < 24 else 144 + face
            at = n // FACE_ROWS * FACE_PAD + n % FACE_ROWS
            rows[at, :125] = derivs[tangents[face][0]][nodes[p]]
            rows[FACES + at, :125] = derivs[tangents[face][1]][nodes[p]]
            face_scale[at, 0] = face_weights[p]
    mass_scale = np.zeros((MASS, 1))
    mass_scale[:125, 0] = mass_weights
    for d in range(3):
        start = 2 * FACES + d * MASS
        rows[start : start + 125, :125] = derivs[d]
    as32 = lambda a: jnp.asarray(a, F32)
    return as32(child.reshape(1024, 128)), as32(rows), as32(np.concatenate([face_scale, mass_scale]))


def source_kernel(
    capacity, nodes_ref, marks_ref, owner_ref, child_ref, rows_ref, scale_ref, out_ref,
    pick_ref, x_ref, cc_ref, dd_ref, deriv_ref, vals_ref, natural_ref, target_ref, onehot_ref, y_ref,
):
    elements = nodes_ref.shape[1]
    marked = marks_ref.shape[1]
    kids = 8 * marked
    devices = out_ref.shape[0] // CHUNK * pl.num_programs(0)

    @pl.when(pl.program_id(0) == 0)
    def _():
        pick_ref[...] = jnp.zeros_like(pick_ref)
        marks = marks_ref[...]

        def pick(k, carry):
            start = pl.multiple_of(k * 256, 256)
            where = lax.broadcasted_iota(jnp.int32, (256, marked), 0) + start
            chosen = jnp.where(where == marks, 1.0, 0.0).astype(BF16)
            for piece in split(nodes_ref[:, pl.ds(start, 256)], 3):
                pick_ref[0:375, :] += jnp.dot(piece, chosen, preferred_element_type=F32)
            return carry

        lax.fori_loop(0, elements // 256, pick, 0)
        for c in range(3):
            x = pick_ref[125 * c : 125 * c + 128, :]
            x = x - 0.5 * (x[0:1] + x[124:125])
            a1, a2, a3 = split(x, 3)
            for k, piece in enumerate((a1, a2, a1, a3, a2, a1)):
                x_ref[128 * k : 128 * k + 128, c * marked : (c + 1) * marked] = piece
        c1, c2, c3 = split(child_ref[...], 3)
        for k, piece in enumerate((c1, c1, c2, c1, c2, c3)):
            cc_ref[:, 128 * k : 128 * k + 128] = piece
        d1, d2 = split(rows_ref[...], 2)
        for k, piece in enumerate((d1, d1, d2, d2)):
            dd_ref[:, 128 * k : 128 * k + 128] = piece

        def octant(o, carry):
            coords = jnp.dot(
                cc_ref[pl.ds(pl.multiple_of(o * 128, 128), 128), :], x_ref[...], preferred_element_type=F32
            )
            y1, y2 = split(coords - coords[62:63], 2)
            deriv_ref[...] = jnp.dot(
                dd_ref[...], jnp.concatenate([y1, y2, y1, y2], axis=0), preferred_element_type=F32
            )
            lanes = pl.ds(pl.multiple_of(o * marked, 128), marked)

            def put(row, value):
                v1, v2 = split(value, 2)
                vals_ref[pl.ds(row, 16), lanes] = v1
                vals_ref[pl.ds(FACES + MASS + row, 16), lanes] = v2

            def face_block(i, carry):
                row = pl.multiple_of(i * 16, 16)
                u = [deriv_ref[pl.ds(row, 16), c * marked : (c + 1) * marked] for c in range(3)]
                v = [deriv_ref[pl.ds(FACES + row, 16), c * marked : (c + 1) * marked] for c in range(3)]
                nx = u[1] * v[2] - u[2] * v[1]
                ny = u[2] * v[0] - u[0] * v[2]
                nz = u[0] * v[1] - u[1] * v[0]
                put(row, jnp.sqrt(nx * nx + ny * ny + nz * nz) * scale_ref[pl.ds(row, 16), :])
                return carry

            def mass_block(i, carry):
                row = pl.multiple_of(i * 16, 16)
                j = [
                    [
                        deriv_ref[pl.ds(2 * FACES + d * MASS + row, 16), c * marked : (c + 1) * marked]
                        for d in range(3)
                    ]
                    for c in range(3)
                ]
                determinant = (
                    j[0][0] * (j[1][1] * j[2][2] - j[1][2] * j[2][1])
                    - j[0][1] * (j[1][0] * j[2][2] - j[1][2] * j[2][0])
                    + j[0][2] * (j[1][0] * j[2][1] - j[1][1] * j[2][0])
                )
                put(FACES + row, determinant * scale_ref[pl.ds(FACES + row, 16), :])
                return carry

            lax.fori_loop(0, FACES // 16, face_block, 0)
            lax.fori_loop(0, MASS // 16, mass_block, 0)
            return carry

        lax.fori_loop(0, 8, octant, 0)

        owner_rows = lax.broadcasted_iota(jnp.int32, (devices, 128), 0)
        earlier = lax.broadcasted_iota(jnp.int32, (128, 128), 0) < lax.broadcasted_iota(jnp.int32, (128, 128), 1)
        earlier = jnp.where(earlier, 1.0, 0.0).astype(BF16)
        ones = jnp.ones((128, 128), BF16)

        def slots(b, seen):
            owner = owner_ref[pl.ds(b, 1), :]
            same = owner_rows == owner
            same_b = jnp.where(same, 1.0, 0.0).astype(BF16)
            before = jnp.dot(same_b, earlier, preferred_element_type=F32) + seen
            position = jnp.sum(jnp.where(same, before, 0.0), axis=0, keepdims=True)
            target = owner.astype(F32) * capacity + position
            target = jnp.broadcast_to(target, (128, 128)).T
            natural_ref[pl.ds(pl.multiple_of(b * 128, 128), 128), :] = target.astype(jnp.int32)
            return seen + jnp.dot(same_b, ones, preferred_element_type=F32)

        lax.fori_loop(0, kids // 128, slots, jnp.zeros((devices, 128), F32))
        for o in range(8):
            target_ref[o * marked : (o + 1) * marked, :] = natural_ref[pl.ds(o, marked, stride=8), :]

    columns = lax.broadcasted_iota(jnp.int32, (128, 128), 1) + pl.program_id(0) * 256

    def fill(i, carry):
        rows = pl.ds(pl.multiple_of(i * 128, 128), 128)
        target = target_ref[rows, :]
        onehot_ref[rows, 0:128] = jnp.where(target == columns, 1.0, 0.0).astype(BF16)
        onehot_ref[rows, 128:256] = jnp.where(target == columns + 128, 1.0, 0.0).astype(BF16)
        return carry

    lax.fori_loop(0, kids // 128, fill, 0)
    moved = jnp.dot(vals_ref[...], onehot_ref[...], preferred_element_type=F32)
    y_ref[...] = moved[0 : FACES + MASS] + moved[FACES + MASS :]
    for tile in range(2):
        lanes = slice(128 * tile, 128 * tile + 128)
        faces = flipped([y_ref[FACE_PAD * g : FACE_PAD * (g + 1), lanes] for g in range(GROUPS)])
        masses = flipped(
            [y_ref[FACES + MASS_ROWS * g : FACES + MASS_ROWS * (g + 1), lanes] for g in range(GROUPS)]
        )
        for j in range(GROUPS):
            start = CHUNK * (GROUPS * tile + j)
            out_ref[start : start + MASS_ROWS, :] = masses[j]
            out_ref[start + MASS_ROWS : start + MASS_ROWS + FACE_ROWS, :] = faces[j][0:FACE_ROWS]
            out_ref[start + MASS_ROWS + FACE_ROWS : start + CHUNK, :] = jnp.zeros(
                (CHUNK - MASS_ROWS - FACE_ROWS, 128), F32
            )


def make_outgoing(nodes, marks, owner, devices, capacity):
    marked = marks.shape[1]
    kids = 8 * marked
    child, rows, scale = constants()
    slots = devices * capacity
    whole = lambda a: pl.BlockSpec(a.shape, lambda i: (0, 0))
    operands = (nodes, marks, owner, child, rows, scale)
    height = FACES + MASS
    return pl.pallas_call(
        functools.partial(source_kernel, capacity),
        out_shape=jax.ShapeDtypeStruct((devices * CHUNK, 128), F32),
        grid=(slots // 256,),
        in_specs=[whole(a) for a in operands],
        out_specs=pl.BlockSpec((2 * GROUPS * CHUNK, 128), lambda i: (i, 0)),
        scratch_shapes=[
            pltpu.VMEM((384, marked), F32),
            pltpu.VMEM((768, 3 * marked), BF16),
            pltpu.VMEM((1024, 768), BF16),
            pltpu.VMEM((rows.shape[0], 512), BF16),
            pltpu.VMEM((rows.shape[0], 3 * marked), F32),
            pltpu.VMEM((2 * height, kids), BF16),
            pltpu.VMEM((kids, 128), jnp.int32),
            pltpu.VMEM((kids, 128), jnp.int32),
            pltpu.VMEM((kids, 256), BF16),
            pltpu.VMEM((height, 256), F32),
        ],
        compiler_params=pltpu.CompilerParams(vmem_limit_bytes=48 << 20),
        name="source",
    )(*operands)


def unpack_kernel(in_ref, mass_ref, faces_ref):
    for tile in range(2):
        lanes = slice(128 * tile, 128 * tile + 128)
        starts = [CHUNK * (GROUPS * tile + j) for j in range(GROUPS)]
        masses = flipped([in_ref[s : s + MASS_ROWS, :] for s in starts])
        for g in range(GROUPS):
            count = min(MASS_ROWS, 125 - MASS_ROWS * g)
            mass_ref[MASS_ROWS * g : MASS_ROWS * g + count, lanes] = masses[g][0:count]
        faces = flipped([in_ref[s + MASS_ROWS : s + MASS_ROWS + FACE_ROWS, :] for s in starts])
        for g in range(GROUPS):
            count = min(FACE_ROWS, 150 - FACE_ROWS * g)
            faces_ref[FACE_ROWS * g : FACE_ROWS * g + count, lanes] = faces[g][0:count]


def unpack(arrived, slots):
    return pl.pallas_call(
        unpack_kernel,
        out_shape=(jax.ShapeDtypeStruct((125, slots), F32), jax.ShapeDtypeStruct((150, slots), F32)),
        grid=(slots // 256,),
        in_specs=[pl.BlockSpec((2 * GROUPS * CHUNK, 128), lambda i: (i, 0))],
        out_specs=(pl.BlockSpec((125, 256), lambda i: (0, i)), pl.BlockSpec((150, 256), lambda i: (0, i))),
        name="unpack",
    )(arrived)


def collect_kernel(link_ref, before_ref, faces_ref, after_ref, out_ref, table_ref, tail_ref):
    sources = (before_ref, faces_ref, after_ref)
    per_source = faces_ref.shape[1] // 256
    tiles = 3 * per_source
    body_rows = 24 * tiles

    @pl.when(pl.program_id(0) == 0)
    def _():
        for f in range(6):
            other = f + 1 - 2 * (f % 2)
            for k, source in enumerate(sources):

                def pair(i, carry):
                    lanes = [pl.ds(pl.multiple_of(512 * i + 256 * e, 256), 256) for e in range(2)]
                    values = jnp.concatenate([source[24 * other : 24 * other + 24, l] for l in lanes], axis=0)
                    row = pl.multiple_of(24 * per_source * k + 48 * i, 16)
                    for part, piece in enumerate(split(values, 2)):
                        table_ref[f, pl.ds(row, 48), 256 * part : 256 * part + 256] = piece
                    for e in range(2):
                        tail_ref[pl.ds(per_source * k + 2 * i + e, 1), :] = source[
                            144 + other : 145 + other, lanes[e]
                        ]
                    return carry

                lax.fori_loop(0, per_source // 2, pair, 0)
            for part, piece in enumerate(split(tail_ref[...], 2)):
                table_ref[f, body_rows : body_rows + tiles, 256 * part : 256 * part + 256] = piece

    here = pl.ds(pl.multiple_of(pl.program_id(0) * 256, 256), 256)
    for f in range(6):
        link = link_ref[f : f + 1, here]
        low, high = link & 255, link >> 8
        chosen = jnp.where(lax.broadcasted_iota(jnp.int32, (256, 256), 0) == low, 1.0, 0.0).astype(BF16)
        found = jnp.dot(table_ref[f], jnp.concatenate([chosen, chosen], axis=0), preferred_element_type=F32)
        high24 = jnp.broadcast_to(high, (24, 256))
        picked = jnp.zeros((24, 256), F32)
        for h in range(tiles):
            picked = jnp.where(high24 == h, found[24 * h : 24 * h + 24], picked)
        last = jnp.where(lax.broadcasted_iota(jnp.int32, (tiles, 256), 0) == high, found[body_rows:], 0.0)
        out_ref[25 * f : 25 * f + 24, :] = faces_ref[24 * f : 24 * f + 24, here] + picked
        out_ref[25 * f + 24 : 25 * f + 25, :] = faces_ref[144 + f : 145 + f, here] + jnp.sum(
            last, axis=0, keepdims=True
        )


def collect(before, faces, after, links):
    slots = faces.shape[1]
    tiles = 3 * slots // 256
    whole = lambda a: pl.BlockSpec(a.shape, lambda i: (0, 0))
    operands = (links, before, faces, after)
    return pl.pallas_call(
        collect_kernel,
        out_shape=jax.ShapeDtypeStruct((150, slots), F32),
        grid=(slots // 256,),
        in_specs=[whole(a) for a in operands],
        out_specs=pl.BlockSpec((150, 256), lambda i: (0, i)),
        scratch_shapes=[pltpu.VMEM((6, 25 * tiles, 512), BF16), pltpu.VMEM((tiles, 256), F32)],
        compiler_params=pltpu.CompilerParams(vmem_limit_bytes=48 << 20),
        name="collect",
    )(*operands)


def body(parent_nodes, marks, child_owner, face_link):
    devices = lax.axis_size("seg") * lax.axis_size("rank")
    kids = child_owner.shape[0]
    capacity = max(2, 2 * kids // devices)
    slots = devices * capacity
    outgoing = make_outgoing(parent_nodes.T, marks, child_owner.reshape(kids // 128, 128), devices, capacity)
    arrived = lax.all_to_all(
        outgoing.reshape(devices, CHUNK // 2, 2, 128), ("seg", "rank"), split_axis=0, concat_axis=0, tiled=True
    ).reshape(devices * CHUNK, 128)
    mass, faces = unpack(arrived, slots)
    before = shifted(faces, "rank", 1)
    after = shifted(faces, "rank", -1)
    return (mass, collect(before, faces, after, face_link.T))


def solution(mesh):
    return jax.shard_map(
        body,
        mesh=mesh,
        in_specs=(P(("seg", "rank"), None),) * 4,
        out_specs=(P(None, ("seg", "rank")), P(None, ("seg", "rank"))),
        check_vma=False,
    )
```

```python
import functools
import math

import jax
import jax.numpy as jnp
import numpy as np
from jax import lax
from jax.experimental import pallas as pl
from jax.experimental.pallas import tpu as pltpu
from jax.sharding import PartitionSpec as P

F32 = jnp.float32
BF16 = jnp.bfloat16
GROUPS = 8
FACE_ROWS = 19
FACES = GROUPS * FACE_ROWS
FACE_CHUNK = 20
MASS_ROWS = 16
MASS = GROUPS * MASS_ROWS


def shifted(array, axis, by):
    count = lax.axis_size(axis)
    pairs = [(i, i + by) for i in range(count) if 0 <= i + by < count]
    return lax.ppermute(array, axis, pairs)


def gll_tables():
    points = np.array([-1.0, -math.sqrt(3.0 / 7.0), 0.0, math.sqrt(3.0 / 7.0), 1.0])
    weights = np.array([0.1, 49.0 / 90.0, 32.0 / 45.0, 49.0 / 90.0, 0.1])
    barycentric = np.array(
        [1.0 / np.prod([points[j] - points[m] for m in range(5) if m != j]) for j in range(5)]
    )
    slopes = np.zeros((5, 5))
    for i in range(5):
        for j in range(5):
            if i != j:
                slopes[i, j] = barycentric[j] / barycentric[i] / (points[i] - points[j])
        slopes[i, i] = -np.sum(slopes[i])

    def lagrange_at(where):
        table = np.ones((5, 5))
        for a in range(5):
            for j in range(5):
                for m in range(5):
                    if m != j:
                        table[a, j] *= (where[a] - points[m]) / (points[j] - points[m])
        return table

    def blend(value, side):
        return (1.0 - value) / 2.0 if side == 0 else (1.0 + value) / 2.0

    def flat(i, j, k):
        return i * 25 + j * 5 + k

    ends = (0, 4)
    gordon = np.zeros((125, 125))
    for i in range(5):
        for j in range(5):
            for k in range(5):
                r, s, t = (points[i], points[j], points[k])
                target = flat(i, j, k)
                for a in range(2):
                    gordon[target, flat(ends[a], j, k)] += blend(r, a)
                    gordon[target, flat(i, ends[a], k)] += blend(s, a)
                    gordon[target, flat(i, j, ends[a])] += blend(t, a)
                    for b in range(2):
                        gordon[target, flat(ends[a], ends[b], k)] -= blend(r, a) * blend(s, b)
                        gordon[target, flat(ends[a], j, ends[b])] -= blend(r, a) * blend(t, b)
                        gordon[target, flat(i, ends[a], ends[b])] -= blend(s, a) * blend(t, b)
                        for c in range(2):
                            gordon[target, flat(ends[a], ends[b], ends[c])] += (
                                blend(r, a) * blend(s, b) * blend(t, c)
                            )
    children = np.zeros((8, 125, 125))
    for octant in range(8):
        shifts = [2 * (octant >> 2 & 1) - 1, 2 * (octant >> 1 & 1) - 1, 2 * (octant & 1) - 1]
        tables = [lagrange_at((points + shifts[q]) / 2.0) for q in range(3)]
        children[octant] = np.kron(np.kron(tables[0], tables[1]), tables[2]) @ gordon
    identity = np.eye(5)
    derivs = [
        np.kron(np.kron(slopes, identity), identity),
        np.kron(np.kron(identity, slopes), identity),
        np.kron(np.kron(identity, identity), slopes),
    ]
    deriv_table = np.concatenate([derivs[q].T for q in range(3)], axis=1)
    mass_weights = np.kron(np.kron(weights, weights), weights)
    face_weights = np.kron(weights, weights)
    tangents = [(1, 2), (1, 2), (0, 2), (0, 2), (0, 1), (0, 1)]
    boundary = [
        flat(i, j, k)
        for i in range(5)
        for j in range(5)
        for k in range(5)
        if i in ends or j in ends or k in ends
    ]
    children_map = children.transpose(2, 0, 1).reshape(125, 1000)
    return (children_map, deriv_table, mass_weights, face_weights, tangents, np.array(boundary))


def split(value, parts):
    pieces = []
    for _ in range(parts):
        piece = value.astype(BF16)
        pieces.append(piece)
        value = value - piece.astype(F32)
    return pieces


def flipped(blocks):
    lanes = lax.broadcasted_iota(jnp.int32, blocks[0].shape, 1) // (128 // GROUPS)
    blocks = list(blocks)
    for bit in (1, 2, 4):
        low = (lanes & bit) == 0
        step = bit * (128 // GROUPS)
        for i in range(GROUPS):
            if i & bit == 0:
                a, c = blocks[i], blocks[i | bit]
                blocks[i] = jnp.where(low, a, pltpu.roll(c, step, 1))
                blocks[i | bit] = jnp.where(low, pltpu.roll(a, 128 - step, 1), c)
    return blocks


def face_order():
    return [25 * f + p for f in range(6) for p in range(24)] + [25 * f + 24 for f in range(6)]


def constants():
    children_map, deriv_table, mass_weights, face_weights, tangents, _ = gll_tables()
    child = np.zeros((8, 128, 128))
    child[:, :125, :125] = children_map.reshape(125, 8, 125).transpose(1, 2, 0)
    derivs = deriv_table.reshape(125, 3, 125).transpose(1, 2, 0)
    grid = np.arange(125).reshape(5, 5, 5)
    face_rows = np.zeros((2 * FACES, 128))
    face_scale = np.zeros((FACES, 1))
    for face in range(6):
        nodes = np.take(grid, 0 if face % 2 == 0 else 4, axis=face // 2).reshape(-1)
        for p in range(25):
            n = 24 * face + p if p < 24 else 144 + face
            face_rows[n, :125] = derivs[tangents[face][0]][nodes[p]]
            face_rows[FACES + n, :125] = derivs[tangents[face][1]][nodes[p]]
            face_scale[n, 0] = face_weights[p]
    mass_rows = np.zeros((3 * MASS, 128))
    mass_scale = np.zeros((MASS, 1))
    mass_scale[:125, 0] = mass_weights
    for d in range(3):
        mass_rows[d * MASS : d * MASS + 125, :125] = derivs[d]
    arrays = (child.reshape(1024, 128), face_rows, face_scale, mass_rows, mass_scale)
    return [jnp.asarray(a, F32) for a in arrays]


def fill_table(dd_ref, rows_ref):
    d1, d2 = split(rows_ref[...], 2)
    for k, piece in enumerate((d1, d1, d2, d2)):
        dd_ref[:, 128 * k : 128 * k + 128] = piece


def slopes_of(dd_ref, deriv_ref, coords):
    deriv_ref[...] = jnp.dot(
        dd_ref[...], jnp.concatenate([coords, coords], axis=0), preferred_element_type=F32
    )


def put(vals_ref, row, lanes, value):
    v1, v2 = split(value, 2)
    vals_ref[pl.ds(row, 8 * (value.shape[0] // 8)), lanes] = v1
    vals_ref[pl.ds(vals_ref.shape[0] // 2 + row, 8 * (value.shape[0] // 8)), lanes] = v2


def scattered(vals_ref, target_ref, onehot_ref, y_ref):
    kids = target_ref.shape[0]
    columns = lax.broadcasted_iota(jnp.int32, (128, 128), 1) + pl.program_id(0) * 256

    def fill(i, carry):
        rows = pl.ds(pl.multiple_of(i * 128, 128), 128)
        target = target_ref[rows, :]
        onehot_ref[rows, 0:128] = jnp.where(target == columns, 1.0, 0.0).astype(BF16)
        onehot_ref[rows, 128:256] = jnp.where(target == columns + 128, 1.0, 0.0).astype(BF16)
        return carry

    lax.fori_loop(0, kids // 128, fill, 0, unroll=True)
    moved = jnp.dot(vals_ref[...], onehot_ref[...], preferred_element_type=F32)
    height = y_ref.shape[0]
    y_ref[...] = moved[0:height] + moved[height:]


def send(y_ref, out_ref, rows, chunk):
    for tile in range(2):
        lanes = slice(128 * tile, 128 * tile + 128)
        blocks = flipped([y_ref[rows * g : rows * (g + 1), lanes] for g in range(GROUPS)])
        for j in range(GROUPS):
            start = chunk * (GROUPS * tile + j)
            out_ref[start : start + rows, :] = blocks[j]
            if chunk > rows:
                out_ref[start + rows : start + chunk, :] = jnp.zeros((chunk - rows, 128), F32)


def face_kernel(
    capacity, nodes_ref, marks_ref, owner_ref, child_ref, rows_ref, scale_ref, out_ref, coords_ref, target_ref,
    pick_ref, x_ref, cc_ref, dd_ref, deriv_ref, vals_ref, natural_ref, onehot_ref, y_ref,
):
    elements = nodes_ref.shape[1]
    marked = marks_ref.shape[1]
    kids = 8 * marked
    devices = out_ref.shape[0] // FACE_CHUNK * pl.num_programs(0)

    @pl.when(pl.program_id(0) == 0)
    def _():
        pick_ref[...] = jnp.zeros_like(pick_ref)
        marks = marks_ref[...]

        def pick(k, carry):
            start = pl.multiple_of(k * 256, 256)
            where = lax.broadcasted_iota(jnp.int32, (256, marked), 0) + start
            chosen = jnp.where(where == marks, 1.0, 0.0).astype(BF16)
            for piece in split(nodes_ref[:, pl.ds(start, 256)], 3):
                pick_ref[0:375, :] += jnp.dot(piece, chosen, preferred_element_type=F32)
            return carry

        lax.fori_loop(0, elements // 256, pick, 0)
        for c in range(3):
            x = pick_ref[125 * c : 125 * c + 128, :]
            x = x - 0.5 * (x[0:1] + x[124:125])
            a1, a2, a3 = split(x, 3)
            for k, piece in enumerate((a1, a2, a1, a3, a2, a1)):
                x_ref[128 * k : 128 * k + 128, c * marked : (c + 1) * marked] = piece
        c1, c2, c3 = split(child_ref[...], 3)
        for k, piece in enumerate((c1, c1, c2, c1, c2, c3)):
            cc_ref[:, 128 * k : 128 * k + 128] = piece
        fill_table(dd_ref, rows_ref)

        def octant(o, carry):
            coords = jnp.dot(
                cc_ref[pl.ds(pl.multiple_of(o * 128, 128), 128), :], x_ref[...], preferred_element_type=F32
            )
            both = jnp.concatenate(split(coords - coords[62:63], 2), axis=0)
            coords_ref[pl.ds(pl.multiple_of(o * 256, 256), 256), :] = both
            slopes_of(dd_ref, deriv_ref, both)
            lanes = pl.ds(pl.multiple_of(o * marked, 128), marked)

            def face_block(row, rows):
                u = [deriv_ref[pl.ds(row, rows), c * marked : (c + 1) * marked] for c in range(3)]
                v = [deriv_ref[pl.ds(FACES + row, rows), c * marked : (c + 1) * marked] for c in range(3)]
                nx = u[1] * v[2] - u[2] * v[1]
                ny = u[2] * v[0] - u[0] * v[2]
                nz = u[0] * v[1] - u[1] * v[0]
                put(vals_ref, row, lanes, jnp.sqrt(nx * nx + ny * ny + nz * nz) * scale_ref[pl.ds(row, rows), :])

            for row in range(0, FACES, 8):
                face_block(row, 8)
            return carry

        lax.fori_loop(0, 8, octant, 0)

        owner_rows = lax.broadcasted_iota(jnp.int32, (devices, 128), 0)
        earlier = lax.broadcasted_iota(jnp.int32, (128, 128), 0) < lax.broadcasted_iota(jnp.int32, (128, 128), 1)
        earlier = jnp.where(earlier, 1.0, 0.0).astype(BF16)
        ones = jnp.ones((128, 128), BF16)

        def slots(b, seen):
            owner = owner_ref[pl.ds(b, 1), :]
            same = owner_rows == owner
            same_b = jnp.where(same, 1.0, 0.0).astype(BF16)
            before = jnp.dot(same_b, earlier, preferred_element_type=F32) + seen
            position = jnp.sum(jnp.where(same, before, 0.0), axis=0, keepdims=True)
            target = owner.astype(F32) * capacity + position
            target = jnp.broadcast_to(target, (128, 128)).T
            natural_ref[pl.ds(pl.multiple_of(b * 128, 128), 128), :] = target.astype(jnp.int32)
            return seen + jnp.dot(same_b, ones, preferred_element_type=F32)

        lax.fori_loop(0, kids // 128, slots, jnp.zeros((devices, 128), F32))
        for o in range(8):
            target_ref[o * marked : (o + 1) * marked, :] = natural_ref[pl.ds(o, marked, stride=8), :]

    scattered(vals_ref, target_ref, onehot_ref, y_ref)
    send(y_ref, out_ref, FACE_ROWS, FACE_CHUNK)


def mass_kernel(coords_ref, target_ref, rows_ref, scale_ref, out_ref, dd_ref, deriv_ref, vals_ref, onehot_ref, y_ref):
    marked = coords_ref.shape[1] // 3

    @pl.when(pl.program_id(0) == 0)
    def _():
        fill_table(dd_ref, rows_ref)

        def octant(o, carry):
            slopes_of(dd_ref, deriv_ref, coords_ref[pl.ds(pl.multiple_of(o * 256, 256), 256), :])
            lanes = pl.ds(pl.multiple_of(o * marked, 128), marked)
            for row in range(0, MASS, 8):
                j = [
                    [deriv_ref[d * MASS + row : d * MASS + row + 8, c * marked : (c + 1) * marked] for d in range(3)]
                    for c in range(3)
                ]
                determinant = (
                    j[0][0] * (j[1][1] * j[2][2] - j[1][2] * j[2][1])
                    - j[0][1] * (j[1][0] * j[2][2] - j[1][2] * j[2][0])
                    + j[0][2] * (j[1][0] * j[2][1] - j[1][1] * j[2][0])
                )
                put(vals_ref, row, lanes, determinant * scale_ref[row : row + 8, :])
            return carry

        lax.fori_loop(0, 8, octant, 0)

    scattered(vals_ref, target_ref, onehot_ref, y_ref)
    send(y_ref, out_ref, MASS_ROWS, MASS_ROWS)


def whole(a):
    return pl.BlockSpec(a.shape, lambda i: (0, 0))


def make_outgoing(nodes, marks, owner, devices, capacity):
    marked = marks.shape[1]
    kids = 8 * marked
    child, face_rows, face_scale, mass_rows, mass_scale = constants()
    steps = devices * capacity // 256
    operands = (nodes, marks, owner, child, face_rows, face_scale)
    shapes = (
        jax.ShapeDtypeStruct((devices * FACE_CHUNK, 128), F32),
        jax.ShapeDtypeStruct((2048, 3 * marked), BF16),
        jax.ShapeDtypeStruct((kids, 128), jnp.int32),
    )
    faces, coords, target = pl.pallas_call(
        functools.partial(face_kernel, capacity),
        out_shape=shapes,
        grid=(steps,),
        in_specs=[whole(a) for a in operands],
        out_specs=(pl.BlockSpec((2 * GROUPS * FACE_CHUNK, 128), lambda i: (i, 0)), whole(shapes[1]), whole(shapes[2])),
        scratch_shapes=[
            pltpu.VMEM((384, marked), F32),
            pltpu.VMEM((768, 3 * marked), BF16),
            pltpu.VMEM((1024, 768), BF16),
            pltpu.VMEM((2 * FACES, 512), BF16),
            pltpu.VMEM((2 * FACES, 3 * marked), F32),
            pltpu.VMEM((2 * FACES, kids), BF16),
            pltpu.VMEM((kids, 128), jnp.int32),
            pltpu.VMEM((kids, 256), BF16),
            pltpu.VMEM((FACES, 256), F32),
        ],
        compiler_params=pltpu.CompilerParams(vmem_limit_bytes=40 << 20),
        name="faces",
    )(*operands)
    operands = (coords, target, mass_rows, mass_scale)
    masses = pl.pallas_call(
        mass_kernel,
        out_shape=jax.ShapeDtypeStruct((devices * MASS_ROWS, 128), F32),
        grid=(steps,),
        in_specs=[whole(a) for a in operands],
        out_specs=pl.BlockSpec((2 * GROUPS * MASS_ROWS, 128), lambda i: (i, 0)),
        scratch_shapes=[
            pltpu.VMEM((3 * MASS, 512), BF16),
            pltpu.VMEM((3 * MASS, 3 * marked), F32),
            pltpu.VMEM((2 * MASS, kids), BF16),
            pltpu.VMEM((kids, 256), BF16),
            pltpu.VMEM((MASS, 256), F32),
        ],
        compiler_params=pltpu.CompilerParams(vmem_limit_bytes=32 << 20),
        name="masses",
    )(*operands)
    return faces, masses


def unpack_kernel(rows, chunk, height, in_ref, out_ref):
    for tile in range(2):
        lanes = slice(128 * tile, 128 * tile + 128)
        starts = [chunk * (GROUPS * tile + j) for j in range(GROUPS)]
        blocks = flipped([in_ref[s : s + rows, :] for s in starts])
        for g in range(GROUPS):
            count = min(rows, height - rows * g)
            out_ref[rows * g : rows * g + count, lanes] = blocks[g][0:count]


def unpack(arrived, slots, rows, chunk, height, name):
    return pl.pallas_call(
        functools.partial(unpack_kernel, rows, chunk, height),
        out_shape=jax.ShapeDtypeStruct((height, slots), F32),
        grid=(slots // 256,),
        in_specs=[pl.BlockSpec((2 * GROUPS * chunk, 128), lambda i: (i, 0))],
        out_specs=pl.BlockSpec((height, 256), lambda i: (0, i)),
        name=name,
    )(arrived)


def collect_kernel(link_ref, before_ref, faces_ref, after_ref, out_ref, table_ref, tail_ref):
    sources = (before_ref, faces_ref, after_ref)
    per_source = faces_ref.shape[1] // 256
    tiles = 3 * per_source
    body_rows = 24 * tiles

    @pl.when(pl.program_id(0) == 0)
    def _():
        for f in range(6):
            other = f + 1 - 2 * (f % 2)
            for k, source in enumerate(sources):

                def pair(i, carry):
                    lanes = [pl.ds(pl.multiple_of(512 * i + 256 * e, 256), 256) for e in range(2)]
                    values = jnp.concatenate([source[24 * other : 24 * other + 24, l] for l in lanes], axis=0)
                    row = pl.multiple_of(24 * per_source * k + 48 * i, 16)
                    for part, piece in enumerate(split(values, 2)):
                        table_ref[f, pl.ds(row, 48), 256 * part : 256 * part + 256] = piece
                    for e in range(2):
                        tail_ref[pl.ds(per_source * k + 2 * i + e, 1), :] = source[
                            144 + other : 145 + other, lanes[e]
                        ]
                    return carry

                lax.fori_loop(0, per_source // 2, pair, 0)
            for part, piece in enumerate(split(tail_ref[...], 2)):
                table_ref[f, body_rows : body_rows + tiles, 256 * part : 256 * part + 256] = piece

    here = pl.ds(pl.multiple_of(pl.program_id(0) * 256, 256), 256)
    for f in range(6):
        link = link_ref[f : f + 1, here]
        low, high = link & 255, link >> 8
        chosen = jnp.where(lax.broadcasted_iota(jnp.int32, (256, 256), 0) == low, 1.0, 0.0).astype(BF16)
        found = jnp.dot(table_ref[f], jnp.concatenate([chosen, chosen], axis=0), preferred_element_type=F32)
        high24 = jnp.broadcast_to(high, (24, 256))
        picked = jnp.zeros((24, 256), F32)
        for h in range(tiles):
            picked = jnp.where(high24 == h, found[24 * h : 24 * h + 24], picked)
        last = jnp.where(lax.broadcasted_iota(jnp.int32, (tiles, 256), 0) == high, found[body_rows:], 0.0)
        out_ref[25 * f : 25 * f + 24, :] = faces_ref[24 * f : 24 * f + 24, here] + picked
        out_ref[25 * f + 24 : 25 * f + 25, :] = faces_ref[144 + f : 145 + f, here] + jnp.sum(
            last, axis=0, keepdims=True
        )


def collect(before, faces, after, links):
    slots = faces.shape[1]
    tiles = 3 * slots // 256
    operands = (links, before, faces, after)
    return pl.pallas_call(
        collect_kernel,
        out_shape=jax.ShapeDtypeStruct((150, slots), F32),
        grid=(slots // 256,),
        in_specs=[whole(a) for a in operands],
        out_specs=pl.BlockSpec((150, 256), lambda i: (0, i)),
        scratch_shapes=[pltpu.VMEM((6, 25 * tiles, 512), BF16), pltpu.VMEM((tiles, 256), F32)],
        compiler_params=pltpu.CompilerParams(vmem_limit_bytes=48 << 20),
        name="collect",
    )(*operands)


def exchanged(rows, devices, tile):
    blocks = rows.reshape(devices, rows.shape[0] // devices // tile, tile, 128)
    return lax.all_to_all(blocks, ("seg", "rank"), split_axis=0, concat_axis=0, tiled=True).reshape(rows.shape)


def body(parent_nodes, marks, child_owner, face_link):
    devices = lax.axis_size("seg") * lax.axis_size("rank")
    kids = child_owner.shape[0]
    capacity = max(2, 2 * kids // devices)
    slots = devices * capacity
    faces, masses = make_outgoing(parent_nodes.T, marks, child_owner.reshape(kids // 128, 128), devices, capacity)
    faces = unpack(exchanged(faces, devices, 4), slots, FACE_ROWS, FACE_CHUNK, 150, "unpack_faces")
    masses = exchanged(masses, devices, 8)
    before = shifted(faces, "rank", 1)
    after = shifted(faces, "rank", -1)
    face_mass = collect(before, faces, after, face_link.T)
    masses, face_mass = lax.optimization_barrier((masses, face_mass))
    return (unpack(masses, slots, MASS_ROWS, MASS_ROWS, 125, "unpack_masses"), face_mass)


def solution(mesh):
    return jax.shard_map(
        body,
        mesh=mesh,
        in_specs=(P(("seg", "rank"), None),) * 4,
        out_specs=(P(None, ("seg", "rank")), P(None, ("seg", "rank"))),
        check_vma=False,
    )
```

```python
import functools
import math

import jax
import jax.numpy as jnp
import numpy as np
from jax import lax
from jax.experimental import pallas as pl
from jax.experimental.pallas import tpu as pltpu
from jax.sharding import PartitionSpec as P

F32 = jnp.float32
BF16 = jnp.bfloat16
VMEM = 60 << 20
GROUPS = 8
FACE_ROWS = 19
FACES = GROUPS * FACE_ROWS
FACE_CHUNK = 20
MASS_ROWS = 16
MASS = GROUPS * MASS_ROWS


def shifted(array, axis, by):
    count = lax.axis_size(axis)
    pairs = [(i, i + by) for i in range(count) if 0 <= i + by < count]
    return lax.ppermute(array, axis, pairs)


def gll_tables():
    points = np.array([-1.0, -math.sqrt(3.0 / 7.0), 0.0, math.sqrt(3.0 / 7.0), 1.0])
    weights = np.array([0.1, 49.0 / 90.0, 32.0 / 45.0, 49.0 / 90.0, 0.1])
    barycentric = np.array(
        [1.0 / np.prod([points[j] - points[m] for m in range(5) if m != j]) for j in range(5)]
    )
    slopes = np.zeros((5, 5))
    for i in range(5):
        for j in range(5):
            if i != j:
                slopes[i, j] = barycentric[j] / barycentric[i] / (points[i] - points[j])
        slopes[i, i] = -np.sum(slopes[i])

    def lagrange_at(where):
        table = np.ones((5, 5))
        for a in range(5):
            for j in range(5):
                for m in range(5):
                    if m != j:
                        table[a, j] *= (where[a] - points[m]) / (points[j] - points[m])
        return table

    def blend(value, side):
        return (1.0 - value) / 2.0 if side == 0 else (1.0 + value) / 2.0

    def flat(i, j, k):
        return i * 25 + j * 5 + k

    ends = (0, 4)
    gordon = np.zeros((125, 125))
    for i in range(5):
        for j in range(5):
            for k in range(5):
                r, s, t = (points[i], points[j], points[k])
                target = flat(i, j, k)
                for a in range(2):
                    gordon[target, flat(ends[a], j, k)] += blend(r, a)
                    gordon[target, flat(i, ends[a], k)] += blend(s, a)
                    gordon[target, flat(i, j, ends[a])] += blend(t, a)
                    for b in range(2):
                        gordon[target, flat(ends[a], ends[b], k)] -= blend(r, a) * blend(s, b)
                        gordon[target, flat(ends[a], j, ends[b])] -= blend(r, a) * blend(t, b)
                        gordon[target, flat(i, ends[a], ends[b])] -= blend(s, a) * blend(t, b)
                        for c in range(2):
                            gordon[target, flat(ends[a], ends[b], ends[c])] += (
                                blend(r, a) * blend(s, b) * blend(t, c)
                            )
    children = np.zeros((8, 125, 125))
    for octant in range(8):
        shifts = [2 * (octant >> 2 & 1) - 1, 2 * (octant >> 1 & 1) - 1, 2 * (octant & 1) - 1]
        tables = [lagrange_at((points + shifts[q]) / 2.0) for q in range(3)]
        children[octant] = np.kron(np.kron(tables[0], tables[1]), tables[2]) @ gordon
    identity = np.eye(5)
    derivs = [
        np.kron(np.kron(slopes, identity), identity),
        np.kron(np.kron(identity, slopes), identity),
        np.kron(np.kron(identity, identity), slopes),
    ]
    deriv_table = np.concatenate([derivs[q].T for q in range(3)], axis=1)
    mass_weights = np.kron(np.kron(weights, weights), weights)
    face_weights = np.kron(weights, weights)
    tangents = [(1, 2), (1, 2), (0, 2), (0, 2), (0, 1), (0, 1)]
    boundary = [
        flat(i, j, k)
        for i in range(5)
        for j in range(5)
        for k in range(5)
        if i in ends or j in ends or k in ends
    ]
    children_map = children.transpose(2, 0, 1).reshape(125, 1000)
    return (children_map, deriv_table, mass_weights, face_weights, tangents, np.array(boundary))


def split(value, parts):
    pieces = []
    for _ in range(parts):
        piece = value.astype(BF16)
        pieces.append(piece)
        value = value - piece.astype(F32)
    return pieces


def flipped(blocks):
    lanes = lax.broadcasted_iota(jnp.int32, blocks[0].shape, 1) // (128 // GROUPS)
    blocks = list(blocks)
    for bit in (1, 2, 4):
        low = (lanes & bit) == 0
        step = bit * (128 // GROUPS)
        for i in range(GROUPS):
            if i & bit == 0:
                a, c = blocks[i], blocks[i | bit]
                blocks[i] = jnp.where(low, a, pltpu.roll(c, step, 1))
                blocks[i | bit] = jnp.where(low, pltpu.roll(a, 128 - step, 1), c)
    return blocks


def face_order():
    return [25 * f + p for f in range(6) for p in range(24)] + [25 * f + 24 for f in range(6)]


def constants():
    children_map, deriv_table, mass_weights, face_weights, tangents, _ = gll_tables()
    child = np.zeros((8, 128, 128))
    child[:, :125, :125] = children_map.reshape(125, 8, 125).transpose(1, 2, 0)
    derivs = deriv_table.reshape(125, 3, 125).transpose(1, 2, 0)
    grid = np.arange(125).reshape(5, 5, 5)
    face_rows = np.zeros((2 * FACES, 128))
    for face in range(6):
        nodes = np.take(grid, 0 if face % 2 == 0 else 4, axis=face // 2).reshape(-1)
        for p in range(25):
            n = 24 * face + p if p < 24 else 144 + face
            face_rows[n, :125] = face_weights[p] * derivs[tangents[face][0]][nodes[p]]
            face_rows[FACES + n, :125] = derivs[tangents[face][1]][nodes[p]]
    mass_rows = np.zeros((3 * MASS, 128))
    for d in range(3):
        weights = mass_weights[:, None] if d == 0 else 1.0
        mass_rows[d * MASS : d * MASS + 125, :125] = weights * derivs[d]
    first = np.concatenate([child.reshape(1024, 128), face_rows])
    return jnp.asarray(first, F32), jnp.asarray(mass_rows, F32)


def fill_table(dd_ref, rows):
    d1, d2 = split(rows, 2)
    for k, piece in enumerate((d1, d1, d2, d2)):
        dd_ref[:, 128 * k : 128 * k + 128] = piece


def slopes_of(dd_ref, deriv_ref, coords):
    deriv_ref[...] = jnp.dot(
        dd_ref[...], jnp.concatenate([coords, coords], axis=0), preferred_element_type=F32
    )


def put(vals_ref, row, lanes, value):
    v1, v2 = split(value, 2)
    vals_ref[pl.ds(row, 8 * (value.shape[0] // 8)), lanes] = v1
    vals_ref[pl.ds(vals_ref.shape[0] // 2 + row, 8 * (value.shape[0] // 8)), lanes] = v2


def scattered(vals_ref, target_ref, onehot_ref, y_ref):
    kids = target_ref.shape[0]
    columns = lax.broadcasted_iota(jnp.int32, (128, 128), 1) + pl.program_id(0) * 256

    def fill(i, carry):
        rows = pl.ds(pl.multiple_of(i * 128, 128), 128)
        target = target_ref[rows, :]
        onehot_ref[rows, 0:128] = jnp.where(target == columns, 1.0, 0.0).astype(BF16)
        onehot_ref[rows, 128:256] = jnp.where(target == columns + 128, 1.0, 0.0).astype(BF16)
        return carry

    lax.fori_loop(0, kids // 128, fill, 0, unroll=True)
    moved = jnp.dot(vals_ref[...], onehot_ref[...], preferred_element_type=F32)
    height = y_ref.shape[0]
    y_ref[...] = moved[0:height] + moved[height:]


def send(y_ref, out_ref, rows, chunk):
    for tile in range(2):
        lanes = slice(128 * tile, 128 * tile + 128)
        blocks = flipped([y_ref[rows * g : rows * (g + 1), lanes] for g in range(GROUPS)])
        for j in range(GROUPS):
            start = chunk * (GROUPS * tile + j)
            out_ref[start : start + rows, :] = blocks[j]
            if chunk > rows:
                out_ref[start + rows : start + chunk, :] = jnp.zeros((chunk - rows, 128), F32)


def face_kernel(
    capacity, nodes_hbm, marks_hbm, owner_hbm, table_hbm, out_ref, coords_ref, target_ref,
    nodes_ref, marks_ref, owner_ref, table_ref, sems, pick_ref, x_ref, cc_ref, dd_ref, deriv_ref, vals_ref, natural_ref, onehot_ref, y_ref,
):
    elements = nodes_ref.shape[1]
    marked = marks_ref.shape[1]
    kids = 8 * marked
    devices = out_ref.shape[0] // FACE_CHUNK * pl.num_programs(0)

    @pl.when(pl.program_id(0) == 0)
    def _():
        copies = [
            pltpu.make_async_copy(source, kept, sems.at[i])
            for i, (source, kept) in enumerate(
                ((marks_hbm, marks_ref), (owner_hbm, owner_ref), (table_hbm, table_ref))
            )
        ]
        chunks = [
            pltpu.make_async_copy(
                nodes_hbm.at[:, pl.ds(at, 512)], nodes_ref.at[:, pl.ds(at, 512)], sems.at[3 + at // 512]
            )
            for at in range(0, elements, 512)
        ]
        for copy in copies[:1] + chunks + copies[1:]:
            copy.start()
        pick_ref[...] = jnp.zeros_like(pick_ref)
        copies[0].wait()
        marks = marks_ref[...]

        def pick(k, carry):
            start = pl.multiple_of(k * 256, 256)
            where = lax.broadcasted_iota(jnp.int32, (256, marked), 0) + start
            chosen = jnp.where(where == marks, 1.0, 0.0).astype(BF16)
            for piece in split(nodes_ref[:, pl.ds(start, 256)], 3):
                pick_ref[0:375, :] += jnp.dot(piece, chosen, preferred_element_type=F32)
            return carry

        for k, copy in enumerate(chunks):
            copy.wait()
            lax.fori_loop(2 * k, 2 * k + 2, pick, 0)
        for copy in copies[1:]:
            copy.wait()
        for c in range(3):
            x = pick_ref[125 * c : 125 * c + 128, :]
            x = x - 0.5 * (x[0:1] + x[124:125])
            a1, a2, a3 = split(x, 3)
            for k, piece in enumerate((a1, a2, a1, a3, a2, a1)):
                x_ref[128 * k : 128 * k + 128, c * marked : (c + 1) * marked] = piece
        c1, c2, c3 = split(table_ref[0:1024, :], 3)
        for k, piece in enumerate((c1, c1, c2, c1, c2, c3)):
            cc_ref[:, 128 * k : 128 * k + 128] = piece
        fill_table(dd_ref, table_ref[1024:, :])

        def octant(o, carry):
            coords = jnp.dot(
                cc_ref[pl.ds(pl.multiple_of(o * 128, 128), 128), :], x_ref[...], preferred_element_type=F32
            )
            both = jnp.concatenate(split(coords - coords[62:63], 2), axis=0)
            coords_ref[pl.ds(pl.multiple_of(o * 256, 256), 256), :] = both
            slopes_of(dd_ref, deriv_ref, both)
            lanes = pl.ds(pl.multiple_of(o * marked, 128), marked)

            def face_block(row, rows):
                u = [deriv_ref[pl.ds(row, rows), c * marked : (c + 1) * marked] for c in range(3)]
                v = [deriv_ref[pl.ds(FACES + row, rows), c * marked : (c + 1) * marked] for c in range(3)]
                nx = u[1] * v[2] - u[2] * v[1]
                ny = u[2] * v[0] - u[0] * v[2]
                nz = u[0] * v[1] - u[1] * v[0]
                put(vals_ref, row, lanes, jnp.sqrt(nx * nx + ny * ny + nz * nz))

            for row in range(0, FACES, 8):
                face_block(row, 8)
            return carry

        lax.fori_loop(0, 8, octant, 0)

        owner_rows = lax.broadcasted_iota(jnp.int32, (devices, 128), 0)
        earlier = lax.broadcasted_iota(jnp.int32, (128, 128), 0) < lax.broadcasted_iota(jnp.int32, (128, 128), 1)
        earlier = jnp.where(earlier, 1.0, 0.0).astype(BF16)
        ones = jnp.ones((128, 128), BF16)

        def slots(b, seen):
            owner = owner_ref[pl.ds(b, 1), :]
            same = owner_rows == owner
            same_b = jnp.where(same, 1.0, 0.0).astype(BF16)
            before = jnp.dot(same_b, earlier, preferred_element_type=F32) + seen
            position = jnp.sum(jnp.where(same, before, 0.0), axis=0, keepdims=True)
            target = owner.astype(F32) * capacity + position
            target = jnp.broadcast_to(target, (128, 128)).T
            natural_ref[pl.ds(pl.multiple_of(b * 128, 128), 128), :] = target.astype(jnp.int32)
            return seen + jnp.dot(same_b, ones, preferred_element_type=F32)

        lax.fori_loop(0, kids // 128, slots, jnp.zeros((devices, 128), F32))
        for o in range(8):
            target_ref[o * marked : (o + 1) * marked, :] = natural_ref[pl.ds(o, marked, stride=8), :]

    scattered(vals_ref, target_ref, onehot_ref, y_ref)
    send(y_ref, out_ref, FACE_ROWS, FACE_CHUNK)


def mass_kernel(coords_ref, target_ref, rows_ref, out_ref, dd_ref, deriv_ref, vals_ref, onehot_ref, y_ref):
    marked = coords_ref.shape[1] // 3

    @pl.when(pl.program_id(0) == 0)
    def _():
        fill_table(dd_ref, rows_ref[...])

        def octant(o, carry):
            slopes_of(dd_ref, deriv_ref, coords_ref[pl.ds(pl.multiple_of(o * 256, 256), 256), :])
            lanes = pl.ds(pl.multiple_of(o * marked, 128), marked)
            for row in range(0, MASS, 8):
                j = [
                    [deriv_ref[d * MASS + row : d * MASS + row + 8, c * marked : (c + 1) * marked] for d in range(3)]
                    for c in range(3)
                ]
                determinant = (
                    j[0][0] * (j[1][1] * j[2][2] - j[1][2] * j[2][1])
                    - j[0][1] * (j[1][0] * j[2][2] - j[1][2] * j[2][0])
                    + j[0][2] * (j[1][0] * j[2][1] - j[1][1] * j[2][0])
                )
                put(vals_ref, row, lanes, determinant)
            return carry

        lax.fori_loop(0, 8, octant, 0)

    scattered(vals_ref, target_ref, onehot_ref, y_ref)
    send(y_ref, out_ref, MASS_ROWS, MASS_ROWS)


def whole(a):
    return pl.BlockSpec(a.shape, lambda i: (0, 0))


def make_outgoing(nodes, marks, owner, devices, capacity):
    marked = marks.shape[1]
    kids = 8 * marked
    table, mass_rows = constants()
    steps = devices * capacity // 256
    operands = (nodes, marks, owner, table)
    shapes = (
        jax.ShapeDtypeStruct((devices * FACE_CHUNK, 128), F32),
        jax.ShapeDtypeStruct((2048, 3 * marked), BF16),
        jax.ShapeDtypeStruct((kids, 128), jnp.int32),
    )
    faces, coords, target = pl.pallas_call(
        functools.partial(face_kernel, capacity),
        out_shape=shapes,
        grid=(steps,),
        in_specs=[pl.BlockSpec(memory_space=pltpu.HBM)] * 4,
        out_specs=(pl.BlockSpec((2 * GROUPS * FACE_CHUNK, 128), lambda i: (i, 0)), whole(shapes[1]), whole(shapes[2])),
        scratch_shapes=[
            *(pltpu.VMEM(a.shape, a.dtype) for a in operands),
            pltpu.SemaphoreType.DMA((3 + nodes.shape[1] // 512,)),
            pltpu.VMEM((384, marked), F32),
            pltpu.VMEM((768, 3 * marked), BF16),
            pltpu.VMEM((1024, 768), BF16),
            pltpu.VMEM((2 * FACES, 512), BF16),
            pltpu.VMEM((2 * FACES, 3 * marked), F32),
            pltpu.VMEM((2 * FACES, kids), BF16),
            pltpu.VMEM((kids, 128), jnp.int32),
            pltpu.VMEM((kids, 256), BF16),
            pltpu.VMEM((FACES, 256), F32),
        ],
        compiler_params=pltpu.CompilerParams(vmem_limit_bytes=VMEM),
        name="faces",
    )(*operands)
    operands = (coords, target, mass_rows)
    masses = pl.pallas_call(
        mass_kernel,
        out_shape=jax.ShapeDtypeStruct((devices * MASS_ROWS, 128), F32),
        grid=(steps,),
        in_specs=[whole(a) for a in operands],
        out_specs=pl.BlockSpec((2 * GROUPS * MASS_ROWS, 128), lambda i: (i, 0)),
        scratch_shapes=[
            pltpu.VMEM((3 * MASS, 512), BF16),
            pltpu.VMEM((3 * MASS, 3 * marked), F32),
            pltpu.VMEM((2 * MASS, kids), BF16),
            pltpu.VMEM((kids, 256), BF16),
            pltpu.VMEM((MASS, 256), F32),
        ],
        compiler_params=pltpu.CompilerParams(vmem_limit_bytes=VMEM),
        name="masses",
    )(*operands)
    return faces, masses


def unpack_tile(rows, chunk, height, in_ref, out_ref, tile):
    start = pl.multiple_of(tile * (chunk * GROUPS), 8)
    lanes = pl.ds(pl.multiple_of(tile * 128, 128), 128)
    arrived = in_ref[pl.ds(start, chunk * GROUPS), :]
    blocks = flipped([arrived[chunk * j : chunk * j + rows] for j in range(GROUPS)])
    for g in range(GROUPS):
        count = min(rows, height - rows * g)
        out_ref[rows * g : rows * g + count, lanes] = blocks[g][0:count]


def unpack_kernel(rows, chunk, height, in_ref, out_ref):
    def tiles(i, carry):
        for k in range(2):
            unpack_tile(rows, chunk, height, in_ref, out_ref, 2 * i + k)
        return carry

    lax.fori_loop(0, out_ref.shape[1] // 256, tiles, 0)


def unpack(arrived, slots, rows, chunk, height, name):
    return pl.pallas_call(
        functools.partial(unpack_kernel, rows, chunk, height),
        out_shape=jax.ShapeDtypeStruct((height, slots), F32),
        grid=(slots // 1024,),
        in_specs=[pl.BlockSpec((8 * GROUPS * chunk, 128), lambda i: (i, 0))],
        out_specs=pl.BlockSpec((height, 1024), lambda i: (0, i)),
        compiler_params=pltpu.CompilerParams(vmem_limit_bytes=VMEM),
        name=name,
    )(arrived)


def collect_kernel(link_ref, faces_ref, packed_before, packed_after, out_ref, table_ref, tail_ref, before_ref, after_ref):
    sources = (before_ref, faces_ref, after_ref)
    per_source = faces_ref.shape[1] // 256
    tiles = 3 * per_source
    body_rows = 24 * tiles

    @pl.when(pl.program_id(0) == 0)
    def _():
        def tile(i, carry):
            for packed, unpacked in ((packed_before, before_ref), (packed_after, after_ref)):
                unpack_tile(FACE_ROWS, FACE_CHUNK, 150, packed, unpacked, i)
            return carry

        lax.fori_loop(0, faces_ref.shape[1] // 128, tile, 0)
        for f in range(6):
            other = f + 1 - 2 * (f % 2)
            for k, source in enumerate(sources):

                def pair(i, carry):
                    lanes = [pl.ds(pl.multiple_of(512 * i + 256 * e, 256), 256) for e in range(2)]
                    values = jnp.concatenate([source[24 * other : 24 * other + 24, l] for l in lanes], axis=0)
                    row = pl.multiple_of(24 * per_source * k + 48 * i, 16)
                    for part, piece in enumerate(split(values, 2)):
                        table_ref[f, pl.ds(row, 48), 256 * part : 256 * part + 256] = piece
                    for e in range(2):
                        tail_ref[pl.ds(per_source * k + 2 * i + e, 1), :] = source[
                            144 + other : 145 + other, lanes[e]
                        ]
                    return carry

                lax.fori_loop(0, per_source // 2, pair, 0)
            for part, piece in enumerate(split(tail_ref[...], 2)):
                table_ref[f, body_rows : body_rows + tiles, 256 * part : 256 * part + 256] = piece

    here = pl.ds(pl.multiple_of(pl.program_id(0) * 256, 256), 256)
    for f in range(6):
        link = link_ref[f : f + 1, here]
        low, high = link & 255, link >> 8
        chosen = jnp.where(lax.broadcasted_iota(jnp.int32, (256, 256), 0) == low, 1.0, 0.0).astype(BF16)
        found = jnp.dot(table_ref[f], jnp.concatenate([chosen, chosen], axis=0), preferred_element_type=F32)
        high24 = jnp.broadcast_to(high, (24, 256))
        picked = jnp.zeros((24, 256), F32)
        for h in range(tiles):
            picked = jnp.where(high24 == h, found[24 * h : 24 * h + 24], picked)
        last = jnp.where(lax.broadcasted_iota(jnp.int32, (tiles, 256), 0) == high, found[body_rows:], 0.0)
        out_ref[25 * f : 25 * f + 24, :] = faces_ref[24 * f : 24 * f + 24, here] + picked
        out_ref[25 * f + 24 : 25 * f + 25, :] = faces_ref[144 + f : 145 + f, here] + jnp.sum(
            last, axis=0, keepdims=True
        )


def collect(faces, before, after, links):
    slots = faces.shape[1]
    tiles = 3 * slots // 256
    operands = (links, faces, before, after)
    return pl.pallas_call(
        collect_kernel,
        out_shape=jax.ShapeDtypeStruct((150, slots), F32),
        grid=(slots // 256,),
        in_specs=[whole(a) for a in operands],
        out_specs=pl.BlockSpec((150, 256), lambda i: (0, i)),
        scratch_shapes=[
            pltpu.VMEM((6, 25 * tiles, 512), BF16),
            pltpu.VMEM((tiles, 256), F32),
            pltpu.VMEM(faces.shape, F32),
            pltpu.VMEM(faces.shape, F32),
        ],
        compiler_params=pltpu.CompilerParams(vmem_limit_bytes=VMEM),
        name="collect",
    )(*operands)


def exchanged(rows, devices, tile):
    blocks = rows.reshape(devices, rows.shape[0] // devices // tile, tile, 128)
    return lax.all_to_all(blocks, ("seg", "rank"), split_axis=0, concat_axis=0, tiled=True).reshape(rows.shape)


def body(parent_nodes, marks, child_owner, face_link):
    devices = lax.axis_size("seg") * lax.axis_size("rank")
    kids = child_owner.shape[0]
    capacity = max(2, 2 * kids // devices)
    slots = devices * capacity
    faces, masses = make_outgoing(parent_nodes.T, marks, child_owner.reshape(kids // 128, 128), devices, capacity)
    arrived = exchanged(faces, devices, 4)
    arrived, masses = lax.optimization_barrier((arrived, masses))
    before = shifted(arrived, "rank", 1)
    after = shifted(arrived, "rank", -1)
    faces = unpack(arrived, slots, FACE_ROWS, FACE_CHUNK, 150, "unpack_faces")
    masses, before, after, faces = lax.optimization_barrier((masses, before, after, faces))
    masses = exchanged(masses, devices, 8)
    face_mass = collect(faces, before, after, face_link.T)
    masses, face_mass = lax.optimization_barrier((masses, face_mass))
    return (unpack(masses, slots, MASS_ROWS, MASS_ROWS, 125, "unpack_masses"), face_mass)


def solution(mesh):
    return jax.shard_map(
        body,
        mesh=mesh,
        in_specs=(P(("seg", "rank"), None),) * 4,
        out_specs=(P(None, ("seg", "rank")), P(None, ("seg", "rank"))),
        check_vma=False,
    )
```

```python
import functools
import math

import jax
import jax.numpy as jnp
import numpy as np
from jax import lax
from jax.experimental import pallas as pl
from jax.experimental.pallas import tpu as pltpu
from jax.sharding import PartitionSpec as P

F32 = jnp.float32
BF16 = jnp.bfloat16
VMEM = 60 << 20
GROUPS = 8
FACE_ROWS = 19
FACES = GROUPS * FACE_ROWS
FACE_CHUNK = 20
MASS_ROWS = 16
MASS = GROUPS * MASS_ROWS


def shifted(array, axis, by):
    count = lax.axis_size(axis)
    pairs = [(i, i + by) for i in range(count) if 0 <= i + by < count]
    return lax.ppermute(array, axis, pairs)


def gll_tables():
    points = np.array([-1.0, -math.sqrt(3.0 / 7.0), 0.0, math.sqrt(3.0 / 7.0), 1.0])
    weights = np.array([0.1, 49.0 / 90.0, 32.0 / 45.0, 49.0 / 90.0, 0.1])
    barycentric = np.array(
        [1.0 / np.prod([points[j] - points[m] for m in range(5) if m != j]) for j in range(5)]
    )
    slopes = np.zeros((5, 5))
    for i in range(5):
        for j in range(5):
            if i != j:
                slopes[i, j] = barycentric[j] / barycentric[i] / (points[i] - points[j])
        slopes[i, i] = -np.sum(slopes[i])

    def lagrange_at(where):
        table = np.ones((5, 5))
        for a in range(5):
            for j in range(5):
                for m in range(5):
                    if m != j:
                        table[a, j] *= (where[a] - points[m]) / (points[j] - points[m])
        return table

    def blend(value, side):
        return (1.0 - value) / 2.0 if side == 0 else (1.0 + value) / 2.0

    def flat(i, j, k):
        return i * 25 + j * 5 + k

    ends = (0, 4)
    gordon = np.zeros((125, 125))
    for i in range(5):
        for j in range(5):
            for k in range(5):
                r, s, t = (points[i], points[j], points[k])
                target = flat(i, j, k)
                for a in range(2):
                    gordon[target, flat(ends[a], j, k)] += blend(r, a)
                    gordon[target, flat(i, ends[a], k)] += blend(s, a)
                    gordon[target, flat(i, j, ends[a])] += blend(t, a)
                    for b in range(2):
                        gordon[target, flat(ends[a], ends[b], k)] -= blend(r, a) * blend(s, b)
                        gordon[target, flat(ends[a], j, ends[b])] -= blend(r, a) * blend(t, b)
                        gordon[target, flat(i, ends[a], ends[b])] -= blend(s, a) * blend(t, b)
                        for c in range(2):
                            gordon[target, flat(ends[a], ends[b], ends[c])] += (
                                blend(r, a) * blend(s, b) * blend(t, c)
                            )
    children = np.zeros((8, 125, 125))
    for octant in range(8):
        shifts = [2 * (octant >> 2 & 1) - 1, 2 * (octant >> 1 & 1) - 1, 2 * (octant & 1) - 1]
        tables = [lagrange_at((points + shifts[q]) / 2.0) for q in range(3)]
        children[octant] = np.kron(np.kron(tables[0], tables[1]), tables[2]) @ gordon
    identity = np.eye(5)
    derivs = [
        np.kron(np.kron(slopes, identity), identity),
        np.kron(np.kron(identity, slopes), identity),
        np.kron(np.kron(identity, identity), slopes),
    ]
    deriv_table = np.concatenate([derivs[q].T for q in range(3)], axis=1)
    mass_weights = np.kron(np.kron(weights, weights), weights)
    face_weights = np.kron(weights, weights)
    tangents = [(1, 2), (1, 2), (0, 2), (0, 2), (0, 1), (0, 1)]
    boundary = [
        flat(i, j, k)
        for i in range(5)
        for j in range(5)
        for k in range(5)
        if i in ends or j in ends or k in ends
    ]
    children_map = children.transpose(2, 0, 1).reshape(125, 1000)
    return (children_map, deriv_table, mass_weights, face_weights, tangents, np.array(boundary))


def split(value, parts):
    pieces = []
    for _ in range(parts):
        piece = value.astype(BF16)
        pieces.append(piece)
        value = value - piece.astype(F32)
    return pieces


def flipped(blocks):
    lanes = lax.broadcasted_iota(jnp.int32, blocks[0].shape, 1) // (128 // GROUPS)
    blocks = list(blocks)
    for bit in (1, 2, 4):
        low = (lanes & bit) == 0
        step = bit * (128 // GROUPS)
        for i in range(GROUPS):
            if i & bit == 0:
                a, c = blocks[i], blocks[i | bit]
                blocks[i] = jnp.where(low, a, pltpu.roll(c, step, 1))
                blocks[i | bit] = jnp.where(low, pltpu.roll(a, 128 - step, 1), c)
    return blocks


def face_order():
    return [25 * f + p for f in range(6) for p in range(24)] + [25 * f + 24 for f in range(6)]


def constants():
    children_map, deriv_table, mass_weights, face_weights, tangents, _ = gll_tables()
    child = np.zeros((8, 128, 128))
    child[:, :125, :125] = children_map.reshape(125, 8, 125).transpose(1, 2, 0)
    derivs = deriv_table.reshape(125, 3, 125).transpose(1, 2, 0)
    grid = np.arange(125).reshape(5, 5, 5)
    face_rows = np.zeros((2 * FACES, 128))
    for face in range(6):
        nodes = np.take(grid, 0 if face % 2 == 0 else 4, axis=face // 2).reshape(-1)
        for p in range(25):
            n = 24 * face + p if p < 24 else 144 + face
            face_rows[n, :125] = face_weights[p] * derivs[tangents[face][0]][nodes[p]]
            face_rows[FACES + n, :125] = derivs[tangents[face][1]][nodes[p]]
    mass_rows = np.zeros((3 * MASS, 128))
    for d in range(3):
        weights = mass_weights[:, None] if d == 0 else 1.0
        mass_rows[d * MASS : d * MASS + 125, :125] = weights * derivs[d]
    first = np.concatenate([child.reshape(1024, 128), face_rows])
    return jnp.asarray(first, F32), jnp.asarray(mass_rows, F32)


def fill_table(dd_ref, rows):
    d1, d2 = split(rows, 2)
    for k, piece in enumerate((d1, d1, d2, d2)):
        dd_ref[:, 128 * k : 128 * k + 128] = piece


def slopes_of(dd_ref, deriv_ref, coords):
    deriv_ref[...] = jnp.dot(
        dd_ref[...], jnp.concatenate([coords, coords], axis=0), preferred_element_type=F32
    )


def put(vals_ref, row, lanes, value):
    v1, v2 = split(value, 2)
    vals_ref[pl.ds(row, 8 * (value.shape[0] // 8)), lanes] = v1
    vals_ref[pl.ds(vals_ref.shape[0] // 2 + row, 8 * (value.shape[0] // 8)), lanes] = v2


def scattered(vals_ref, target_ref, onehot_ref, y_ref):
    kids = target_ref.shape[0]
    columns = lax.broadcasted_iota(jnp.int32, (128, 128), 1) + pl.program_id(0) * 256

    def fill(i, carry):
        rows = pl.ds(pl.multiple_of(i * 128, 128), 128)
        target = target_ref[rows, :]
        onehot_ref[rows, 0:128] = jnp.where(target == columns, 1.0, 0.0).astype(BF16)
        onehot_ref[rows, 128:256] = jnp.where(target == columns + 128, 1.0, 0.0).astype(BF16)
        return carry

    lax.fori_loop(0, kids // 128, fill, 0, unroll=True)
    moved = jnp.dot(vals_ref[...], onehot_ref[...], preferred_element_type=F32)
    height = y_ref.shape[0]
    y_ref[...] = moved[0:height] + moved[height:]


def send(y_ref, out_ref, rows, chunk):
    for tile in range(2):
        lanes = slice(128 * tile, 128 * tile + 128)
        blocks = flipped([y_ref[rows * g : rows * (g + 1), lanes] for g in range(GROUPS)])
        for j in range(GROUPS):
            start = chunk * (GROUPS * tile + j)
            out_ref[start : start + rows, :] = blocks[j]
            if chunk > rows:
                out_ref[start + rows : start + chunk, :] = jnp.zeros((chunk - rows, 128), F32)


def face_kernel(
    capacity, nodes_hbm, marks_hbm, owner_hbm, table_hbm, out_ref, coords_ref, target_ref,
    nodes_ref, marks_ref, owner_ref, table_ref, sems, pick_ref, x_ref, cc_ref, dd_ref, deriv_ref, vals_ref, natural_ref, onehot_ref, y_ref,
):
    elements = nodes_ref.shape[1]
    marked = marks_ref.shape[1]
    kids = 8 * marked
    devices = out_ref.shape[0] // FACE_CHUNK * pl.num_programs(0)

    @pl.when(pl.program_id(0) == 0)
    def _():
        copies = [
            pltpu.make_async_copy(source, kept, sems.at[i])
            for i, (source, kept) in enumerate(
                ((marks_hbm, marks_ref), (owner_hbm, owner_ref), (table_hbm, table_ref))
            )
        ]
        chunks = [
            pltpu.make_async_copy(
                nodes_hbm.at[:, pl.ds(at, 512)], nodes_ref.at[:, pl.ds(at, 512)], sems.at[3 + at // 512]
            )
            for at in range(0, elements, 512)
        ]
        for copy in copies[:1] + chunks + copies[1:]:
            copy.start()
        pick_ref[...] = jnp.zeros_like(pick_ref)
        copies[0].wait()
        marks = marks_ref[...]

        def pick(k, carry):
            start = pl.multiple_of(k * 256, 256)
            where = lax.broadcasted_iota(jnp.int32, (256, marked), 0) + start
            chosen = jnp.where(where == marks, 1.0, 0.0).astype(BF16)
            for piece in split(nodes_ref[:, pl.ds(start, 256)], 3):
                pick_ref[0:375, :] += jnp.dot(piece, chosen, preferred_element_type=F32)
            return carry

        for k, copy in enumerate(chunks):
            copy.wait()
            lax.fori_loop(2 * k, 2 * k + 2, pick, 0)
        for copy in copies[1:]:
            copy.wait()
        for c in range(3):
            x = pick_ref[125 * c : 125 * c + 128, :]
            x = x - 0.5 * (x[0:1] + x[124:125])
            a1, a2, a3 = split(x, 3)
            for k, piece in enumerate((a1, a2, a1, a3, a2, a1)):
                x_ref[128 * k : 128 * k + 128, c * marked : (c + 1) * marked] = piece
        c1, c2, c3 = split(table_ref[0:1024, :], 3)
        for k, piece in enumerate((c1, c1, c2, c1, c2, c3)):
            cc_ref[:, 128 * k : 128 * k + 128] = piece
        fill_table(dd_ref, table_ref[1024:, :])

        def octant(o, carry):
            coords = jnp.dot(
                cc_ref[pl.ds(pl.multiple_of(o * 128, 128), 128), :], x_ref[...], preferred_element_type=F32
            )
            both = jnp.concatenate(split(coords - coords[62:63], 2), axis=0)
            coords_ref[pl.ds(pl.multiple_of(o * 256, 256), 256), :] = both
            slopes_of(dd_ref, deriv_ref, both)
            lanes = pl.ds(pl.multiple_of(o * marked, 128), marked)

            def face_block(row, rows):
                u = [deriv_ref[pl.ds(row, rows), c * marked : (c + 1) * marked] for c in range(3)]
                v = [deriv_ref[pl.ds(FACES + row, rows), c * marked : (c + 1) * marked] for c in range(3)]
                nx = u[1] * v[2] - u[2] * v[1]
                ny = u[2] * v[0] - u[0] * v[2]
                nz = u[0] * v[1] - u[1] * v[0]
                put(vals_ref, row, lanes, jnp.sqrt(nx * nx + ny * ny + nz * nz))

            for row in range(0, FACES, 8):
                face_block(row, 8)
            return carry

        lax.fori_loop(0, 8, octant, 0)

        owner_rows = lax.broadcasted_iota(jnp.int32, (devices, 128), 0)
        earlier = lax.broadcasted_iota(jnp.int32, (128, 128), 0) < lax.broadcasted_iota(jnp.int32, (128, 128), 1)
        earlier = jnp.where(earlier, 1.0, 0.0).astype(BF16)
        ones = jnp.ones((128, 128), BF16)

        def slots(b, seen):
            owner = owner_ref[pl.ds(b, 1), :]
            same = owner_rows == owner
            same_b = jnp.where(same, 1.0, 0.0).astype(BF16)
            before = jnp.dot(same_b, earlier, preferred_element_type=F32) + seen
            position = jnp.sum(jnp.where(same, before, 0.0), axis=0, keepdims=True)
            target = owner.astype(F32) * capacity + position
            target = jnp.broadcast_to(target, (128, 128)).T
            natural_ref[pl.ds(pl.multiple_of(b * 128, 128), 128), :] = target.astype(jnp.int32)
            return seen + jnp.dot(same_b, ones, preferred_element_type=F32)

        lax.fori_loop(0, kids // 128, slots, jnp.zeros((devices, 128), F32))
        for o in range(8):
            target_ref[o * marked : (o + 1) * marked, :] = natural_ref[pl.ds(o, marked, stride=8), :]

    scattered(vals_ref, target_ref, onehot_ref, y_ref)
    send(y_ref, out_ref, FACE_ROWS, FACE_CHUNK)


def mass_kernel(coords_ref, target_ref, rows_ref, out_ref, dd_ref, deriv_ref, vals_ref, onehot_ref, y_ref):
    marked = coords_ref.shape[1] // 3

    @pl.when(pl.program_id(0) == 0)
    def _():
        fill_table(dd_ref, rows_ref[...])

        def octant(o, carry):
            slopes_of(dd_ref, deriv_ref, coords_ref[pl.ds(pl.multiple_of(o * 256, 256), 256), :])
            lanes = pl.ds(pl.multiple_of(o * marked, 128), marked)
            for row in range(0, MASS, 8):
                j = [
                    [deriv_ref[d * MASS + row : d * MASS + row + 8, c * marked : (c + 1) * marked] for d in range(3)]
                    for c in range(3)
                ]
                determinant = (
                    j[0][0] * (j[1][1] * j[2][2] - j[1][2] * j[2][1])
                    - j[0][1] * (j[1][0] * j[2][2] - j[1][2] * j[2][0])
                    + j[0][2] * (j[1][0] * j[2][1] - j[1][1] * j[2][0])
                )
                put(vals_ref, row, lanes, determinant)
            return carry

        lax.fori_loop(0, 8, octant, 0)

    scattered(vals_ref, target_ref, onehot_ref, y_ref)
    send(y_ref, out_ref, MASS_ROWS, MASS_ROWS)


def whole(a):
    return pl.BlockSpec(a.shape, lambda i: (0, 0))


def make_outgoing(nodes, marks, owner, devices, capacity):
    marked = marks.shape[1]
    kids = 8 * marked
    table, mass_rows = constants()
    steps = devices * capacity // 256
    operands = (nodes, marks, owner, table)
    shapes = (
        jax.ShapeDtypeStruct((devices * FACE_CHUNK, 128), F32),
        jax.ShapeDtypeStruct((2048, 3 * marked), BF16),
        jax.ShapeDtypeStruct((kids, 128), jnp.int32),
    )
    faces, coords, target = pl.pallas_call(
        functools.partial(face_kernel, capacity),
        out_shape=shapes,
        grid=(steps,),
        in_specs=[pl.BlockSpec(memory_space=pltpu.HBM)] * 4,
        out_specs=(pl.BlockSpec((2 * GROUPS * FACE_CHUNK, 128), lambda i: (i, 0)), whole(shapes[1]), whole(shapes[2])),
        scratch_shapes=[
            *(pltpu.VMEM(a.shape, a.dtype) for a in operands),
            pltpu.SemaphoreType.DMA((3 + nodes.shape[1] // 512,)),
            pltpu.VMEM((384, marked), F32),
            pltpu.VMEM((768, 3 * marked), BF16),
            pltpu.VMEM((1024, 768), BF16),
            pltpu.VMEM((2 * FACES, 512), BF16),
            pltpu.VMEM((2 * FACES, 3 * marked), F32),
            pltpu.VMEM((2 * FACES, kids), BF16),
            pltpu.VMEM((kids, 128), jnp.int32),
            pltpu.VMEM((kids, 256), BF16),
            pltpu.VMEM((FACES, 256), F32),
        ],
        compiler_params=pltpu.CompilerParams(vmem_limit_bytes=VMEM),
        name="faces",
    )(*operands)
    operands = (coords, target, mass_rows)
    masses = pl.pallas_call(
        mass_kernel,
        out_shape=jax.ShapeDtypeStruct((devices * MASS_ROWS, 128), F32),
        grid=(steps,),
        in_specs=[whole(a) for a in operands],
        out_specs=pl.BlockSpec((2 * GROUPS * MASS_ROWS, 128), lambda i: (i, 0)),
        scratch_shapes=[
            pltpu.VMEM((3 * MASS, 512), BF16),
            pltpu.VMEM((3 * MASS, 3 * marked), F32),
            pltpu.VMEM((2 * MASS, kids), BF16),
            pltpu.VMEM((kids, 256), BF16),
            pltpu.VMEM((MASS, 256), F32),
        ],
        compiler_params=pltpu.CompilerParams(vmem_limit_bytes=VMEM),
        name="masses",
    )(*operands)
    return faces, masses


def unpack_tile(rows, chunk, height, in_ref, out_ref, tile):
    start = pl.multiple_of(tile * (chunk * GROUPS), 8)
    lanes = pl.ds(pl.multiple_of(tile * 128, 128), 128)
    arrived = in_ref[pl.ds(start, chunk * GROUPS), :]
    blocks = flipped([arrived[chunk * j : chunk * j + rows] for j in range(GROUPS)])
    for g in range(GROUPS):
        count = min(rows, height - rows * g)
        out_ref[rows * g : rows * g + count, lanes] = blocks[g][0:count]


def unpack_kernel(rows, chunk, height, in_ref, out_ref):
    def tiles(i, carry):
        for k in range(2):
            unpack_tile(rows, chunk, height, in_ref, out_ref, 2 * i + k)
        return carry

    lax.fori_loop(0, out_ref.shape[1] // 256, tiles, 0)


def unpack(arrived, slots, rows, chunk, height, name):
    return pl.pallas_call(
        functools.partial(unpack_kernel, rows, chunk, height),
        out_shape=jax.ShapeDtypeStruct((height, slots), F32),
        grid=(slots // 1024,),
        in_specs=[pl.BlockSpec((8 * GROUPS * chunk, 128), lambda i: (i, 0))],
        out_specs=pl.BlockSpec((height, 1024), lambda i: (0, i)),
        compiler_params=pltpu.CompilerParams(vmem_limit_bytes=VMEM),
        name=name,
    )(arrived)


def fill_face_table(table_ref, tail_ref, sources):
    per_source = sources[0].shape[1] // 256
    tiles = len(sources) * per_source
    body_rows = 24 * tiles
    for f in range(6):
        other = f + 1 - 2 * (f % 2)
        for k, source in enumerate(sources):

            def pair(i, carry):
                lanes = [pl.ds(pl.multiple_of(512 * i + 256 * e, 256), 256) for e in range(2)]
                values = jnp.concatenate([source[24 * other : 24 * other + 24, l] for l in lanes], axis=0)
                row = pl.multiple_of(24 * per_source * k + 48 * i, 16)
                for part, piece in enumerate(split(values, 2)):
                    table_ref[f, pl.ds(row, 48), 256 * part : 256 * part + 256] = piece
                for e in range(2):
                    tail_ref[pl.ds(per_source * k + 2 * i + e, 1), :] = source[144 + other : 145 + other, lanes[e]]
                return carry

            lax.fori_loop(0, per_source // 2, pair, 0)
        for part, piece in enumerate(split(tail_ref[...], 2)):
            table_ref[f, body_rows : body_rows + tiles, 256 * part : 256 * part + 256] = piece


def look_up(table_ref, f, low, high):
    tiles = table_ref.shape[1] // 25
    chosen = jnp.where(lax.broadcasted_iota(jnp.int32, (256, 256), 0) == low, 1.0, 0.0).astype(BF16)
    found = jnp.dot(table_ref[f], jnp.concatenate([chosen, chosen], axis=0), preferred_element_type=F32)
    high24 = jnp.broadcast_to(high, (24, 256))
    picked = jnp.zeros((24, 256), F32)
    for h in range(tiles):
        picked = jnp.where(high24 == h, found[24 * h : 24 * h + 24], picked)
    last = jnp.where(lax.broadcasted_iota(jnp.int32, (tiles, 256), 0) == high, found[24 * tiles :], 0.0)
    return picked, jnp.sum(last, axis=0, keepdims=True)


def own_kernel(link_ref, faces_ref, out_ref, table_ref, tail_ref):
    per_source = faces_ref.shape[1] // 256

    @pl.when(pl.program_id(0) == 0)
    def _():
        fill_face_table(table_ref, tail_ref, (faces_ref,))

    here = pl.ds(pl.multiple_of(pl.program_id(0) * 256, 256), 256)
    for f in range(6):
        link = link_ref[f : f + 1, here]
        picked, last = look_up(table_ref, f, link & 255, (link >> 8) - per_source)
        out_ref[25 * f : 25 * f + 24, :] = faces_ref[24 * f : 24 * f + 24, here] + picked
        out_ref[25 * f + 24 : 25 * f + 25, :] = faces_ref[144 + f : 145 + f, here] + last


def neighbour_kernel(link_ref, before_ref, after_ref, part_ref, out_ref, table_ref, tail_ref, unpacked_before, unpacked_after):
    per_source = unpacked_before.shape[1] // 256

    @pl.when(pl.program_id(0) == 0)
    def _():
        def tile(i, carry):
            for packed, unpacked in ((before_ref, unpacked_before), (after_ref, unpacked_after)):
                unpack_tile(FACE_ROWS, FACE_CHUNK, 150, packed, unpacked, i)
            return carry

        lax.fori_loop(0, unpacked_before.shape[1] // 128, tile, 0)
        fill_face_table(table_ref, tail_ref, (unpacked_before, unpacked_after))

    here = pl.ds(pl.multiple_of(pl.program_id(0) * 256, 256), 256)
    for f in range(6):
        link = link_ref[f : f + 1, here]
        high = link >> 8
        high = jnp.where(high < per_source, high, jnp.where(high < 2 * per_source, -1, high - per_source))
        picked, last = look_up(table_ref, f, link & 255, high)
        out_ref[25 * f : 25 * f + 24, :] = part_ref[25 * f : 25 * f + 24, :] + picked
        out_ref[25 * f + 24 : 25 * f + 25, :] = part_ref[25 * f + 24 : 25 * f + 25, :] + last


def collect_own(faces, links):
    slots = faces.shape[1]
    tiles = slots // 256
    return pl.pallas_call(
        own_kernel,
        out_shape=jax.ShapeDtypeStruct((150, slots), F32),
        grid=(tiles,),
        in_specs=[whole(links), whole(faces)],
        out_specs=pl.BlockSpec((150, 256), lambda i: (0, i)),
        scratch_shapes=[pltpu.VMEM((6, 25 * tiles, 512), BF16), pltpu.VMEM((tiles, 256), F32)],
        compiler_params=pltpu.CompilerParams(vmem_limit_bytes=VMEM),
        cost_estimate=pl.CostEstimate(flops=0, bytes_accessed=1024, transcendentals=0),
        name="collect_own",
    )(links, faces)


def collect_neighbours(part, before, after, links):
    slots = part.shape[1]
    tiles = 2 * slots // 256
    block = pl.BlockSpec((150, 256), lambda i: (0, i))
    return pl.pallas_call(
        neighbour_kernel,
        out_shape=jax.ShapeDtypeStruct((150, slots), F32),
        grid=(slots // 256,),
        in_specs=[whole(links), whole(before), whole(after), block],
        out_specs=block,
        scratch_shapes=[
            pltpu.VMEM((6, 25 * tiles, 512), BF16),
            pltpu.VMEM((tiles, 256), F32),
            pltpu.VMEM((150, slots), F32),
            pltpu.VMEM((150, slots), F32),
        ],
        compiler_params=pltpu.CompilerParams(vmem_limit_bytes=VMEM),
        cost_estimate=pl.CostEstimate(flops=10**12, bytes_accessed=10**9, transcendentals=0),
        name="collect_neighbours",
    )(links, before, after, part)


def exchanged(rows, devices, tile):
    blocks = rows.reshape(devices, rows.shape[0] // devices // tile, tile, 128)
    return lax.all_to_all(blocks, ("seg", "rank"), split_axis=0, concat_axis=0, tiled=True).reshape(rows.shape)


def body(parent_nodes, marks, child_owner, face_link):
    devices = lax.axis_size("seg") * lax.axis_size("rank")
    kids = child_owner.shape[0]
    capacity = max(2, 2 * kids // devices)
    slots = devices * capacity
    faces, masses = make_outgoing(parent_nodes.T, marks, child_owner.reshape(kids // 128, 128), devices, capacity)
    arrived = exchanged(faces, devices, 4)
    arrived, masses = lax.optimization_barrier((arrived, masses))
    before = shifted(arrived, "rank", 1)
    after = shifted(arrived, "rank", -1)
    faces = unpack(arrived, slots, FACE_ROWS, FACE_CHUNK, 150, "unpack_faces")
    masses, faces = lax.optimization_barrier((masses, faces))
    masses = exchanged(masses, devices, 8)
    part = collect_own(faces, face_link.T)
    part, before, after = lax.optimization_barrier((part, before, after))
    face_mass = collect_neighbours(part, before, after, face_link.T)
    masses, face_mass = lax.optimization_barrier((masses, face_mass))
    return (unpack(masses, slots, MASS_ROWS, MASS_ROWS, 125, "unpack_masses"), face_mass)


def solution(mesh):
    return jax.shard_map(
        body,
        mesh=mesh,
        in_specs=(P(("seg", "rank"), None),) * 4,
        out_specs=(P(None, ("seg", "rank")), P(None, ("seg", "rank"))),
        check_vma=False,
    )
```

```python
import functools
import math

import jax
import jax.numpy as jnp
import numpy as np
from jax import lax
from jax.experimental import pallas as pl
from jax.experimental.pallas import tpu as pltpu
from jax.sharding import PartitionSpec as P

F32 = jnp.float32
BF16 = jnp.bfloat16
VMEM = 60 << 20
GROUPS = 8
FACE_ROWS = 19
FACES = GROUPS * FACE_ROWS
FACE_CHUNK = 20
MASS_ROWS = 16
MASS = GROUPS * MASS_ROWS


def shifted(array, axis, by):
    count = lax.axis_size(axis)
    pairs = [(i, i + by) for i in range(count) if 0 <= i + by < count]
    return lax.ppermute(array, axis, pairs)


def gll_tables():
    points = np.array([-1.0, -math.sqrt(3.0 / 7.0), 0.0, math.sqrt(3.0 / 7.0), 1.0])
    weights = np.array([0.1, 49.0 / 90.0, 32.0 / 45.0, 49.0 / 90.0, 0.1])
    barycentric = np.array(
        [1.0 / np.prod([points[j] - points[m] for m in range(5) if m != j]) for j in range(5)]
    )
    slopes = np.zeros((5, 5))
    for i in range(5):
        for j in range(5):
            if i != j:
                slopes[i, j] = barycentric[j] / barycentric[i] / (points[i] - points[j])
        slopes[i, i] = -np.sum(slopes[i])

    def lagrange_at(where):
        table = np.ones((5, 5))
        for a in range(5):
            for j in range(5):
                for m in range(5):
                    if m != j:
                        table[a, j] *= (where[a] - points[m]) / (points[j] - points[m])
        return table

    def blend(value, side):
        return (1.0 - value) / 2.0 if side == 0 else (1.0 + value) / 2.0

    def flat(i, j, k):
        return i * 25 + j * 5 + k

    ends = (0, 4)
    gordon = np.zeros((125, 125))
    for i in range(5):
        for j in range(5):
            for k in range(5):
                r, s, t = (points[i], points[j], points[k])
                target = flat(i, j, k)
                for a in range(2):
                    gordon[target, flat(ends[a], j, k)] += blend(r, a)
                    gordon[target, flat(i, ends[a], k)] += blend(s, a)
                    gordon[target, flat(i, j, ends[a])] += blend(t, a)
                    for b in range(2):
                        gordon[target, flat(ends[a], ends[b], k)] -= blend(r, a) * blend(s, b)
                        gordon[target, flat(ends[a], j, ends[b])] -= blend(r, a) * blend(t, b)
                        gordon[target, flat(i, ends[a], ends[b])] -= blend(s, a) * blend(t, b)
                        for c in range(2):
                            gordon[target, flat(ends[a], ends[b], ends[c])] += (
                                blend(r, a) * blend(s, b) * blend(t, c)
                            )
    children = np.zeros((8, 125, 125))
    for octant in range(8):
        shifts = [2 * (octant >> 2 & 1) - 1, 2 * (octant >> 1 & 1) - 1, 2 * (octant & 1) - 1]
        tables = [lagrange_at((points + shifts[q]) / 2.0) for q in range(3)]
        children[octant] = np.kron(np.kron(tables[0], tables[1]), tables[2]) @ gordon
    identity = np.eye(5)
    derivs = [
        np.kron(np.kron(slopes, identity), identity),
        np.kron(np.kron(identity, slopes), identity),
        np.kron(np.kron(identity, identity), slopes),
    ]
    deriv_table = np.concatenate([derivs[q].T for q in range(3)], axis=1)
    mass_weights = np.kron(np.kron(weights, weights), weights)
    face_weights = np.kron(weights, weights)
    tangents = [(1, 2), (1, 2), (0, 2), (0, 2), (0, 1), (0, 1)]
    boundary = [
        flat(i, j, k)
        for i in range(5)
        for j in range(5)
        for k in range(5)
        if i in ends or j in ends or k in ends
    ]
    children_map = children.transpose(2, 0, 1).reshape(125, 1000)
    return (children_map, deriv_table, mass_weights, face_weights, tangents, np.array(boundary))


def split(value, parts):
    pieces = []
    for _ in range(parts):
        piece = value.astype(BF16)
        pieces.append(piece)
        value = value - piece.astype(F32)
    return pieces


def flipped(blocks):
    lanes = lax.broadcasted_iota(jnp.int32, blocks[0].shape, 1) // (128 // GROUPS)
    blocks = list(blocks)
    for bit in (1, 2, 4):
        low = (lanes & bit) == 0
        step = bit * (128 // GROUPS)
        for i in range(GROUPS):
            if i & bit == 0:
                a, c = blocks[i], blocks[i | bit]
                blocks[i] = jnp.where(low, a, pltpu.roll(c, step, 1))
                blocks[i | bit] = jnp.where(low, pltpu.roll(a, 128 - step, 1), c)
    return blocks


def face_order():
    return [25 * f + p for f in range(6) for p in range(24)] + [25 * f + 24 for f in range(6)]


def constants():
    children_map, deriv_table, mass_weights, face_weights, tangents, _ = gll_tables()
    child = np.zeros((8, 128, 128))
    child[:, :125, :125] = children_map.reshape(125, 8, 125).transpose(1, 2, 0)
    derivs = deriv_table.reshape(125, 3, 125).transpose(1, 2, 0)
    grid = np.arange(125).reshape(5, 5, 5)
    face_rows = np.zeros((2 * FACES, 128))
    for face in range(6):
        nodes = np.take(grid, 0 if face % 2 == 0 else 4, axis=face // 2).reshape(-1)
        for p in range(25):
            n = 24 * face + p if p < 24 else 144 + face
            face_rows[n, :125] = face_weights[p] * derivs[tangents[face][0]][nodes[p]]
            face_rows[FACES + n, :125] = derivs[tangents[face][1]][nodes[p]]
    mass_rows = np.zeros((3 * MASS, 128))
    for d in range(3):
        weights = mass_weights[:, None] if d == 0 else 1.0
        mass_rows[d * MASS : d * MASS + 125, :125] = weights * derivs[d]
    child = child.reshape(1024, 128)
    return [jnp.asarray(np.concatenate([child, rows]), F32) for rows in (face_rows, mass_rows)]


def face_values(deriv_ref, row, marked):
    u = [deriv_ref[row : row + 8, c * marked : (c + 1) * marked] for c in range(3)]
    v = [deriv_ref[FACES + row : FACES + row + 8, c * marked : (c + 1) * marked] for c in range(3)]
    nx = u[1] * v[2] - u[2] * v[1]
    ny = u[2] * v[0] - u[0] * v[2]
    nz = u[0] * v[1] - u[1] * v[0]
    return jnp.sqrt(nx * nx + ny * ny + nz * nz)


def mass_values(deriv_ref, row, marked):
    j = [
        [deriv_ref[d * MASS + row : d * MASS + row + 8, c * marked : (c + 1) * marked] for d in range(3)]
        for c in range(3)
    ]
    return (
        j[0][0] * (j[1][1] * j[2][2] - j[1][2] * j[2][1])
        - j[0][1] * (j[1][0] * j[2][2] - j[1][2] * j[2][0])
        + j[0][2] * (j[1][0] * j[2][1] - j[1][1] * j[2][0])
    )


def child_kernel(
    values, rows, chunk, capacity, nodes_hbm, marks_hbm, owner_hbm, table_hbm, out_ref,
    nodes_ref, marks_ref, owner_ref, table_ref, sems, pick_ref, x_ref, cc_ref, dd_ref, deriv_a, deriv_b,
    vals_ref, natural_ref, target_ref, onehot_ref, y_ref,
):
    elements = nodes_ref.shape[1]
    marked = marks_ref.shape[1]
    kids = 8 * marked
    height = GROUPS * rows
    columns = onehot_ref.shape[1]
    destinations = columns // capacity
    devices = out_ref.shape[0] // chunk * pl.num_programs(0)

    @pl.when(pl.program_id(0) == 0)
    def _():
        copies = [
            pltpu.make_async_copy(source, kept, sems.at[i])
            for i, (source, kept) in enumerate(
                ((owner_hbm, owner_ref), (marks_hbm, marks_ref), (table_hbm, table_ref))
            )
        ]
        chunks = [
            pltpu.make_async_copy(
                nodes_hbm.at[:, pl.ds(at, 512)], nodes_ref.at[:, pl.ds(at, 512)], sems.at[3 + at // 512]
            )
            for at in range(0, elements, 512)
        ]
        for copy in copies[:2] + chunks + copies[2:]:
            copy.start()

        owner_rows = lax.broadcasted_iota(jnp.int32, (devices, 128), 0)
        earlier = lax.broadcasted_iota(jnp.int32, (128, 128), 0) < lax.broadcasted_iota(jnp.int32, (128, 128), 1)
        earlier = jnp.where(earlier, 1.0, 0.0).astype(BF16)
        ones = jnp.ones((128, 128), BF16)
        copies[0].wait()
        seen = jnp.zeros((devices, 128), F32)
        for b in range(kids // 128):
            owner = owner_ref[b : b + 1, :]
            same = owner_rows == owner
            same_b = jnp.where(same, 1.0, 0.0).astype(BF16)
            before = jnp.dot(same_b, earlier, preferred_element_type=F32) + seen
            position = jnp.sum(jnp.where(same, before, 0.0), axis=0, keepdims=True)
            target = owner.astype(F32) * capacity + position
            natural_ref[128 * b : 128 * b + 128, :] = jnp.broadcast_to(target, (128, 128)).T.astype(jnp.int32)
            seen = seen + jnp.dot(same_b, ones, preferred_element_type=F32)
        for o in range(8):
            target_ref[o * marked : (o + 1) * marked, :] = natural_ref[pl.ds(o, marked, stride=8), :]

        pick_ref[...] = jnp.zeros_like(pick_ref)
        copies[1].wait()
        marks = marks_ref[...]

        def pick(k, carry):
            start = pl.multiple_of(k * 256, 256)
            where = lax.broadcasted_iota(jnp.int32, (256, marked), 0) + start
            chosen = jnp.where(where == marks, 1.0, 0.0).astype(BF16)
            for piece in split(nodes_ref[:, pl.ds(start, 256)], 3):
                pick_ref[0:375, :] += jnp.dot(piece, chosen, preferred_element_type=F32)
            return carry

        for k, copy in enumerate(chunks):
            copy.wait()
            lax.fori_loop(2 * k, 2 * k + 2, pick, 0)
        copies[2].wait()
        for c in range(3):
            x = pick_ref[125 * c : 125 * c + 128, :]
            x = x - 0.5 * (x[0:1] + x[124:125])
            a1, a2, a3 = split(x, 3)
            for k, piece in enumerate((a1, a2, a1, a3, a2, a1)):
                x_ref[128 * k : 128 * k + 128, c * marked : (c + 1) * marked] = piece
        c1, c2, c3 = split(table_ref[0:1024, :], 3)
        for k, piece in enumerate((c1, c1, c2, c1, c2, c3)):
            cc_ref[:, 128 * k : 128 * k + 128] = piece
        d1, d2 = split(table_ref[1024:, :], 2)
        for k, piece in enumerate((d1, d1, d2, d2)):
            dd_ref[:, 128 * k : 128 * k + 128] = piece

        def octants(i, carry):
            for e, deriv_ref in enumerate((deriv_a, deriv_b)):
                o = 2 * i + e
                coords = jnp.dot(
                    cc_ref[pl.ds(pl.multiple_of(o * 128, 128), 128), :], x_ref[...], preferred_element_type=F32
                )
                y1, y2 = split(coords - coords[62:63], 2)
                deriv_ref[...] = jnp.dot(
                    dd_ref[...], jnp.concatenate([y1, y2, y1, y2], axis=0), preferred_element_type=F32
                )
                lanes = pl.ds(pl.multiple_of(o * marked, 128), marked)
                for row in range(0, height, 8):
                    v1, v2 = split(values(deriv_ref, row, marked), 2)
                    vals_ref[row : row + 8, lanes] = v1
                    vals_ref[height + row : height + row + 8, lanes] = v2
            return carry

        lax.fori_loop(0, 4, octants, 0)

    numbers = lax.broadcasted_iota(jnp.int32, (128, 128), 1)

    def part(i, carry):
        first = pl.program_id(0) * (out_ref.shape[0] // chunk * capacity) + i * columns
        for at in range(0, kids, 128):
            target = target_ref[at : at + 128, :] - first
            for tile in range(columns // 128):
                onehot_ref[at : at + 128, 128 * tile : 128 * tile + 128] = jnp.where(
                    target == numbers + 128 * tile, 1.0, 0.0
                ).astype(BF16)
        moved = jnp.dot(vals_ref[...], onehot_ref[...], preferred_element_type=F32)
        y_ref[...] = moved[0:height] + moved[height:]
        for tile in range(columns // 128):
            lanes = slice(128 * tile, 128 * tile + 128)
            blocks = flipped([y_ref[rows * g : rows * (g + 1), lanes] for g in range(GROUPS)])
            if chunk > rows:
                blocks = [jnp.concatenate([b, jnp.zeros((chunk - rows, 128), F32)], axis=0) for b in blocks]
            start = pl.multiple_of(i * (destinations * chunk) + tile * (GROUPS * chunk), 8)
            out_ref[pl.ds(start, GROUPS * chunk), :] = jnp.concatenate(blocks, axis=0)
        return carry

    lax.fori_loop(0, out_ref.shape[0] // (chunk * destinations), part, 0)


def whole(a):
    return pl.BlockSpec(a.shape, lambda i: (0, 0))


def outgoing(values, rows, chunk, table, nodes, marks, owner, devices, capacity, name):
    marked = marks.shape[1]
    kids = 8 * marked
    operands = (nodes, marks, owner, table)
    steps = 4
    height = GROUPS * rows
    return pl.pallas_call(
        functools.partial(child_kernel, values, rows, chunk, capacity),
        out_shape=jax.ShapeDtypeStruct((devices * chunk, 128), F32),
        grid=(steps,),
        in_specs=[pl.BlockSpec(memory_space=pltpu.HBM)] * 4,
        out_specs=pl.BlockSpec((devices * chunk // steps, 128), lambda i: (i, 0)),
        scratch_shapes=[
            *(pltpu.VMEM(a.shape, a.dtype) for a in operands),
            pltpu.SemaphoreType.DMA((3 + nodes.shape[1] // 512,)),
            pltpu.VMEM((384, marked), F32),
            pltpu.VMEM((768, 3 * marked), BF16),
            pltpu.VMEM((1024, 768), BF16),
            pltpu.VMEM((table.shape[0] - 1024, 512), BF16),
            pltpu.VMEM((table.shape[0] - 1024, 3 * marked), F32),
            pltpu.VMEM((table.shape[0] - 1024, 3 * marked), F32),
            pltpu.VMEM((2 * height, kids), BF16),
            pltpu.VMEM((kids, 128), jnp.int32),
            pltpu.VMEM((kids, 128), jnp.int32),
            pltpu.VMEM((kids, 512), BF16),
            pltpu.VMEM((height, 512), F32),
        ],
        compiler_params=pltpu.CompilerParams(vmem_limit_bytes=VMEM),
        name=name,
    )(*operands)


def make_outgoing(nodes, marks, owner, devices, capacity):
    face_table, mass_table = constants()
    args = (nodes, marks, owner, devices, capacity)
    return (
        outgoing(face_values, FACE_ROWS, FACE_CHUNK, face_table, *args, "faces"),
        outgoing(mass_values, MASS_ROWS, MASS_ROWS, mass_table, *args, "masses"),
    )


def unpack_tile(rows, chunk, height, in_ref, out_ref, tile):
    start = pl.multiple_of(tile * (chunk * GROUPS), 8)
    lanes = pl.ds(pl.multiple_of(tile * 128, 128), 128)
    arrived = in_ref[pl.ds(start, chunk * GROUPS), :]
    blocks = flipped([arrived[chunk * j : chunk * j + rows] for j in range(GROUPS)])
    for g in range(GROUPS):
        count = min(rows, height - rows * g)
        out_ref[rows * g : rows * g + count, lanes] = blocks[g][0:count]


def unpack_kernel(rows, chunk, height, in_ref, out_ref):
    def tiles(i, carry):
        for k in range(2):
            unpack_tile(rows, chunk, height, in_ref, out_ref, 2 * i + k)
        return carry

    lax.fori_loop(0, out_ref.shape[1] // 256, tiles, 0)


def unpack(arrived, slots, rows, chunk, height, name):
    return pl.pallas_call(
        functools.partial(unpack_kernel, rows, chunk, height),
        out_shape=jax.ShapeDtypeStruct((height, slots), F32),
        grid=(slots // 1024,),
        in_specs=[pl.BlockSpec((8 * GROUPS * chunk, 128), lambda i: (i, 0))],
        out_specs=pl.BlockSpec((height, 1024), lambda i: (0, i)),
        compiler_params=pltpu.CompilerParams(vmem_limit_bytes=VMEM),
        name=name,
    )(arrived)


def fill_face_table(table_ref, tail_ref, sources):
    per_source = sources[0].shape[1] // 256
    tiles = len(sources) * per_source
    body_rows = 24 * tiles
    for f in range(6):
        other = f + 1 - 2 * (f % 2)
        for k, source in enumerate(sources):

            def pair(i, carry):
                lanes = [pl.ds(pl.multiple_of(512 * i + 256 * e, 256), 256) for e in range(2)]
                values = jnp.concatenate([source[24 * other : 24 * other + 24, l] for l in lanes], axis=0)
                row = pl.multiple_of(24 * per_source * k + 48 * i, 16)
                for part, piece in enumerate(split(values, 2)):
                    table_ref[f, pl.ds(row, 48), 256 * part : 256 * part + 256] = piece
                for e in range(2):
                    tail_ref[pl.ds(per_source * k + 2 * i + e, 1), :] = source[144 + other : 145 + other, lanes[e]]
                return carry

            lax.fori_loop(0, per_source // 2, pair, 0)
        for part, piece in enumerate(split(tail_ref[...], 2)):
            table_ref[f, body_rows : body_rows + tiles, 256 * part : 256 * part + 256] = piece


def look_up(table_ref, f, low, high):
    tiles = table_ref.shape[1] // 25
    chosen = jnp.where(lax.broadcasted_iota(jnp.int32, (256, 256), 0) == low, 1.0, 0.0).astype(BF16)
    found = jnp.dot(table_ref[f], jnp.concatenate([chosen, chosen], axis=0), preferred_element_type=F32)
    high24 = jnp.broadcast_to(high, (24, 256))
    picked = jnp.zeros((24, 256), F32)
    for h in range(tiles):
        picked = jnp.where(high24 == h, found[24 * h : 24 * h + 24], picked)
    last = jnp.where(lax.broadcasted_iota(jnp.int32, (tiles, 256), 0) == high, found[24 * tiles :], 0.0)
    return picked, jnp.sum(last, axis=0, keepdims=True)


def own_kernel(link_ref, faces_ref, out_ref, table_ref, tail_ref):
    per_source = faces_ref.shape[1] // 256

    @pl.when(pl.program_id(0) == 0)
    def _():
        fill_face_table(table_ref, tail_ref, (faces_ref,))

    here = pl.ds(pl.multiple_of(pl.program_id(0) * 256, 256), 256)
    for f in range(6):
        link = link_ref[f : f + 1, here]
        picked, last = look_up(table_ref, f, link & 255, (link >> 8) - per_source)
        out_ref[25 * f : 25 * f + 24, :] = faces_ref[24 * f : 24 * f + 24, here] + picked
        out_ref[25 * f + 24 : 25 * f + 25, :] = faces_ref[144 + f : 145 + f, here] + last


def neighbour_kernel(link_ref, before_ref, after_ref, part_ref, out_ref, table_ref, tail_ref, unpacked_before, unpacked_after):
    per_source = unpacked_before.shape[1] // 256

    @pl.when(pl.program_id(0) == 0)
    def _():
        def tile(i, carry):
            for packed, unpacked in ((before_ref, unpacked_before), (after_ref, unpacked_after)):
                unpack_tile(FACE_ROWS, FACE_CHUNK, 150, packed, unpacked, i)
            return carry

        lax.fori_loop(0, unpacked_before.shape[1] // 128, tile, 0)
        fill_face_table(table_ref, tail_ref, (unpacked_before, unpacked_after))

    here = pl.ds(pl.multiple_of(pl.program_id(0) * 256, 256), 256)
    for f in range(6):
        link = link_ref[f : f + 1, here]
        high = link >> 8
        high = jnp.where(high < per_source, high, jnp.where(high < 2 * per_source, -1, high - per_source))
        picked, last = look_up(table_ref, f, link & 255, high)
        out_ref[25 * f : 25 * f + 24, :] = part_ref[25 * f : 25 * f + 24, :] + picked
        out_ref[25 * f + 24 : 25 * f + 25, :] = part_ref[25 * f + 24 : 25 * f + 25, :] + last


def collect_own(faces, links):
    slots = faces.shape[1]
    tiles = slots // 256
    return pl.pallas_call(
        own_kernel,
        out_shape=jax.ShapeDtypeStruct((150, slots), F32),
        grid=(tiles,),
        in_specs=[whole(links), whole(faces)],
        out_specs=pl.BlockSpec((150, 256), lambda i: (0, i)),
        scratch_shapes=[pltpu.VMEM((6, 25 * tiles, 512), BF16), pltpu.VMEM((tiles, 256), F32)],
        compiler_params=pltpu.CompilerParams(vmem_limit_bytes=VMEM),
        cost_estimate=pl.CostEstimate(flops=0, bytes_accessed=1024, transcendentals=0),
        name="collect_own",
    )(links, faces)


def collect_neighbours(part, before, after, links):
    slots = part.shape[1]
    tiles = 2 * slots // 256
    block = pl.BlockSpec((150, 256), lambda i: (0, i))
    return pl.pallas_call(
        neighbour_kernel,
        out_shape=jax.ShapeDtypeStruct((150, slots), F32),
        grid=(slots // 256,),
        in_specs=[whole(links), whole(before), whole(after), block],
        out_specs=block,
        scratch_shapes=[
            pltpu.VMEM((6, 25 * tiles, 512), BF16),
            pltpu.VMEM((tiles, 256), F32),
            pltpu.VMEM((150, slots), F32),
            pltpu.VMEM((150, slots), F32),
        ],
        compiler_params=pltpu.CompilerParams(vmem_limit_bytes=VMEM),
        cost_estimate=pl.CostEstimate(flops=10**12, bytes_accessed=10**9, transcendentals=0),
        name="collect_neighbours",
    )(links, before, after, part)


def exchanged(rows, devices, tile):
    blocks = rows.reshape(devices, rows.shape[0] // devices // tile, tile, 128)
    return lax.all_to_all(blocks, ("seg", "rank"), split_axis=0, concat_axis=0, tiled=True).reshape(rows.shape)


def body(parent_nodes, marks, child_owner, face_link):
    devices = lax.axis_size("seg") * lax.axis_size("rank")
    kids = child_owner.shape[0]
    capacity = max(2, 2 * kids // devices)
    slots = devices * capacity
    faces, masses = make_outgoing(parent_nodes.T, marks, child_owner.reshape(kids // 128, 128), devices, capacity)
    arrived = exchanged(faces, devices, 4)
    arrived, masses = lax.optimization_barrier((arrived, masses))
    before = shifted(arrived, "rank", 1)
    after = shifted(arrived, "rank", -1)
    faces = unpack(arrived, slots, FACE_ROWS, FACE_CHUNK, 150, "unpack_faces")
    part = collect_own(faces, face_link.T)
    masses, part = lax.optimization_barrier((masses, part))
    masses = exchanged(masses, devices, 8)
    part, before, after = lax.optimization_barrier((part, before, after))
    face_mass = collect_neighbours(part, before, after, face_link.T)
    masses, face_mass = lax.optimization_barrier((masses, face_mass))
    return (unpack(masses, slots, MASS_ROWS, MASS_ROWS, 125, "unpack_masses"), face_mass)


def solution(mesh):
    return jax.shard_map(
        body,
        mesh=mesh,
        in_specs=(P(("seg", "rank"), None),) * 4,
        out_specs=(P(None, ("seg", "rank")), P(None, ("seg", "rank"))),
        check_vma=False,
    )
```

```python
import functools
import math

import jax
import jax.numpy as jnp
import numpy as np
from jax import lax
from jax.experimental import pallas as pl
from jax.experimental.pallas import tpu as pltpu
from jax.sharding import PartitionSpec as P

F32 = jnp.float32
BF16 = jnp.bfloat16
PARTS = 2
VMEM = 60 << 20
GROUPS = 8
FACE_ROWS = 19
FACES = GROUPS * FACE_ROWS
FACE_CHUNK = 20
MASS_ROWS = 16
MASS = GROUPS * MASS_ROWS


def shifted(array, axis, by):
    count = lax.axis_size(axis)
    pairs = [(i, i + by) for i in range(count) if 0 <= i + by < count]
    return lax.ppermute(array, axis, pairs)


def gll_tables():
    points = np.array([-1.0, -math.sqrt(3.0 / 7.0), 0.0, math.sqrt(3.0 / 7.0), 1.0])
    weights = np.array([0.1, 49.0 / 90.0, 32.0 / 45.0, 49.0 / 90.0, 0.1])
    barycentric = np.array(
        [1.0 / np.prod([points[j] - points[m] for m in range(5) if m != j]) for j in range(5)]
    )
    slopes = np.zeros((5, 5))
    for i in range(5):
        for j in range(5):
            if i != j:
                slopes[i, j] = barycentric[j] / barycentric[i] / (points[i] - points[j])
        slopes[i, i] = -np.sum(slopes[i])

    def lagrange_at(where):
        table = np.ones((5, 5))
        for a in range(5):
            for j in range(5):
                for m in range(5):
                    if m != j:
                        table[a, j] *= (where[a] - points[m]) / (points[j] - points[m])
        return table

    def blend(value, side):
        return (1.0 - value) / 2.0 if side == 0 else (1.0 + value) / 2.0

    def flat(i, j, k):
        return i * 25 + j * 5 + k

    ends = (0, 4)
    gordon = np.zeros((125, 125))
    for i in range(5):
        for j in range(5):
            for k in range(5):
                r, s, t = (points[i], points[j], points[k])
                target = flat(i, j, k)
                for a in range(2):
                    gordon[target, flat(ends[a], j, k)] += blend(r, a)
                    gordon[target, flat(i, ends[a], k)] += blend(s, a)
                    gordon[target, flat(i, j, ends[a])] += blend(t, a)
                    for b in range(2):
                        gordon[target, flat(ends[a], ends[b], k)] -= blend(r, a) * blend(s, b)
                        gordon[target, flat(ends[a], j, ends[b])] -= blend(r, a) * blend(t, b)
                        gordon[target, flat(i, ends[a], ends[b])] -= blend(s, a) * blend(t, b)
                        for c in range(2):
                            gordon[target, flat(ends[a], ends[b], ends[c])] += (
                                blend(r, a) * blend(s, b) * blend(t, c)
                            )
    children = np.zeros((8, 125, 125))
    for octant in range(8):
        shifts = [2 * (octant >> 2 & 1) - 1, 2 * (octant >> 1 & 1) - 1, 2 * (octant & 1) - 1]
        tables = [lagrange_at((points + shifts[q]) / 2.0) for q in range(3)]
        children[octant] = np.kron(np.kron(tables[0], tables[1]), tables[2]) @ gordon
    identity = np.eye(5)
    derivs = [
        np.kron(np.kron(slopes, identity), identity),
        np.kron(np.kron(identity, slopes), identity),
        np.kron(np.kron(identity, identity), slopes),
    ]
    deriv_table = np.concatenate([derivs[q].T for q in range(3)], axis=1)
    mass_weights = np.kron(np.kron(weights, weights), weights)
    face_weights = np.kron(weights, weights)
    tangents = [(1, 2), (1, 2), (0, 2), (0, 2), (0, 1), (0, 1)]
    boundary = [
        flat(i, j, k)
        for i in range(5)
        for j in range(5)
        for k in range(5)
        if i in ends or j in ends or k in ends
    ]
    children_map = children.transpose(2, 0, 1).reshape(125, 1000)
    return (children_map, deriv_table, mass_weights, face_weights, tangents, np.array(boundary))


def split(value, parts):
    pieces = []
    for _ in range(parts):
        piece = value.astype(BF16)
        pieces.append(piece)
        value = value - piece.astype(F32)
    return pieces


def flipped(blocks):
    lanes = lax.broadcasted_iota(jnp.int32, blocks[0].shape, 1) // (128 // GROUPS)
    blocks = list(blocks)
    for bit in (1, 2, 4):
        low = (lanes & bit) == 0
        step = bit * (128 // GROUPS)
        for i in range(GROUPS):
            if i & bit == 0:
                a, c = blocks[i], blocks[i | bit]
                blocks[i] = jnp.where(low, a, pltpu.roll(c, step, 1))
                blocks[i | bit] = jnp.where(low, pltpu.roll(a, 128 - step, 1), c)
    return blocks


def face_order():
    return [25 * f + p for f in range(6) for p in range(24)] + [25 * f + 24 for f in range(6)]


def constants():
    children_map, deriv_table, mass_weights, face_weights, tangents, _ = gll_tables()
    child = np.zeros((8, 128, 128))
    child[:, :125, :125] = children_map.reshape(125, 8, 125).transpose(1, 2, 0)
    derivs = deriv_table.reshape(125, 3, 125).transpose(1, 2, 0)
    grid = np.arange(125).reshape(5, 5, 5)
    face_rows = np.zeros((2 * FACES, 128))
    for face in range(6):
        nodes = np.take(grid, 0 if face % 2 == 0 else 4, axis=face // 2).reshape(-1)
        for p in range(25):
            n = 24 * face + p if p < 24 else 144 + face
            face_rows[n, :125] = face_weights[p] * derivs[tangents[face][0]][nodes[p]]
            face_rows[FACES + n, :125] = derivs[tangents[face][1]][nodes[p]]
    mass_rows = np.zeros((3 * MASS, 128))
    for d in range(3):
        weights = mass_weights[:, None] if d == 0 else 1.0
        mass_rows[d * MASS : d * MASS + 125, :125] = weights * derivs[d]
    child = child.reshape(1024, 128)
    return [jnp.asarray(np.concatenate([child, rows]), F32) for rows in (face_rows, mass_rows)]


def face_values(deriv_ref, row, marked):
    u = [deriv_ref[row : row + 8, c * marked : (c + 1) * marked] for c in range(3)]
    v = [deriv_ref[FACES + row : FACES + row + 8, c * marked : (c + 1) * marked] for c in range(3)]
    nx = u[1] * v[2] - u[2] * v[1]
    ny = u[2] * v[0] - u[0] * v[2]
    nz = u[0] * v[1] - u[1] * v[0]
    return jnp.sqrt(nx * nx + ny * ny + nz * nz)


def mass_values(deriv_ref, row, marked):
    j = [
        [deriv_ref[d * MASS + row : d * MASS + row + 8, c * marked : (c + 1) * marked] for d in range(3)]
        for c in range(3)
    ]
    return (
        j[0][0] * (j[1][1] * j[2][2] - j[1][2] * j[2][1])
        - j[0][1] * (j[1][0] * j[2][2] - j[1][2] * j[2][0])
        + j[0][2] * (j[1][0] * j[2][1] - j[1][1] * j[2][0])
    )


def child_kernel(
    values, rows, chunk, capacity, nodes_hbm, marks_hbm, owner_hbm, table_hbm, out_ref,
    nodes_ref, marks_ref, owner_ref, table_ref, sems, pick_ref, x_ref, cc_ref, dd_ref, deriv_a, deriv_b,
    vals_ref, natural_ref, target_ref, *buffers,
):
    elements = nodes_ref.shape[1]
    marked = marks_ref.shape[1]
    kids = 8 * marked
    height = GROUPS * rows
    onehots, ys = buffers[: len(buffers) // 2], buffers[len(buffers) // 2 :]
    columns = onehots[0].shape[1]
    destinations = columns // capacity
    devices = out_ref.shape[0] // chunk * pl.num_programs(0)

    @pl.when(pl.program_id(0) == 0)
    def _():
        copies = [
            pltpu.make_async_copy(source, kept, sems.at[i])
            for i, (source, kept) in enumerate(
                ((owner_hbm, owner_ref), (marks_hbm, marks_ref), (table_hbm, table_ref))
            )
        ]
        chunks = [
            pltpu.make_async_copy(
                nodes_hbm.at[:, pl.ds(at, 512)], nodes_ref.at[:, pl.ds(at, 512)], sems.at[3 + at // 512]
            )
            for at in range(0, elements, 512)
        ]
        for copy in copies[:2] + chunks + copies[2:]:
            copy.start()

        owner_rows = lax.broadcasted_iota(jnp.int32, (devices, 128), 0)
        earlier = lax.broadcasted_iota(jnp.int32, (128, 128), 0) < lax.broadcasted_iota(jnp.int32, (128, 128), 1)
        earlier = jnp.where(earlier, 1.0, 0.0).astype(BF16)
        ones = jnp.ones((128, 128), BF16)
        copies[0].wait()
        seen = jnp.zeros((devices, 128), F32)
        for b in range(kids // 128):
            owner = owner_ref[b : b + 1, :]
            same = owner_rows == owner
            same_b = jnp.where(same, 1.0, 0.0).astype(BF16)
            before = jnp.dot(same_b, earlier, preferred_element_type=F32) + seen
            position = jnp.sum(jnp.where(same, before, 0.0), axis=0, keepdims=True)
            target = owner.astype(F32) * capacity + position
            natural_ref[128 * b : 128 * b + 128, :] = jnp.broadcast_to(target, (128, 128)).T.astype(jnp.int32)
            seen = seen + jnp.dot(same_b, ones, preferred_element_type=F32)
        for o in range(8):
            target_ref[o * marked : (o + 1) * marked, :] = natural_ref[pl.ds(o, marked, stride=8), :]

        pick_ref[...] = jnp.zeros_like(pick_ref)
        copies[1].wait()
        marks = marks_ref[...]

        def pick(k, carry):
            start = pl.multiple_of(k * 256, 256)
            where = lax.broadcasted_iota(jnp.int32, (256, marked), 0) + start
            chosen = jnp.where(where == marks, 1.0, 0.0).astype(BF16)
            for piece in split(nodes_ref[:, pl.ds(start, 256)], 3):
                pick_ref[0:375, :] += jnp.dot(piece, chosen, preferred_element_type=F32)
            return carry

        for k, copy in enumerate(chunks):
            copy.wait()
            lax.fori_loop(2 * k, 2 * k + 2, pick, 0)
        copies[2].wait()
        for c in range(3):
            x = pick_ref[125 * c : 125 * c + 128, :]
            x = x - 0.5 * (x[0:1] + x[124:125])
            a1, a2, a3 = split(x, 3)
            for k, piece in enumerate((a1, a2, a1, a3, a2, a1)):
                x_ref[128 * k : 128 * k + 128, c * marked : (c + 1) * marked] = piece
        c1, c2, c3 = split(table_ref[0:1024, :], 3)
        for k, piece in enumerate((c1, c1, c2, c1, c2, c3)):
            cc_ref[:, 128 * k : 128 * k + 128] = piece
        d1, d2 = split(table_ref[1024:, :], 2)
        for k, piece in enumerate((d1, d1, d2, d2)):
            dd_ref[:, 128 * k : 128 * k + 128] = piece

        def octants(i, carry):
            for e, deriv_ref in enumerate((deriv_a, deriv_b)):
                o = 2 * i + e
                coords = jnp.dot(
                    cc_ref[pl.ds(pl.multiple_of(o * 128, 128), 128), :], x_ref[...], preferred_element_type=F32
                )
                y1, y2 = split(coords - coords[62:63], 2)
                deriv_ref[...] = jnp.dot(
                    dd_ref[...], jnp.concatenate([y1, y2, y1, y2], axis=0), preferred_element_type=F32
                )
                lanes = pl.ds(pl.multiple_of(o * marked, 128), marked)
                for row in range(0, height, 8):
                    v1, v2 = split(values(deriv_ref, row, marked), 2)
                    vals_ref[row : row + 8, lanes] = v1
                    vals_ref[height + row : height + row + 8, lanes] = v2
            return carry

        lax.fori_loop(0, 4, octants, 0)

    numbers = lax.broadcasted_iota(jnp.int32, (128, 128), 1)

    base = pl.program_id(0) * (out_ref.shape[0] // chunk * capacity)
    parts = list(enumerate(zip(onehots, ys)))
    for i, (onehot_ref, y_ref) in parts:
        for at in range(0, kids, 128):
            target = target_ref[at : at + 128, :] - (base + i * columns)
            for tile in range(columns // 128):
                onehot_ref[at : at + 128, 128 * tile : 128 * tile + 128] = jnp.where(
                    target == numbers + 128 * tile, 1.0, 0.0
                ).astype(BF16)
        moved = jnp.dot(vals_ref[...], onehot_ref[...], preferred_element_type=F32)
        y_ref[...] = moved[0:height] + moved[height:]
    for i, (_, y_ref) in parts:
        for tile in range(columns // 128):
            lanes = slice(128 * tile, 128 * tile + 128)
            blocks = flipped([y_ref[rows * g : rows * (g + 1), lanes] for g in range(GROUPS)])
            if chunk > rows:
                blocks = [jnp.concatenate([b, jnp.zeros((chunk - rows, 128), F32)], axis=0) for b in blocks]
            start = (i * destinations + tile * GROUPS) * chunk
            out_ref[start : start + GROUPS * chunk, :] = jnp.concatenate(blocks, axis=0)


def whole(a):
    return pl.BlockSpec(a.shape, lambda i: (0, 0))


def outgoing(values, rows, chunk, table, nodes, marks, owner, devices, capacity, name):
    marked = marks.shape[1]
    kids = 8 * marked
    operands = (nodes, marks, owner, table)
    steps = 4
    height = GROUPS * rows
    return pl.pallas_call(
        functools.partial(child_kernel, values, rows, chunk, capacity),
        out_shape=jax.ShapeDtypeStruct((devices * chunk, 128), F32),
        grid=(steps,),
        in_specs=[pl.BlockSpec(memory_space=pltpu.HBM)] * 4,
        out_specs=pl.BlockSpec((devices * chunk // steps, 128), lambda i: (i, 0)),
        scratch_shapes=[
            *(pltpu.VMEM(a.shape, a.dtype) for a in operands),
            pltpu.SemaphoreType.DMA((3 + nodes.shape[1] // 512,)),
            pltpu.VMEM((384, marked), F32),
            pltpu.VMEM((768, 3 * marked), BF16),
            pltpu.VMEM((1024, 768), BF16),
            pltpu.VMEM((table.shape[0] - 1024, 512), BF16),
            pltpu.VMEM((table.shape[0] - 1024, 3 * marked), F32),
            pltpu.VMEM((table.shape[0] - 1024, 3 * marked), F32),
            pltpu.VMEM((2 * height, kids), BF16),
            pltpu.VMEM((kids, 128), jnp.int32),
            pltpu.VMEM((kids, 128), jnp.int32),
            *(pltpu.VMEM((kids, 1024 // PARTS), BF16) for _ in range(PARTS)),
            *(pltpu.VMEM((height, 1024 // PARTS), F32) for _ in range(PARTS)),
        ],
        compiler_params=pltpu.CompilerParams(vmem_limit_bytes=VMEM),
        name=name,
    )(*operands)


def make_outgoing(nodes, marks, owner, devices, capacity):
    face_table, mass_table = constants()
    args = (nodes, marks, owner, devices, capacity)
    return (
        outgoing(face_values, FACE_ROWS, FACE_CHUNK, face_table, *args, "faces"),
        outgoing(mass_values, MASS_ROWS, MASS_ROWS, mass_table, *args, "masses"),
    )


def unpack_tile(rows, chunk, height, in_ref, out_ref, tile):
    start = pl.multiple_of(tile * (chunk * GROUPS), 8)
    lanes = pl.ds(pl.multiple_of(tile * 128, 128), 128)
    arrived = in_ref[pl.ds(start, chunk * GROUPS), :]
    blocks = flipped([arrived[chunk * j : chunk * j + rows] for j in range(GROUPS)])
    for g in range(GROUPS):
        count = min(rows, height - rows * g)
        out_ref[rows * g : rows * g + count, lanes] = blocks[g][0:count]


def unpack_kernel(rows, chunk, height, in_ref, out_ref):
    def tiles(i, carry):
        for k in range(4):
            unpack_tile(rows, chunk, height, in_ref, out_ref, 4 * i + k)
        return carry

    lax.fori_loop(0, out_ref.shape[1] // 512, tiles, 0)


def unpack(arrived, slots, rows, chunk, height, name):
    return pl.pallas_call(
        functools.partial(unpack_kernel, rows, chunk, height),
        out_shape=jax.ShapeDtypeStruct((height, slots), F32),
        grid=(slots // 1024,),
        in_specs=[pl.BlockSpec((8 * GROUPS * chunk, 128), lambda i: (i, 0))],
        out_specs=pl.BlockSpec((height, 1024), lambda i: (0, i)),
        compiler_params=pltpu.CompilerParams(vmem_limit_bytes=VMEM),
        name=name,
    )(arrived)


def fill_face_table(table_ref, tail_ref, sources):
    per_source = sources[0].shape[1] // 256
    tiles = len(sources) * per_source
    body_rows = 24 * tiles
    for f in range(6):
        other = f + 1 - 2 * (f % 2)
        for k, source in enumerate(sources):

            def pair(i, carry):
                lanes = [pl.ds(pl.multiple_of(512 * i + 256 * e, 256), 256) for e in range(2)]
                values = jnp.concatenate([source[24 * other : 24 * other + 24, l] for l in lanes], axis=0)
                row = pl.multiple_of(24 * per_source * k + 48 * i, 16)
                for part, piece in enumerate(split(values, 2)):
                    table_ref[f, pl.ds(row, 48), 256 * part : 256 * part + 256] = piece
                for e in range(2):
                    tail_ref[pl.ds(per_source * k + 2 * i + e, 1), :] = source[144 + other : 145 + other, lanes[e]]
                return carry

            lax.fori_loop(0, per_source // 2, pair, 0)
        for part, piece in enumerate(split(tail_ref[...], 2)):
            table_ref[f, body_rows : body_rows + tiles, 256 * part : 256 * part + 256] = piece


def look_up(table_ref, f, low, high):
    tiles = table_ref.shape[1] // 25
    chosen = jnp.where(lax.broadcasted_iota(jnp.int32, (256, 256), 0) == low, 1.0, 0.0).astype(BF16)
    found = jnp.dot(table_ref[f], jnp.concatenate([chosen, chosen], axis=0), preferred_element_type=F32)
    high24 = jnp.broadcast_to(high, (24, 256))
    picked = jnp.zeros((24, 256), F32)
    for h in range(tiles):
        picked = jnp.where(high24 == h, found[24 * h : 24 * h + 24], picked)
    last = jnp.where(lax.broadcasted_iota(jnp.int32, (tiles, 256), 0) == high, found[24 * tiles :], 0.0)
    return picked, jnp.sum(last, axis=0, keepdims=True)


def own_kernel(link_ref, faces_ref, out_ref, table_ref, tail_ref):
    per_source = faces_ref.shape[1] // 256

    @pl.when(pl.program_id(0) == 0)
    def _():
        fill_face_table(table_ref, tail_ref, (faces_ref,))

    here = pl.ds(pl.multiple_of(pl.program_id(0) * 256, 256), 256)
    for f in range(6):
        link = link_ref[f : f + 1, here]
        picked, last = look_up(table_ref, f, link & 255, (link >> 8) - per_source)
        out_ref[25 * f : 25 * f + 24, :] = faces_ref[24 * f : 24 * f + 24, here] + picked
        out_ref[25 * f + 24 : 25 * f + 25, :] = faces_ref[144 + f : 145 + f, here] + last


def neighbour_kernel(link_ref, before_ref, after_ref, part_ref, out_ref, table_ref, tail_ref, unpacked_before, unpacked_after):
    per_source = unpacked_before.shape[1] // 256

    @pl.when(pl.program_id(0) == 0)
    def _():
        def tile(i, carry):
            for packed, unpacked in ((before_ref, unpacked_before), (after_ref, unpacked_after)):
                unpack_tile(FACE_ROWS, FACE_CHUNK, 150, packed, unpacked, i)
            return carry

        lax.fori_loop(0, unpacked_before.shape[1] // 128, tile, 0)
        fill_face_table(table_ref, tail_ref, (unpacked_before, unpacked_after))

    here = pl.ds(pl.multiple_of(pl.program_id(0) * 256, 256), 256)
    for f in range(6):
        link = link_ref[f : f + 1, here]
        high = link >> 8
        high = jnp.where(high < per_source, high, jnp.where(high < 2 * per_source, -1, high - per_source))
        picked, last = look_up(table_ref, f, link & 255, high)
        out_ref[25 * f : 25 * f + 24, :] = part_ref[25 * f : 25 * f + 24, :] + picked
        out_ref[25 * f + 24 : 25 * f + 25, :] = part_ref[25 * f + 24 : 25 * f + 25, :] + last


def collect_own(faces, links):
    slots = faces.shape[1]
    tiles = slots // 256
    return pl.pallas_call(
        own_kernel,
        out_shape=jax.ShapeDtypeStruct((150, slots), F32),
        grid=(tiles,),
        in_specs=[whole(links), whole(faces)],
        out_specs=pl.BlockSpec((150, 256), lambda i: (0, i)),
        scratch_shapes=[pltpu.VMEM((6, 25 * tiles, 512), BF16), pltpu.VMEM((tiles, 256), F32)],
        compiler_params=pltpu.CompilerParams(vmem_limit_bytes=VMEM),
        cost_estimate=pl.CostEstimate(flops=0, bytes_accessed=1024, transcendentals=0),
        name="collect_own",
    )(links, faces)


def collect_neighbours(part, before, after, links):
    slots = part.shape[1]
    tiles = 2 * slots // 256
    block = pl.BlockSpec((150, 256), lambda i: (0, i))
    return pl.pallas_call(
        neighbour_kernel,
        out_shape=jax.ShapeDtypeStruct((150, slots), F32),
        grid=(slots // 256,),
        in_specs=[whole(links), whole(before), whole(after), block],
        out_specs=block,
        scratch_shapes=[
            pltpu.VMEM((6, 25 * tiles, 512), BF16),
            pltpu.VMEM((tiles, 256), F32),
            pltpu.VMEM((150, slots), F32),
            pltpu.VMEM((150, slots), F32),
        ],
        compiler_params=pltpu.CompilerParams(vmem_limit_bytes=VMEM),
        cost_estimate=pl.CostEstimate(flops=10**12, bytes_accessed=10**9, transcendentals=0),
        name="collect_neighbours",
    )(links, before, after, part)


def exchanged(rows, devices, tile):
    blocks = rows.reshape(devices, rows.shape[0] // devices // tile, tile, 128)
    return lax.all_to_all(blocks, ("seg", "rank"), split_axis=0, concat_axis=0, tiled=True).reshape(rows.shape)


def body(parent_nodes, marks, child_owner, face_link):
    devices = lax.axis_size("seg") * lax.axis_size("rank")
    kids = child_owner.shape[0]
    capacity = max(2, 2 * kids // devices)
    slots = devices * capacity
    faces, masses = make_outgoing(parent_nodes.T, marks, child_owner.reshape(kids // 128, 128), devices, capacity)
    arrived = exchanged(faces, devices, 4)
    arrived, masses = lax.optimization_barrier((arrived, masses))
    before = shifted(arrived, "rank", 1)
    after = shifted(arrived, "rank", -1)
    faces = unpack(arrived, slots, FACE_ROWS, FACE_CHUNK, 150, "unpack_faces")
    part = collect_own(faces, face_link.T)
    masses, part = lax.optimization_barrier((masses, part))
    masses = exchanged(masses, devices, 8)
    part, before, after = lax.optimization_barrier((part, before, after))
    face_mass = collect_neighbours(part, before, after, face_link.T)
    masses, face_mass = lax.optimization_barrier((masses, face_mass))
    return (unpack(masses, slots, MASS_ROWS, MASS_ROWS, 125, "unpack_masses"), face_mass)


def solution(mesh):
    return jax.shard_map(
        body,
        mesh=mesh,
        in_specs=(P(("seg", "rank"), None),) * 4,
        out_specs=(P(None, ("seg", "rank")), P(None, ("seg", "rank"))),
        check_vma=False,
    )
```

```python
import functools
import math

import jax
import jax.numpy as jnp
import numpy as np
from jax import lax
from jax.experimental import pallas as pl
from jax.experimental.pallas import tpu as pltpu
from jax.sharding import PartitionSpec as P

F32 = jnp.float32
BF16 = jnp.bfloat16
PARTS = 2
VMEM = 60 << 20
GROUPS = 8
FACE_ROWS = 19
FACES = GROUPS * FACE_ROWS
FACE_CHUNK = 19
MASS_ROWS = 16
MASS = GROUPS * MASS_ROWS


def shifted(array, axis, by):
    count = lax.axis_size(axis)
    pairs = [(i, i + by) for i in range(count) if 0 <= i + by < count]
    return lax.ppermute(array, axis, pairs)


def gll_tables():
    points = np.array([-1.0, -math.sqrt(3.0 / 7.0), 0.0, math.sqrt(3.0 / 7.0), 1.0])
    weights = np.array([0.1, 49.0 / 90.0, 32.0 / 45.0, 49.0 / 90.0, 0.1])
    barycentric = np.array(
        [1.0 / np.prod([points[j] - points[m] for m in range(5) if m != j]) for j in range(5)]
    )
    slopes = np.zeros((5, 5))
    for i in range(5):
        for j in range(5):
            if i != j:
                slopes[i, j] = barycentric[j] / barycentric[i] / (points[i] - points[j])
        slopes[i, i] = -np.sum(slopes[i])

    def lagrange_at(where):
        table = np.ones((5, 5))
        for a in range(5):
            for j in range(5):
                for m in range(5):
                    if m != j:
                        table[a, j] *= (where[a] - points[m]) / (points[j] - points[m])
        return table

    def blend(value, side):
        return (1.0 - value) / 2.0 if side == 0 else (1.0 + value) / 2.0

    def flat(i, j, k):
        return i * 25 + j * 5 + k

    ends = (0, 4)
    gordon = np.zeros((125, 125))
    for i in range(5):
        for j in range(5):
            for k in range(5):
                r, s, t = (points[i], points[j], points[k])
                target = flat(i, j, k)
                for a in range(2):
                    gordon[target, flat(ends[a], j, k)] += blend(r, a)
                    gordon[target, flat(i, ends[a], k)] += blend(s, a)
                    gordon[target, flat(i, j, ends[a])] += blend(t, a)
                    for b in range(2):
                        gordon[target, flat(ends[a], ends[b], k)] -= blend(r, a) * blend(s, b)
                        gordon[target, flat(ends[a], j, ends[b])] -= blend(r, a) * blend(t, b)
                        gordon[target, flat(i, ends[a], ends[b])] -= blend(s, a) * blend(t, b)
                        for c in range(2):
                            gordon[target, flat(ends[a], ends[b], ends[c])] += (
                                blend(r, a) * blend(s, b) * blend(t, c)
                            )
    children = np.zeros((8, 125, 125))
    for octant in range(8):
        shifts = [2 * (octant >> 2 & 1) - 1, 2 * (octant >> 1 & 1) - 1, 2 * (octant & 1) - 1]
        tables = [lagrange_at((points + shifts[q]) / 2.0) for q in range(3)]
        children[octant] = np.kron(np.kron(tables[0], tables[1]), tables[2]) @ gordon
    identity = np.eye(5)
    derivs = [
        np.kron(np.kron(slopes, identity), identity),
        np.kron(np.kron(identity, slopes), identity),
        np.kron(np.kron(identity, identity), slopes),
    ]
    deriv_table = np.concatenate([derivs[q].T for q in range(3)], axis=1)
    mass_weights = np.kron(np.kron(weights, weights), weights)
    face_weights = np.kron(weights, weights)
    tangents = [(1, 2), (1, 2), (0, 2), (0, 2), (0, 1), (0, 1)]
    boundary = [
        flat(i, j, k)
        for i in range(5)
        for j in range(5)
        for k in range(5)
        if i in ends or j in ends or k in ends
    ]
    children_map = children.transpose(2, 0, 1).reshape(125, 1000)
    return (children_map, deriv_table, mass_weights, face_weights, tangents, np.array(boundary))


def split(value, parts):
    pieces = []
    for _ in range(parts):
        piece = value.astype(BF16)
        pieces.append(piece)
        value = value - piece.astype(F32)
    return pieces


def flipped(blocks):
    lanes = lax.broadcasted_iota(jnp.int32, blocks[0].shape, 1) // (128 // GROUPS)
    blocks = list(blocks)
    for bit in (1, 2, 4):
        low = (lanes & bit) == 0
        step = bit * (128 // GROUPS)
        for i in range(GROUPS):
            if i & bit == 0:
                a, c = blocks[i], blocks[i | bit]
                blocks[i] = jnp.where(low, a, pltpu.roll(c, step, 1))
                blocks[i | bit] = jnp.where(low, pltpu.roll(a, 128 - step, 1), c)
    return blocks


def face_order():
    return [25 * f + p for f in range(6) for p in range(24)] + [25 * f + 24 for f in range(6)]


def constants():
    children_map, deriv_table, mass_weights, face_weights, tangents, _ = gll_tables()
    child = np.zeros((8, 128, 128))
    child[:, :125, :125] = children_map.reshape(125, 8, 125).transpose(1, 2, 0)
    derivs = deriv_table.reshape(125, 3, 125).transpose(1, 2, 0)
    grid = np.arange(125).reshape(5, 5, 5)
    face_rows = np.zeros((2 * FACES, 128))
    for face in range(6):
        nodes = np.take(grid, 0 if face % 2 == 0 else 4, axis=face // 2).reshape(-1)
        for p in range(25):
            n = 24 * face + p if p < 24 else 144 + face
            face_rows[n, :125] = face_weights[p] * derivs[tangents[face][0]][nodes[p]]
            face_rows[FACES + n, :125] = derivs[tangents[face][1]][nodes[p]]
    mass_rows = np.zeros((3 * MASS, 128))
    for d in range(3):
        weights = mass_weights[:, None] if d == 0 else 1.0
        mass_rows[d * MASS : d * MASS + 125, :125] = weights * derivs[d]
    child = child.reshape(1024, 128)
    return [jnp.asarray(np.concatenate([child, rows]), F32) for rows in (face_rows, mass_rows)]


def face_values(deriv_ref, row, marked):
    u = [deriv_ref[row : row + 8, c * marked : (c + 1) * marked] for c in range(3)]
    v = [deriv_ref[FACES + row : FACES + row + 8, c * marked : (c + 1) * marked] for c in range(3)]
    nx = u[1] * v[2] - u[2] * v[1]
    ny = u[2] * v[0] - u[0] * v[2]
    nz = u[0] * v[1] - u[1] * v[0]
    return jnp.sqrt(nx * nx + ny * ny + nz * nz)


def mass_values(deriv_ref, row, marked):
    j = [
        [deriv_ref[d * MASS + row : d * MASS + row + 8, c * marked : (c + 1) * marked] for d in range(3)]
        for c in range(3)
    ]
    return (
        j[0][0] * (j[1][1] * j[2][2] - j[1][2] * j[2][1])
        - j[0][1] * (j[1][0] * j[2][2] - j[1][2] * j[2][0])
        + j[0][2] * (j[1][0] * j[2][1] - j[1][1] * j[2][0])
    )


def child_kernel(
    values, rows, chunk, capacity, nodes_hbm, marks_hbm, owner_hbm, table_hbm, out_ref,
    nodes_ref, marks_ref, owner_ref, table_ref, sems, pick_ref, x_ref, cc_ref, dd_ref, deriv_a, deriv_b,
    vals_ref, natural_ref, target_ref, *buffers,
):
    elements = nodes_ref.shape[1]
    marked = marks_ref.shape[1]
    kids = 8 * marked
    height = GROUPS * rows
    onehots, ys = buffers[: len(buffers) // 2], buffers[len(buffers) // 2 :]
    columns = onehots[0].shape[1]
    destinations = columns // capacity
    devices = out_ref.shape[0] // chunk * pl.num_programs(0)

    @pl.when(pl.program_id(0) == 0)
    def _():
        copies = [
            pltpu.make_async_copy(source, kept, sems.at[i])
            for i, (source, kept) in enumerate(
                ((owner_hbm, owner_ref), (marks_hbm, marks_ref), (table_hbm, table_ref))
            )
        ]
        chunks = [
            pltpu.make_async_copy(
                nodes_hbm.at[:, pl.ds(at, 512)], nodes_ref.at[:, pl.ds(at, 512)], sems.at[3 + at // 512]
            )
            for at in range(0, elements, 512)
        ]
        for copy in copies[:2] + chunks + copies[2:]:
            copy.start()

        owner_rows = lax.broadcasted_iota(jnp.int32, (devices, 128), 0)
        earlier = lax.broadcasted_iota(jnp.int32, (128, 128), 0) < lax.broadcasted_iota(jnp.int32, (128, 128), 1)
        earlier = jnp.where(earlier, 1.0, 0.0).astype(BF16)
        ones = jnp.ones((128, 128), BF16)
        copies[0].wait()
        seen = jnp.zeros((devices, 128), F32)
        for b in range(kids // 128):
            owner = owner_ref[b : b + 1, :]
            same = owner_rows == owner
            same_b = jnp.where(same, 1.0, 0.0).astype(BF16)
            before = jnp.dot(same_b, earlier, preferred_element_type=F32) + seen
            position = jnp.sum(jnp.where(same, before, 0.0), axis=0, keepdims=True)
            target = owner.astype(F32) * capacity + position
            natural_ref[128 * b : 128 * b + 128, :] = jnp.broadcast_to(target, (128, 128)).T.astype(jnp.int32)
            seen = seen + jnp.dot(same_b, ones, preferred_element_type=F32)
        for o in range(8):
            target_ref[o * marked : (o + 1) * marked, :] = natural_ref[pl.ds(o, marked, stride=8), :]

        pick_ref[...] = jnp.zeros_like(pick_ref)
        copies[1].wait()
        marks = marks_ref[...]

        def pick(k, carry):
            start = pl.multiple_of(k * 256, 256)
            where = lax.broadcasted_iota(jnp.int32, (256, marked), 0) + start
            chosen = jnp.where(where == marks, 1.0, 0.0).astype(BF16)
            for piece in split(nodes_ref[:, pl.ds(start, 256)], 3):
                pick_ref[0:375, :] += jnp.dot(piece, chosen, preferred_element_type=F32)
            return carry

        for k, copy in enumerate(chunks):
            copy.wait()
            lax.fori_loop(2 * k, 2 * k + 2, pick, 0)
        copies[2].wait()
        for c in range(3):
            x = pick_ref[125 * c : 125 * c + 128, :]
            x = x - 0.5 * (x[0:1] + x[124:125])
            a1, a2, a3 = split(x, 3)
            for k, piece in enumerate((a1, a2, a1, a3, a2, a1)):
                x_ref[128 * k : 128 * k + 128, c * marked : (c + 1) * marked] = piece
        c1, c2, c3 = split(table_ref[0:1024, :], 3)
        for k, piece in enumerate((c1, c1, c2, c1, c2, c3)):
            cc_ref[:, 128 * k : 128 * k + 128] = piece
        d1, d2 = split(table_ref[1024:, :], 2)
        for k, piece in enumerate((d1, d1, d2, d2)):
            dd_ref[:, 128 * k : 128 * k + 128] = piece

        def octants(i, carry):
            for e, deriv_ref in enumerate((deriv_a, deriv_b)):
                o = 2 * i + e
                coords = jnp.dot(
                    cc_ref[pl.ds(pl.multiple_of(o * 128, 128), 128), :], x_ref[...], preferred_element_type=F32
                )
                y1, y2 = split(coords - coords[62:63], 2)
                deriv_ref[...] = jnp.dot(
                    dd_ref[...], jnp.concatenate([y1, y2, y1, y2], axis=0), preferred_element_type=F32
                )
                lanes = pl.ds(pl.multiple_of(o * marked, 128), marked)
                for row in range(0, height, 8):
                    v1, v2 = split(values(deriv_ref, row, marked), 2)
                    vals_ref[row : row + 8, lanes] = v1
                    vals_ref[height + row : height + row + 8, lanes] = v2
            return carry

        lax.fori_loop(0, 4, octants, 0)

    numbers = lax.broadcasted_iota(jnp.int32, (128, 128), 1)

    base = pl.program_id(0) * (out_ref.shape[0] // chunk * capacity)
    parts = list(enumerate(zip(onehots, ys)))
    for i, (onehot_ref, y_ref) in parts:
        for at in range(0, kids, 128):
            target = target_ref[at : at + 128, :] - (base + i * columns)
            for tile in range(columns // 128):
                onehot_ref[at : at + 128, 128 * tile : 128 * tile + 128] = jnp.where(
                    target == numbers + 128 * tile, 1.0, 0.0
                ).astype(BF16)
        moved = jnp.dot(vals_ref[...], onehot_ref[...], preferred_element_type=F32)
        y_ref[...] = moved[0:height] + moved[height:]
    for i, (_, y_ref) in parts:
        for tile in range(columns // 128):
            lanes = slice(128 * tile, 128 * tile + 128)
            blocks = flipped([y_ref[rows * g : rows * (g + 1), lanes] for g in range(GROUPS)])
            if chunk > rows:
                blocks = [jnp.concatenate([b, jnp.zeros((chunk - rows, 128), F32)], axis=0) for b in blocks]
            start = (i * destinations + tile * GROUPS) * chunk
            out_ref[start : start + GROUPS * chunk, :] = jnp.concatenate(blocks, axis=0)


def whole(a):
    return pl.BlockSpec(a.shape, lambda i: (0, 0))


def outgoing(values, rows, chunk, table, nodes, marks, owner, devices, capacity, name):
    marked = marks.shape[1]
    kids = 8 * marked
    operands = (nodes, marks, owner, table)
    steps = 4
    height = GROUPS * rows
    return pl.pallas_call(
        functools.partial(child_kernel, values, rows, chunk, capacity),
        out_shape=jax.ShapeDtypeStruct((devices * chunk, 128), F32),
        grid=(steps,),
        in_specs=[pl.BlockSpec(memory_space=pltpu.HBM)] * 4,
        out_specs=pl.BlockSpec((devices * chunk // steps, 128), lambda i: (i, 0)),
        scratch_shapes=[
            *(pltpu.VMEM(a.shape, a.dtype) for a in operands),
            pltpu.SemaphoreType.DMA((3 + nodes.shape[1] // 512,)),
            pltpu.VMEM((384, marked), F32),
            pltpu.VMEM((768, 3 * marked), BF16),
            pltpu.VMEM((1024, 768), BF16),
            pltpu.VMEM((table.shape[0] - 1024, 512), BF16),
            pltpu.VMEM((table.shape[0] - 1024, 3 * marked), F32),
            pltpu.VMEM((table.shape[0] - 1024, 3 * marked), F32),
            pltpu.VMEM((2 * height, kids), BF16),
            pltpu.VMEM((kids, 128), jnp.int32),
            pltpu.VMEM((kids, 128), jnp.int32),
            *(pltpu.VMEM((kids, 1024 // PARTS), BF16) for _ in range(PARTS)),
            *(pltpu.VMEM((height, 1024 // PARTS), F32) for _ in range(PARTS)),
        ],
        compiler_params=pltpu.CompilerParams(vmem_limit_bytes=VMEM),
        name=name,
    )(*operands)


def make_outgoing(nodes, marks, owner, devices, capacity):
    face_table, mass_table = constants()
    args = (nodes, marks, owner, devices, capacity)
    return (
        outgoing(face_values, FACE_ROWS, FACE_CHUNK, face_table, *args, "faces"),
        outgoing(mass_values, MASS_ROWS, MASS_ROWS, mass_table, *args, "masses"),
    )


def unpack_tile(rows, chunk, height, in_ref, out_ref, tile):
    start = pl.multiple_of(tile * (chunk * GROUPS), 8)
    lanes = pl.ds(pl.multiple_of(tile * 128, 128), 128)
    arrived = in_ref[pl.ds(start, chunk * GROUPS), :]
    blocks = flipped([arrived[chunk * j : chunk * j + rows] for j in range(GROUPS)])
    for g in range(GROUPS):
        count = min(rows, height - rows * g)
        out_ref[rows * g : rows * g + count, lanes] = blocks[g][0:count]


def unpack_kernel(rows, chunk, height, in_ref, out_ref):
    def tiles(i, carry):
        for k in range(4):
            unpack_tile(rows, chunk, height, in_ref, out_ref, 4 * i + k)
        return carry

    lax.fori_loop(0, out_ref.shape[1] // 512, tiles, 0)


def unpack(arrived, slots, rows, chunk, height, name):
    return pl.pallas_call(
        functools.partial(unpack_kernel, rows, chunk, height),
        out_shape=jax.ShapeDtypeStruct((height, slots), F32),
        grid=(slots // 1024,),
        in_specs=[pl.BlockSpec((8 * GROUPS * chunk, 128), lambda i: (i, 0))],
        out_specs=pl.BlockSpec((height, 1024), lambda i: (0, i)),
        compiler_params=pltpu.CompilerParams(vmem_limit_bytes=VMEM),
        name=name,
    )(arrived)


def fill_face_table(table_ref, tail_ref, sources):
    per_source = sources[0].shape[1] // 256
    tiles = len(sources) * per_source
    body_rows = 24 * tiles
    for f in range(6):
        other = f + 1 - 2 * (f % 2)
        for k, source in enumerate(sources):

            def pair(i, carry):
                lanes = [pl.ds(pl.multiple_of(512 * i + 256 * e, 256), 256) for e in range(2)]
                values = jnp.concatenate([source[24 * other : 24 * other + 24, l] for l in lanes], axis=0)
                row = pl.multiple_of(24 * per_source * k + 48 * i, 16)
                for part, piece in enumerate(split(values, 2)):
                    table_ref[f, pl.ds(row, 48), 256 * part : 256 * part + 256] = piece
                for e in range(2):
                    tail_ref[pl.ds(per_source * k + 2 * i + e, 1), :] = source[144 + other : 145 + other, lanes[e]]
                return carry

            lax.fori_loop(0, per_source // 2, pair, 0)
        for part, piece in enumerate(split(tail_ref[...], 2)):
            table_ref[f, body_rows : body_rows + tiles, 256 * part : 256 * part + 256] = piece


def look_up(table_ref, f, low, high):
    tiles = table_ref.shape[1] // 25
    chosen = jnp.where(lax.broadcasted_iota(jnp.int32, (256, 256), 0) == low, 1.0, 0.0).astype(BF16)
    found = jnp.dot(table_ref[f], jnp.concatenate([chosen, chosen], axis=0), preferred_element_type=F32)
    high24 = jnp.broadcast_to(high, (24, 256))
    picked = jnp.zeros((24, 256), F32)
    for h in range(tiles):
        picked = jnp.where(high24 == h, found[24 * h : 24 * h + 24], picked)
    last = jnp.where(lax.broadcasted_iota(jnp.int32, (tiles, 256), 0) == high, found[24 * tiles :], 0.0)
    return picked, jnp.sum(last, axis=0, keepdims=True)


def own_kernel(link_ref, faces_ref, out_ref, table_ref, tail_ref):
    per_source = faces_ref.shape[1] // 256

    @pl.when(pl.program_id(0) == 0)
    def _():
        fill_face_table(table_ref, tail_ref, (faces_ref,))

    here = pl.ds(pl.multiple_of(pl.program_id(0) * 256, 256), 256)
    for f in range(6):
        link = link_ref[f : f + 1, here]
        picked, last = look_up(table_ref, f, link & 255, (link >> 8) - per_source)
        out_ref[25 * f : 25 * f + 24, :] = faces_ref[24 * f : 24 * f + 24, here] + picked
        out_ref[25 * f + 24 : 25 * f + 25, :] = faces_ref[144 + f : 145 + f, here] + last


def neighbour_kernel(link_ref, before_ref, after_ref, part_ref, out_ref, table_ref, tail_ref, unpacked_before, unpacked_after):
    per_source = unpacked_before.shape[1] // 256

    @pl.when(pl.program_id(0) == 0)
    def _():
        def tile(i, carry):
            for packed, unpacked in ((before_ref, unpacked_before), (after_ref, unpacked_after)):
                unpack_tile(FACE_ROWS, FACE_CHUNK, 150, packed, unpacked, i)
            return carry

        lax.fori_loop(0, unpacked_before.shape[1] // 128, tile, 0)
        fill_face_table(table_ref, tail_ref, (unpacked_before, unpacked_after))

    here = pl.ds(pl.multiple_of(pl.program_id(0) * 256, 256), 256)
    for f in range(6):
        link = link_ref[f : f + 1, here]
        high = link >> 8
        high = jnp.where(high < per_source, high, jnp.where(high < 2 * per_source, -1, high - per_source))
        picked, last = look_up(table_ref, f, link & 255, high)
        out_ref[25 * f : 25 * f + 24, :] = part_ref[25 * f : 25 * f + 24, :] + picked
        out_ref[25 * f + 24 : 25 * f + 25, :] = part_ref[25 * f + 24 : 25 * f + 25, :] + last


def collect_own(faces, links):
    slots = faces.shape[1]
    tiles = slots // 256
    return pl.pallas_call(
        own_kernel,
        out_shape=jax.ShapeDtypeStruct((150, slots), F32),
        grid=(tiles,),
        in_specs=[whole(links), whole(faces)],
        out_specs=pl.BlockSpec((150, 256), lambda i: (0, i)),
        scratch_shapes=[pltpu.VMEM((6, 25 * tiles, 512), BF16), pltpu.VMEM((tiles, 256), F32)],
        compiler_params=pltpu.CompilerParams(vmem_limit_bytes=VMEM),
        cost_estimate=pl.CostEstimate(flops=0, bytes_accessed=1024, transcendentals=0),
        name="collect_own",
    )(links, faces)


def collect_neighbours(part, before, after, links):
    slots = part.shape[1]
    tiles = 2 * slots // 256
    block = pl.BlockSpec((150, 256), lambda i: (0, i))
    return pl.pallas_call(
        neighbour_kernel,
        out_shape=jax.ShapeDtypeStruct((150, slots), F32),
        grid=(slots // 256,),
        in_specs=[whole(links), whole(before), whole(after), block],
        out_specs=block,
        scratch_shapes=[
            pltpu.VMEM((6, 25 * tiles, 512), BF16),
            pltpu.VMEM((tiles, 256), F32),
            pltpu.VMEM((150, slots), F32),
            pltpu.VMEM((150, slots), F32),
        ],
        compiler_params=pltpu.CompilerParams(vmem_limit_bytes=VMEM),
        cost_estimate=pl.CostEstimate(flops=10**12, bytes_accessed=10**9, transcendentals=0),
        name="collect_neighbours",
    )(links, before, after, part)


def exchanged(rows, devices, tile):
    blocks = rows.reshape(devices, rows.shape[0] // devices // tile, tile, 128)
    return lax.all_to_all(blocks, ("seg", "rank"), split_axis=0, concat_axis=0, tiled=True).reshape(rows.shape)


def body(parent_nodes, marks, child_owner, face_link):
    devices = lax.axis_size("seg") * lax.axis_size("rank")
    kids = child_owner.shape[0]
    capacity = max(2, 2 * kids // devices)
    slots = devices * capacity
    faces, masses = make_outgoing(parent_nodes.T, marks, child_owner.reshape(kids // 128, 128), devices, capacity)
    arrived = exchanged(faces, devices, 1)
    arrived, masses = lax.optimization_barrier((arrived, masses))
    before = shifted(arrived, "rank", 1)
    after = shifted(arrived, "rank", -1)
    faces = unpack(arrived, slots, FACE_ROWS, FACE_CHUNK, 150, "unpack_faces")
    part = collect_own(faces, face_link.T)
    masses, part = lax.optimization_barrier((masses, part))
    masses = exchanged(masses, devices, 8)
    part, before, after = lax.optimization_barrier((part, before, after))
    face_mass = collect_neighbours(part, before, after, face_link.T)
    masses, face_mass = lax.optimization_barrier((masses, face_mass))
    return (unpack(masses, slots, MASS_ROWS, MASS_ROWS, 125, "unpack_masses"), face_mass)


def solution(mesh):
    return jax.shard_map(
        body,
        mesh=mesh,
        in_specs=(P(("seg", "rank"), None),) * 4,
        out_specs=(P(None, ("seg", "rank")), P(None, ("seg", "rank"))),
        check_vma=False,
    )
```

```python
import functools
import math

import jax
import jax.numpy as jnp
import numpy as np
from jax import lax
from jax.experimental import pallas as pl
from jax.experimental.pallas import tpu as pltpu
from jax.sharding import PartitionSpec as P

F32 = jnp.float32
BF16 = jnp.bfloat16
FIRST, SECOND = (0, 1, 2), (3, 4, 5)
PARTS = 2
VMEM = 60 << 20
GROUPS = 8
FACE_ROWS = 19
FACES = GROUPS * FACE_ROWS
FACE_CHUNK = 19
MASS_ROWS = 16
MASS = GROUPS * MASS_ROWS


def shifted(array, axis, by):
    count = lax.axis_size(axis)
    pairs = [(i, i + by) for i in range(count) if 0 <= i + by < count]
    return lax.ppermute(array, axis, pairs)


def gll_tables():
    points = np.array([-1.0, -math.sqrt(3.0 / 7.0), 0.0, math.sqrt(3.0 / 7.0), 1.0])
    weights = np.array([0.1, 49.0 / 90.0, 32.0 / 45.0, 49.0 / 90.0, 0.1])
    barycentric = np.array(
        [1.0 / np.prod([points[j] - points[m] for m in range(5) if m != j]) for j in range(5)]
    )
    slopes = np.zeros((5, 5))
    for i in range(5):
        for j in range(5):
            if i != j:
                slopes[i, j] = barycentric[j] / barycentric[i] / (points[i] - points[j])
        slopes[i, i] = -np.sum(slopes[i])

    def lagrange_at(where):
        table = np.ones((5, 5))
        for a in range(5):
            for j in range(5):
                for m in range(5):
                    if m != j:
                        table[a, j] *= (where[a] - points[m]) / (points[j] - points[m])
        return table

    def blend(value, side):
        return (1.0 - value) / 2.0 if side == 0 else (1.0 + value) / 2.0

    def flat(i, j, k):
        return i * 25 + j * 5 + k

    ends = (0, 4)
    gordon = np.zeros((125, 125))
    for i in range(5):
        for j in range(5):
            for k in range(5):
                r, s, t = (points[i], points[j], points[k])
                target = flat(i, j, k)
                for a in range(2):
                    gordon[target, flat(ends[a], j, k)] += blend(r, a)
                    gordon[target, flat(i, ends[a], k)] += blend(s, a)
                    gordon[target, flat(i, j, ends[a])] += blend(t, a)
                    for b in range(2):
                        gordon[target, flat(ends[a], ends[b], k)] -= blend(r, a) * blend(s, b)
                        gordon[target, flat(ends[a], j, ends[b])] -= blend(r, a) * blend(t, b)
                        gordon[target, flat(i, ends[a], ends[b])] -= blend(s, a) * blend(t, b)
                        for c in range(2):
                            gordon[target, flat(ends[a], ends[b], ends[c])] += (
                                blend(r, a) * blend(s, b) * blend(t, c)
                            )
    children = np.zeros((8, 125, 125))
    for octant in range(8):
        shifts = [2 * (octant >> 2 & 1) - 1, 2 * (octant >> 1 & 1) - 1, 2 * (octant & 1) - 1]
        tables = [lagrange_at((points + shifts[q]) / 2.0) for q in range(3)]
        children[octant] = np.kron(np.kron(tables[0], tables[1]), tables[2]) @ gordon
    identity = np.eye(5)
    derivs = [
        np.kron(np.kron(slopes, identity), identity),
        np.kron(np.kron(identity, slopes), identity),
        np.kron(np.kron(identity, identity), slopes),
    ]
    deriv_table = np.concatenate([derivs[q].T for q in range(3)], axis=1)
    mass_weights = np.kron(np.kron(weights, weights), weights)
    face_weights = np.kron(weights, weights)
    tangents = [(1, 2), (1, 2), (0, 2), (0, 2), (0, 1), (0, 1)]
    boundary = [
        flat(i, j, k)
        for i in range(5)
        for j in range(5)
        for k in range(5)
        if i in ends or j in ends or k in ends
    ]
    children_map = children.transpose(2, 0, 1).reshape(125, 1000)
    return (children_map, deriv_table, mass_weights, face_weights, tangents, np.array(boundary))


def split(value, parts):
    pieces = []
    for _ in range(parts):
        piece = value.astype(BF16)
        pieces.append(piece)
        value = value - piece.astype(F32)
    return pieces


def flipped(blocks):
    lanes = lax.broadcasted_iota(jnp.int32, blocks[0].shape, 1) // (128 // GROUPS)
    blocks = list(blocks)
    for bit in (1, 2, 4):
        low = (lanes & bit) == 0
        step = bit * (128 // GROUPS)
        for i in range(GROUPS):
            if i & bit == 0:
                a, c = blocks[i], blocks[i | bit]
                blocks[i] = jnp.where(low, a, pltpu.roll(c, step, 1))
                blocks[i | bit] = jnp.where(low, pltpu.roll(a, 128 - step, 1), c)
    return blocks


def face_order():
    return [25 * f + p for f in range(6) for p in range(24)] + [25 * f + 24 for f in range(6)]


def constants():
    children_map, deriv_table, mass_weights, face_weights, tangents, _ = gll_tables()
    child = np.zeros((8, 128, 128))
    child[:, :125, :125] = children_map.reshape(125, 8, 125).transpose(1, 2, 0)
    derivs = deriv_table.reshape(125, 3, 125).transpose(1, 2, 0)
    grid = np.arange(125).reshape(5, 5, 5)
    face_rows = np.zeros((2 * FACES, 128))
    for face in range(6):
        nodes = np.take(grid, 0 if face % 2 == 0 else 4, axis=face // 2).reshape(-1)
        for p in range(25):
            n = 24 * face + p if p < 24 else 144 + face
            face_rows[n, :125] = face_weights[p] * derivs[tangents[face][0]][nodes[p]]
            face_rows[FACES + n, :125] = derivs[tangents[face][1]][nodes[p]]
    mass_rows = np.zeros((3 * MASS, 128))
    for d in range(3):
        weights = mass_weights[:, None] if d == 0 else 1.0
        mass_rows[d * MASS : d * MASS + 125, :125] = weights * derivs[d]
    child = child.reshape(1024, 128)
    return [jnp.asarray(np.concatenate([child, rows]), F32) for rows in (face_rows, mass_rows)]


def face_values(deriv_ref, row, marked):
    u = [deriv_ref[row : row + 8, c * marked : (c + 1) * marked] for c in range(3)]
    v = [deriv_ref[FACES + row : FACES + row + 8, c * marked : (c + 1) * marked] for c in range(3)]
    nx = u[1] * v[2] - u[2] * v[1]
    ny = u[2] * v[0] - u[0] * v[2]
    nz = u[0] * v[1] - u[1] * v[0]
    return jnp.sqrt(nx * nx + ny * ny + nz * nz)


def mass_values(deriv_ref, row, marked):
    j = [
        [deriv_ref[d * MASS + row : d * MASS + row + 8, c * marked : (c + 1) * marked] for d in range(3)]
        for c in range(3)
    ]
    return (
        j[0][0] * (j[1][1] * j[2][2] - j[1][2] * j[2][1])
        - j[0][1] * (j[1][0] * j[2][2] - j[1][2] * j[2][0])
        + j[0][2] * (j[1][0] * j[2][1] - j[1][1] * j[2][0])
    )


def child_kernel(
    values, rows, chunk, capacity, nodes_hbm, marks_hbm, owner_hbm, table_hbm, out_ref,
    nodes_ref, marks_ref, owner_ref, table_ref, sems, pick_ref, x_ref, cc_ref, dd_ref, deriv_a, deriv_b,
    vals_ref, natural_ref, target_ref, *buffers,
):
    elements = nodes_ref.shape[1]
    marked = marks_ref.shape[1]
    kids = 8 * marked
    height = GROUPS * rows
    onehots, ys = buffers[: len(buffers) // 2], buffers[len(buffers) // 2 :]
    columns = onehots[0].shape[1]
    destinations = columns // capacity
    devices = out_ref.shape[0] // chunk * pl.num_programs(0)

    @pl.when(pl.program_id(0) == 0)
    def _():
        copies = [
            pltpu.make_async_copy(source, kept, sems.at[i])
            for i, (source, kept) in enumerate(
                ((owner_hbm, owner_ref), (marks_hbm, marks_ref), (table_hbm, table_ref))
            )
        ]
        chunks = [
            pltpu.make_async_copy(
                nodes_hbm.at[:, pl.ds(at, 512)], nodes_ref.at[:, pl.ds(at, 512)], sems.at[3 + at // 512]
            )
            for at in range(0, elements, 512)
        ]
        for copy in copies[:2] + chunks + copies[2:]:
            copy.start()

        owner_rows = lax.broadcasted_iota(jnp.int32, (devices, 128), 0)
        earlier = lax.broadcasted_iota(jnp.int32, (128, 128), 0) < lax.broadcasted_iota(jnp.int32, (128, 128), 1)
        earlier = jnp.where(earlier, 1.0, 0.0).astype(BF16)
        ones = jnp.ones((128, 128), BF16)
        copies[0].wait()
        seen = jnp.zeros((devices, 128), F32)
        for b in range(kids // 128):
            owner = owner_ref[b : b + 1, :]
            same = owner_rows == owner
            same_b = jnp.where(same, 1.0, 0.0).astype(BF16)
            before = jnp.dot(same_b, earlier, preferred_element_type=F32) + seen
            position = jnp.sum(jnp.where(same, before, 0.0), axis=0, keepdims=True)
            target = owner.astype(F32) * capacity + position
            natural_ref[128 * b : 128 * b + 128, :] = jnp.broadcast_to(target, (128, 128)).T.astype(jnp.int32)
            seen = seen + jnp.dot(same_b, ones, preferred_element_type=F32)
        for o in range(8):
            target_ref[o * marked : (o + 1) * marked, :] = natural_ref[pl.ds(o, marked, stride=8), :]

        pick_ref[...] = jnp.zeros_like(pick_ref)
        copies[1].wait()
        marks = marks_ref[...]

        def pick(k, carry):
            start = pl.multiple_of(k * 256, 256)
            where = lax.broadcasted_iota(jnp.int32, (256, marked), 0) + start
            chosen = jnp.where(where == marks, 1.0, 0.0).astype(BF16)
            for piece in split(nodes_ref[:, pl.ds(start, 256)], 3):
                pick_ref[0:375, :] += jnp.dot(piece, chosen, preferred_element_type=F32)
            return carry

        for k, copy in enumerate(chunks):
            copy.wait()
            lax.fori_loop(2 * k, 2 * k + 2, pick, 0)
        copies[2].wait()
        for c in range(3):
            x = pick_ref[125 * c : 125 * c + 128, :]
            x = x - 0.5 * (x[0:1] + x[124:125])
            a1, a2, a3 = split(x, 3)
            for k, piece in enumerate((a1, a2, a1, a3, a2, a1)):
                x_ref[128 * k : 128 * k + 128, c * marked : (c + 1) * marked] = piece
        c1, c2, c3 = split(table_ref[0:1024, :], 3)
        for k, piece in enumerate((c1, c1, c2, c1, c2, c3)):
            cc_ref[:, 128 * k : 128 * k + 128] = piece
        d1, d2 = split(table_ref[1024:, :], 2)
        for k, piece in enumerate((d1, d1, d2, d2)):
            dd_ref[:, 128 * k : 128 * k + 128] = piece

        def octants(i, carry):
            for e, deriv_ref in enumerate((deriv_a, deriv_b)):
                o = 2 * i + e
                coords = jnp.dot(
                    cc_ref[pl.ds(pl.multiple_of(o * 128, 128), 128), :], x_ref[...], preferred_element_type=F32
                )
                y1, y2 = split(coords - coords[62:63], 2)
                deriv_ref[...] = jnp.dot(
                    dd_ref[...], jnp.concatenate([y1, y2, y1, y2], axis=0), preferred_element_type=F32
                )
                lanes = pl.ds(pl.multiple_of(o * marked, 128), marked)
                for row in range(0, height, 8):
                    v1, v2 = split(values(deriv_ref, row, marked), 2)
                    vals_ref[row : row + 8, lanes] = v1
                    vals_ref[height + row : height + row + 8, lanes] = v2
            return carry

        lax.fori_loop(0, 4, octants, 0)

    numbers = lax.broadcasted_iota(jnp.int32, (128, 128), 1)

    base = pl.program_id(0) * (out_ref.shape[0] // chunk * capacity)
    parts = list(enumerate(zip(onehots, ys)))
    for i, (onehot_ref, y_ref) in parts:
        for at in range(0, kids, 128):
            target = target_ref[at : at + 128, :] - (base + i * columns)
            for tile in range(columns // 128):
                onehot_ref[at : at + 128, 128 * tile : 128 * tile + 128] = jnp.where(
                    target == numbers + 128 * tile, 1.0, 0.0
                ).astype(BF16)
        moved = jnp.dot(vals_ref[...], onehot_ref[...], preferred_element_type=F32)
        y_ref[...] = moved[0:height] + moved[height:]
    for i, (_, y_ref) in parts:
        for tile in range(columns // 128):
            lanes = slice(128 * tile, 128 * tile + 128)
            blocks = flipped([y_ref[rows * g : rows * (g + 1), lanes] for g in range(GROUPS)])
            if chunk > rows:
                blocks = [jnp.concatenate([b, jnp.zeros((chunk - rows, 128), F32)], axis=0) for b in blocks]
            start = (i * destinations + tile * GROUPS) * chunk
            out_ref[start : start + GROUPS * chunk, :] = jnp.concatenate(blocks, axis=0)


def whole(a):
    return pl.BlockSpec(a.shape, lambda i: (0, 0))


def outgoing(values, rows, chunk, table, nodes, marks, owner, devices, capacity, name):
    marked = marks.shape[1]
    kids = 8 * marked
    operands = (nodes, marks, owner, table)
    steps = 4
    height = GROUPS * rows
    return pl.pallas_call(
        functools.partial(child_kernel, values, rows, chunk, capacity),
        out_shape=jax.ShapeDtypeStruct((devices * chunk, 128), F32),
        grid=(steps,),
        in_specs=[pl.BlockSpec(memory_space=pltpu.HBM)] * 4,
        out_specs=pl.BlockSpec((devices * chunk // steps, 128), lambda i: (i, 0)),
        scratch_shapes=[
            *(pltpu.VMEM(a.shape, a.dtype) for a in operands),
            pltpu.SemaphoreType.DMA((3 + nodes.shape[1] // 512,)),
            pltpu.VMEM((384, marked), F32),
            pltpu.VMEM((768, 3 * marked), BF16),
            pltpu.VMEM((1024, 768), BF16),
            pltpu.VMEM((table.shape[0] - 1024, 512), BF16),
            pltpu.VMEM((table.shape[0] - 1024, 3 * marked), F32),
            pltpu.VMEM((table.shape[0] - 1024, 3 * marked), F32),
            pltpu.VMEM((2 * height, kids), BF16),
            pltpu.VMEM((kids, 128), jnp.int32),
            pltpu.VMEM((kids, 128), jnp.int32),
            *(pltpu.VMEM((kids, 1024 // PARTS), BF16) for _ in range(PARTS)),
            *(pltpu.VMEM((height, 1024 // PARTS), F32) for _ in range(PARTS)),
        ],
        compiler_params=pltpu.CompilerParams(vmem_limit_bytes=VMEM),
        name=name,
    )(*operands)


def make_outgoing(nodes, marks, owner, devices, capacity):
    face_table, mass_table = constants()
    args = (nodes, marks, owner, devices, capacity)
    return (
        outgoing(face_values, FACE_ROWS, FACE_CHUNK, face_table, *args, "faces"),
        outgoing(mass_values, MASS_ROWS, MASS_ROWS, mass_table, *args, "masses"),
    )


def unpack_tile(rows, chunk, height, in_ref, out_ref, tile):
    start = pl.multiple_of(tile * (chunk * GROUPS), 8)
    lanes = pl.ds(pl.multiple_of(tile * 128, 128), 128)
    arrived = in_ref[pl.ds(start, chunk * GROUPS), :]
    blocks = flipped([arrived[chunk * j : chunk * j + rows] for j in range(GROUPS)])
    for g in range(GROUPS):
        count = min(rows, height - rows * g)
        out_ref[rows * g : rows * g + count, lanes] = blocks[g][0:count]


def unpack_kernel(rows, chunk, height, in_ref, out_ref):
    def tiles(i, carry):
        for k in range(4):
            unpack_tile(rows, chunk, height, in_ref, out_ref, 4 * i + k)
        return carry

    lax.fori_loop(0, out_ref.shape[1] // 512, tiles, 0)


def unpack(arrived, slots, rows, chunk, height, name):
    return pl.pallas_call(
        functools.partial(unpack_kernel, rows, chunk, height),
        out_shape=jax.ShapeDtypeStruct((height, slots), F32),
        grid=(slots // 1024,),
        in_specs=[pl.BlockSpec((8 * GROUPS * chunk, 128), lambda i: (i, 0))],
        out_specs=pl.BlockSpec((height, 1024), lambda i: (0, i)),
        compiler_params=pltpu.CompilerParams(vmem_limit_bytes=VMEM),
        name=name,
    )(arrived)


def fill_face_table(table_ref, tail_ref, sources, faces):
    per_source = sources[0].shape[1] // 256
    tiles = len(sources) * per_source
    body_rows = 24 * tiles
    for f in faces:
        at = f if table_ref.shape[0] == 6 else faces.index(f)
        other = f + 1 - 2 * (f % 2)
        for k, source in enumerate(sources):

            def pair(i, carry):
                lanes = [pl.ds(pl.multiple_of(512 * i + 256 * e, 256), 256) for e in range(2)]
                values = jnp.concatenate([source[24 * other : 24 * other + 24, l] for l in lanes], axis=0)
                row = pl.multiple_of(24 * per_source * k + 48 * i, 16)
                for part, piece in enumerate(split(values, 2)):
                    table_ref[at, pl.ds(row, 48), 256 * part : 256 * part + 256] = piece
                for e in range(2):
                    tail_ref[pl.ds(per_source * k + 2 * i + e, 1), :] = source[144 + other : 145 + other, lanes[e]]
                return carry

            lax.fori_loop(0, per_source // 2, pair, 0)
        for part, piece in enumerate(split(tail_ref[0:tiles, :], 2)):
            table_ref[at, body_rows : body_rows + tiles, 256 * part : 256 * part + 256] = piece


def look_up(table_ref, at, tiles, low, high):
    chosen = jnp.where(lax.broadcasted_iota(jnp.int32, (256, 256), 0) == low, 1.0, 0.0).astype(BF16)
    found = jnp.dot(table_ref[at, 0 : 25 * tiles], jnp.concatenate([chosen, chosen], axis=0), preferred_element_type=F32)
    high24 = jnp.broadcast_to(high, (24, 256))
    picked = jnp.zeros((24, 256), F32)
    for h in range(tiles):
        picked = jnp.where(high24 == h, found[24 * h : 24 * h + 24], picked)
    last = jnp.where(lax.broadcasted_iota(jnp.int32, (tiles, 256), 0) == high, found[24 * tiles :], 0.0)
    return picked, jnp.sum(last, axis=0, keepdims=True)


def own_kernel(faces, link_ref, faces_ref, out_ref, table_ref, tail_ref):
    per_source = faces_ref.shape[1] // 256

    @pl.when(pl.program_id(0) == 0)
    def _():
        fill_face_table(table_ref, tail_ref, (faces_ref,), faces)

    here = pl.ds(pl.multiple_of(pl.program_id(0) * 256, 256), 256)
    for at, f in enumerate(faces):
        link = link_ref[f : f + 1, here]
        picked, last = look_up(table_ref, at, per_source, link & 255, (link >> 8) - per_source)
        out_ref[25 * at : 25 * at + 24, :] = faces_ref[24 * f : 24 * f + 24, here] + picked
        out_ref[25 * at + 24 : 25 * at + 25, :] = faces_ref[144 + f : 145 + f, here] + last


def neighbour_kernel(link_ref, before_ref, after_ref, faces_ref, first_ref, out_ref, table_ref, tail_ref, unpacked_before, unpacked_after):
    per_source = unpacked_before.shape[1] // 256

    @pl.when(pl.program_id(0) == 0)
    def _():
        def tile(i, carry):
            for packed, unpacked in ((before_ref, unpacked_before), (after_ref, unpacked_after)):
                unpack_tile(FACE_ROWS, FACE_CHUNK, 150, packed, unpacked, i)
            return carry

        lax.fori_loop(0, unpacked_before.shape[1] // 128, tile, 0)
        fill_face_table(table_ref, tail_ref, (unpacked_before, unpacked_after), FIRST)
        fill_face_table(table_ref, tail_ref, (unpacked_before, faces_ref, unpacked_after), SECOND)

    here = pl.ds(pl.multiple_of(pl.program_id(0) * 256, 256), 256)
    for f in range(6):
        link = link_ref[f : f + 1, here]
        high = link >> 8
        if f in FIRST:
            high = jnp.where(high < per_source, high, jnp.where(high < 2 * per_source, -1, high - per_source))
            picked, last = look_up(table_ref, f, 2 * per_source, link & 255, high)
            row = 25 * FIRST.index(f)
            added, added_last = first_ref[row : row + 24, :], first_ref[row + 24 : row + 25, :]
        else:
            picked, last = look_up(table_ref, f, 3 * per_source, link & 255, high)
            added, added_last = faces_ref[24 * f : 24 * f + 24, here], faces_ref[144 + f : 145 + f, here]
        out_ref[25 * f : 25 * f + 24, :] = added + picked
        out_ref[25 * f + 24 : 25 * f + 25, :] = added_last + last


def collect_own(faces, links, chosen, name):
    slots = faces.shape[1]
    tiles = slots // 256
    height = 25 * len(chosen)
    return pl.pallas_call(
        functools.partial(own_kernel, chosen),
        out_shape=jax.ShapeDtypeStruct((height, slots), F32),
        grid=(tiles,),
        in_specs=[whole(links), whole(faces)],
        out_specs=pl.BlockSpec((height, 256), lambda i: (0, i)),
        scratch_shapes=[pltpu.VMEM((len(chosen), 25 * tiles, 512), BF16), pltpu.VMEM((tiles, 256), F32)],
        compiler_params=pltpu.CompilerParams(vmem_limit_bytes=VMEM),
        cost_estimate=pl.CostEstimate(flops=0, bytes_accessed=1024, transcendentals=0),
        name=name,
    )(links, faces)


def collect_neighbours(first, faces, before, after, links):
    slots = first.shape[1]
    tiles = 3 * slots // 256
    block = pl.BlockSpec((first.shape[0], 256), lambda i: (0, i))
    return pl.pallas_call(
        neighbour_kernel,
        out_shape=jax.ShapeDtypeStruct((150, slots), F32),
        grid=(slots // 256,),
        in_specs=[whole(links), whole(before), whole(after), whole(faces), block],
        out_specs=pl.BlockSpec((150, 256), lambda i: (0, i)),
        scratch_shapes=[
            pltpu.VMEM((6, 25 * tiles, 512), BF16),
            pltpu.VMEM((tiles, 256), F32),
            pltpu.VMEM((150, slots), F32),
            pltpu.VMEM((150, slots), F32),
        ],
        compiler_params=pltpu.CompilerParams(vmem_limit_bytes=VMEM),
        cost_estimate=pl.CostEstimate(flops=10**12, bytes_accessed=10**9, transcendentals=0),
        name="collect_neighbours",
    )(links, before, after, faces, first)


def exchanged(rows, devices, tile):
    blocks = rows.reshape(devices, rows.shape[0] // devices // tile, tile, 128)
    return lax.all_to_all(blocks, ("seg", "rank"), split_axis=0, concat_axis=0, tiled=True).reshape(rows.shape)


def body(parent_nodes, marks, child_owner, face_link):
    devices = lax.axis_size("seg") * lax.axis_size("rank")
    kids = child_owner.shape[0]
    capacity = max(2, 2 * kids // devices)
    slots = devices * capacity
    faces, masses = make_outgoing(parent_nodes.T, marks, child_owner.reshape(kids // 128, 128), devices, capacity)
    arrived = exchanged(faces, devices, 1)
    arrived, masses = lax.optimization_barrier((arrived, masses))
    before = shifted(arrived, "rank", 1)
    after = shifted(arrived, "rank", -1)
    faces = unpack(arrived, slots, FACE_ROWS, FACE_CHUNK, 150, "unpack_faces")
    links = face_link.T
    first = collect_own(faces, links, FIRST, "collect_first")
    masses, first = lax.optimization_barrier((masses, first))
    masses = exchanged(masses, devices, 8)
    first, before, after = lax.optimization_barrier((first, before, after))
    face_mass = collect_neighbours(first, faces, before, after, links)
    masses, face_mass = lax.optimization_barrier((masses, face_mass))
    return (unpack(masses, slots, MASS_ROWS, MASS_ROWS, 125, "unpack_masses"), face_mass)


def solution(mesh):
    return jax.shard_map(
        body,
        mesh=mesh,
        in_specs=(P(("seg", "rank"), None),) * 4,
        out_specs=(P(None, ("seg", "rank")), P(None, ("seg", "rank"))),
        check_vma=False,
    )
```

```python
import functools
import math

import jax
import jax.numpy as jnp
import numpy as np
from jax import lax
from jax.experimental import pallas as pl
from jax.experimental.pallas import tpu as pltpu
from jax.sharding import PartitionSpec as P

F32 = jnp.float32
BF16 = jnp.bfloat16
FIRST, SECOND = (0, 1), (2, 3, 4, 5)
PARTS = 2
VMEM = 60 << 20
GROUPS = 8
FACE_ROWS = 19
FACES = GROUPS * FACE_ROWS
FACE_CHUNK = 19
MASS_ROWS = 16
MASS = GROUPS * MASS_ROWS


def shifted(array, axis, by):
    count = lax.axis_size(axis)
    pairs = [(i, i + by) for i in range(count) if 0 <= i + by < count]
    return lax.ppermute(array, axis, pairs)


def gll_tables():
    points = np.array([-1.0, -math.sqrt(3.0 / 7.0), 0.0, math.sqrt(3.0 / 7.0), 1.0])
    weights = np.array([0.1, 49.0 / 90.0, 32.0 / 45.0, 49.0 / 90.0, 0.1])
    barycentric = np.array(
        [1.0 / np.prod([points[j] - points[m] for m in range(5) if m != j]) for j in range(5)]
    )
    slopes = np.zeros((5, 5))
    for i in range(5):
        for j in range(5):
            if i != j:
                slopes[i, j] = barycentric[j] / barycentric[i] / (points[i] - points[j])
        slopes[i, i] = -np.sum(slopes[i])

    def lagrange_at(where):
        table = np.ones((5, 5))
        for a in range(5):
            for j in range(5):
                for m in range(5):
                    if m != j:
                        table[a, j] *= (where[a] - points[m]) / (points[j] - points[m])
        return table

    def blend(value, side):
        return (1.0 - value) / 2.0 if side == 0 else (1.0 + value) / 2.0

    def flat(i, j, k):
        return i * 25 + j * 5 + k

    ends = (0, 4)
    gordon = np.zeros((125, 125))
    for i in range(5):
        for j in range(5):
            for k in range(5):
                r, s, t = (points[i], points[j], points[k])
                target = flat(i, j, k)
                for a in range(2):
                    gordon[target, flat(ends[a], j, k)] += blend(r, a)
                    gordon[target, flat(i, ends[a], k)] += blend(s, a)
                    gordon[target, flat(i, j, ends[a])] += blend(t, a)
                    for b in range(2):
                        gordon[target, flat(ends[a], ends[b], k)] -= blend(r, a) * blend(s, b)
                        gordon[target, flat(ends[a], j, ends[b])] -= blend(r, a) * blend(t, b)
                        gordon[target, flat(i, ends[a], ends[b])] -= blend(s, a) * blend(t, b)
                        for c in range(2):
                            gordon[target, flat(ends[a], ends[b], ends[c])] += (
                                blend(r, a) * blend(s, b) * blend(t, c)
                            )
    children = np.zeros((8, 125, 125))
    for octant in range(8):
        shifts = [2 * (octant >> 2 & 1) - 1, 2 * (octant >> 1 & 1) - 1, 2 * (octant & 1) - 1]
        tables = [lagrange_at((points + shifts[q]) / 2.0) for q in range(3)]
        children[octant] = np.kron(np.kron(tables[0], tables[1]), tables[2]) @ gordon
    identity = np.eye(5)
    derivs = [
        np.kron(np.kron(slopes, identity), identity),
        np.kron(np.kron(identity, slopes), identity),
        np.kron(np.kron(identity, identity), slopes),
    ]
    deriv_table = np.concatenate([derivs[q].T for q in range(3)], axis=1)
    mass_weights = np.kron(np.kron(weights, weights), weights)
    face_weights = np.kron(weights, weights)
    tangents = [(1, 2), (1, 2), (0, 2), (0, 2), (0, 1), (0, 1)]
    boundary = [
        flat(i, j, k)
        for i in range(5)
        for j in range(5)
        for k in range(5)
        if i in ends or j in ends or k in ends
    ]
    children_map = children.transpose(2, 0, 1).reshape(125, 1000)
    return (children_map, deriv_table, mass_weights, face_weights, tangents, np.array(boundary))


def split(value, parts):
    pieces = []
    for _ in range(parts):
        piece = value.astype(BF16)
        pieces.append(piece)
        value = value - piece.astype(F32)
    return pieces


def flipped(blocks):
    lanes = lax.broadcasted_iota(jnp.int32, blocks[0].shape, 1) // (128 // GROUPS)
    blocks = list(blocks)
    for bit in (1, 2, 4):
        low = (lanes & bit) == 0
        step = bit * (128 // GROUPS)
        for i in range(GROUPS):
            if i & bit == 0:
                a, c = blocks[i], blocks[i | bit]
                blocks[i] = jnp.where(low, a, pltpu.roll(c, step, 1))
                blocks[i | bit] = jnp.where(low, pltpu.roll(a, 128 - step, 1), c)
    return blocks


def face_order():
    return [25 * f + p for f in range(6) for p in range(24)] + [25 * f + 24 for f in range(6)]


def constants():
    children_map, deriv_table, mass_weights, face_weights, tangents, _ = gll_tables()
    child = np.zeros((8, 128, 128))
    child[:, :125, :125] = children_map.reshape(125, 8, 125).transpose(1, 2, 0)
    derivs = deriv_table.reshape(125, 3, 125).transpose(1, 2, 0)
    grid = np.arange(125).reshape(5, 5, 5)
    face_rows = np.zeros((2 * FACES, 128))
    for face in range(6):
        nodes = np.take(grid, 0 if face % 2 == 0 else 4, axis=face // 2).reshape(-1)
        for p in range(25):
            n = 24 * face + p if p < 24 else 144 + face
            face_rows[n, :125] = face_weights[p] * derivs[tangents[face][0]][nodes[p]]
            face_rows[FACES + n, :125] = derivs[tangents[face][1]][nodes[p]]
    mass_rows = np.zeros((3 * MASS, 128))
    for d in range(3):
        weights = mass_weights[:, None] if d == 0 else 1.0
        mass_rows[d * MASS : d * MASS + 125, :125] = weights * derivs[d]
    child = child.reshape(1024, 128)
    return [jnp.asarray(np.concatenate([child, rows]), F32) for rows in (face_rows, mass_rows)]


def face_values(deriv_ref, row, marked):
    u = [deriv_ref[row : row + 8, c * marked : (c + 1) * marked] for c in range(3)]
    v = [deriv_ref[FACES + row : FACES + row + 8, c * marked : (c + 1) * marked] for c in range(3)]
    nx = u[1] * v[2] - u[2] * v[1]
    ny = u[2] * v[0] - u[0] * v[2]
    nz = u[0] * v[1] - u[1] * v[0]
    return jnp.sqrt(nx * nx + ny * ny + nz * nz)


def mass_values(deriv_ref, row, marked):
    j = [
        [deriv_ref[d * MASS + row : d * MASS + row + 8, c * marked : (c + 1) * marked] for d in range(3)]
        for c in range(3)
    ]
    return (
        j[0][0] * (j[1][1] * j[2][2] - j[1][2] * j[2][1])
        - j[0][1] * (j[1][0] * j[2][2] - j[1][2] * j[2][0])
        + j[0][2] * (j[1][0] * j[2][1] - j[1][1] * j[2][0])
    )


def child_kernel(
    values, rows, chunk, capacity, nodes_hbm, marks_hbm, owner_hbm, table_hbm, out_ref,
    nodes_ref, marks_ref, owner_ref, table_ref, sems, pick_ref, x_ref, cc_ref, dd_ref, deriv_a, deriv_b,
    vals_ref, natural_ref, target_ref, *buffers,
):
    elements = nodes_ref.shape[1]
    marked = marks_ref.shape[1]
    kids = 8 * marked
    height = GROUPS * rows
    onehots, ys = buffers[: len(buffers) // 2], buffers[len(buffers) // 2 :]
    columns = onehots[0].shape[1]
    destinations = columns // capacity
    devices = out_ref.shape[0] // chunk * pl.num_programs(0)

    @pl.when(pl.program_id(0) == 0)
    def _():
        copies = [
            pltpu.make_async_copy(source, kept, sems.at[i])
            for i, (source, kept) in enumerate(
                ((owner_hbm, owner_ref), (marks_hbm, marks_ref), (table_hbm, table_ref))
            )
        ]
        chunks = [
            pltpu.make_async_copy(
                nodes_hbm.at[:, pl.ds(at, 512)], nodes_ref.at[:, pl.ds(at, 512)], sems.at[3 + at // 512]
            )
            for at in range(0, elements, 512)
        ]
        for copy in copies[:2] + chunks + copies[2:]:
            copy.start()

        owner_rows = lax.broadcasted_iota(jnp.int32, (devices, 128), 0)
        earlier = lax.broadcasted_iota(jnp.int32, (128, 128), 0) < lax.broadcasted_iota(jnp.int32, (128, 128), 1)
        earlier = jnp.where(earlier, 1.0, 0.0).astype(BF16)
        ones = jnp.ones((128, 128), BF16)
        copies[0].wait()
        seen = jnp.zeros((devices, 128), F32)
        for b in range(kids // 128):
            owner = owner_ref[b : b + 1, :]
            same = owner_rows == owner
            same_b = jnp.where(same, 1.0, 0.0).astype(BF16)
            before = jnp.dot(same_b, earlier, preferred_element_type=F32) + seen
            position = jnp.sum(jnp.where(same, before, 0.0), axis=0, keepdims=True)
            target = owner.astype(F32) * capacity + position
            natural_ref[128 * b : 128 * b + 128, :] = jnp.broadcast_to(target, (128, 128)).T.astype(jnp.int32)
            seen = seen + jnp.dot(same_b, ones, preferred_element_type=F32)
        for o in range(8):
            target_ref[o * marked : (o + 1) * marked, :] = natural_ref[pl.ds(o, marked, stride=8), :]

        pick_ref[...] = jnp.zeros_like(pick_ref)
        copies[1].wait()
        marks = marks_ref[...]

        def pick(k, carry):
            start = pl.multiple_of(k * 256, 256)
            where = lax.broadcasted_iota(jnp.int32, (256, marked), 0) + start
            chosen = jnp.where(where == marks, 1.0, 0.0).astype(BF16)
            for piece in split(nodes_ref[:, pl.ds(start, 256)], 3):
                pick_ref[0:375, :] += jnp.dot(piece, chosen, preferred_element_type=F32)
            return carry

        for k, copy in enumerate(chunks):
            copy.wait()
            lax.fori_loop(2 * k, 2 * k + 2, pick, 0)
        copies[2].wait()
        for c in range(3):
            x = pick_ref[125 * c : 125 * c + 128, :]
            x = x - 0.5 * (x[0:1] + x[124:125])
            a1, a2, a3 = split(x, 3)
            for k, piece in enumerate((a1, a2, a1, a3, a2, a1)):
                x_ref[128 * k : 128 * k + 128, c * marked : (c + 1) * marked] = piece
        c1, c2, c3 = split(table_ref[0:1024, :], 3)
        for k, piece in enumerate((c1, c1, c2, c1, c2, c3)):
            cc_ref[:, 128 * k : 128 * k + 128] = piece
        d1, d2 = split(table_ref[1024:, :], 2)
        for k, piece in enumerate((d1, d1, d2, d2)):
            dd_ref[:, 128 * k : 128 * k + 128] = piece

        def octants(i, carry):
            for e, deriv_ref in enumerate((deriv_a, deriv_b)):
                o = 2 * i + e
                coords = jnp.dot(
                    cc_ref[pl.ds(pl.multiple_of(o * 128, 128), 128), :], x_ref[...], preferred_element_type=F32
                )
                y1, y2 = split(coords - coords[62:63], 2)
                deriv_ref[...] = jnp.dot(
                    dd_ref[...], jnp.concatenate([y1, y2, y1, y2], axis=0), preferred_element_type=F32
                )
                lanes = pl.ds(pl.multiple_of(o * marked, 128), marked)
                for row in range(0, height, 8):
                    v1, v2 = split(values(deriv_ref, row, marked), 2)
                    vals_ref[row : row + 8, lanes] = v1
                    vals_ref[height + row : height + row + 8, lanes] = v2
            return carry

        lax.fori_loop(0, 4, octants, 0)

    numbers = lax.broadcasted_iota(jnp.int32, (128, 128), 1)

    base = pl.program_id(0) * (out_ref.shape[0] // chunk * capacity)
    parts = list(enumerate(zip(onehots, ys)))
    for i, (onehot_ref, y_ref) in parts:
        for at in range(0, kids, 128):
            target = target_ref[at : at + 128, :] - (base + i * columns)
            for tile in range(columns // 128):
                onehot_ref[at : at + 128, 128 * tile : 128 * tile + 128] = jnp.where(
                    target == numbers + 128 * tile, 1.0, 0.0
                ).astype(BF16)
        moved = jnp.dot(vals_ref[...], onehot_ref[...], preferred_element_type=F32)
        y_ref[...] = moved[0:height] + moved[height:]
    for i, (_, y_ref) in parts:
        for tile in range(columns // 128):
            lanes = slice(128 * tile, 128 * tile + 128)
            blocks = flipped([y_ref[rows * g : rows * (g + 1), lanes] for g in range(GROUPS)])
            if chunk > rows:
                blocks = [jnp.concatenate([b, jnp.zeros((chunk - rows, 128), F32)], axis=0) for b in blocks]
            start = (i * destinations + tile * GROUPS) * chunk
            out_ref[start : start + GROUPS * chunk, :] = jnp.concatenate(blocks, axis=0)


def whole(a):
    return pl.BlockSpec(a.shape, lambda i: (0, 0))


def outgoing(values, rows, chunk, table, nodes, marks, owner, devices, capacity, name):
    marked = marks.shape[1]
    kids = 8 * marked
    operands = (nodes, marks, owner, table)
    steps = 4
    height = GROUPS * rows
    return pl.pallas_call(
        functools.partial(child_kernel, values, rows, chunk, capacity),
        out_shape=jax.ShapeDtypeStruct((devices * chunk, 128), F32),
        grid=(steps,),
        in_specs=[pl.BlockSpec(memory_space=pltpu.HBM)] * 4,
        out_specs=pl.BlockSpec((devices * chunk // steps, 128), lambda i: (i, 0)),
        scratch_shapes=[
            *(pltpu.VMEM(a.shape, a.dtype) for a in operands),
            pltpu.SemaphoreType.DMA((3 + nodes.shape[1] // 512,)),
            pltpu.VMEM((384, marked), F32),
            pltpu.VMEM((768, 3 * marked), BF16),
            pltpu.VMEM((1024, 768), BF16),
            pltpu.VMEM((table.shape[0] - 1024, 512), BF16),
            pltpu.VMEM((table.shape[0] - 1024, 3 * marked), F32),
            pltpu.VMEM((table.shape[0] - 1024, 3 * marked), F32),
            pltpu.VMEM((2 * height, kids), BF16),
            pltpu.VMEM((kids, 128), jnp.int32),
            pltpu.VMEM((kids, 128), jnp.int32),
            *(pltpu.VMEM((kids, 1024 // PARTS), BF16) for _ in range(PARTS)),
            *(pltpu.VMEM((height, 1024 // PARTS), F32) for _ in range(PARTS)),
        ],
        compiler_params=pltpu.CompilerParams(vmem_limit_bytes=VMEM),
        name=name,
    )(*operands)


def make_outgoing(nodes, marks, owner, devices, capacity):
    face_table, mass_table = constants()
    args = (nodes, marks, owner, devices, capacity)
    return (
        outgoing(face_values, FACE_ROWS, FACE_CHUNK, face_table, *args, "faces"),
        outgoing(mass_values, MASS_ROWS, MASS_ROWS, mass_table, *args, "masses"),
    )


def unpack_tile(rows, chunk, height, in_ref, out_ref, tile):
    start = pl.multiple_of(tile * (chunk * GROUPS), 8)
    lanes = pl.ds(pl.multiple_of(tile * 128, 128), 128)
    arrived = in_ref[pl.ds(start, chunk * GROUPS), :]
    blocks = flipped([arrived[chunk * j : chunk * j + rows] for j in range(GROUPS)])
    for g in range(GROUPS):
        count = min(rows, height - rows * g)
        out_ref[rows * g : rows * g + count, lanes] = blocks[g][0:count]


def unpack_kernel(rows, chunk, height, in_ref, out_ref):
    def tiles(i, carry):
        for k in range(4):
            unpack_tile(rows, chunk, height, in_ref, out_ref, 4 * i + k)
        return carry

    lax.fori_loop(0, out_ref.shape[1] // 512, tiles, 0)


def unpack(arrived, slots, rows, chunk, height, name):
    return pl.pallas_call(
        functools.partial(unpack_kernel, rows, chunk, height),
        out_shape=jax.ShapeDtypeStruct((height, slots), F32),
        grid=(slots // 1024,),
        in_specs=[pl.BlockSpec((8 * GROUPS * chunk, 128), lambda i: (i, 0))],
        out_specs=pl.BlockSpec((height, 1024), lambda i: (0, i)),
        compiler_params=pltpu.CompilerParams(vmem_limit_bytes=VMEM),
        name=name,
    )(arrived)


def fill_face_table(table_ref, tail_ref, sources, faces):
    per_source = sources[0].shape[1] // 256
    tiles = len(sources) * per_source
    body_rows = 24 * tiles
    for f in faces:
        at = f if table_ref.shape[0] == 6 else faces.index(f)
        other = f + 1 - 2 * (f % 2)
        for k, source in enumerate(sources):

            def pair(i, carry):
                lanes = [pl.ds(pl.multiple_of(512 * i + 256 * e, 256), 256) for e in range(2)]
                values = jnp.concatenate([source[24 * other : 24 * other + 24, l] for l in lanes], axis=0)
                row = pl.multiple_of(24 * per_source * k + 48 * i, 16)
                for part, piece in enumerate(split(values, 2)):
                    table_ref[at, pl.ds(row, 48), 256 * part : 256 * part + 256] = piece
                for e in range(2):
                    tail_ref[pl.ds(per_source * k + 2 * i + e, 1), :] = source[144 + other : 145 + other, lanes[e]]
                return carry

            lax.fori_loop(0, per_source // 2, pair, 0)
        for part, piece in enumerate(split(tail_ref[0:tiles, :], 2)):
            table_ref[at, body_rows : body_rows + tiles, 256 * part : 256 * part + 256] = piece


def look_up(table_ref, at, tiles, low, high):
    chosen = jnp.where(lax.broadcasted_iota(jnp.int32, (256, 256), 0) == low, 1.0, 0.0).astype(BF16)
    found = jnp.dot(table_ref[at, 0 : 25 * tiles], jnp.concatenate([chosen, chosen], axis=0), preferred_element_type=F32)
    high24 = jnp.broadcast_to(high, (24, 256))
    picked = jnp.zeros((24, 256), F32)
    for h in range(tiles):
        picked = jnp.where(high24 == h, found[24 * h : 24 * h + 24], picked)
    last = jnp.where(lax.broadcasted_iota(jnp.int32, (tiles, 256), 0) == high, found[24 * tiles :], 0.0)
    return picked, jnp.sum(last, axis=0, keepdims=True)


def own_kernel(faces, link_ref, faces_ref, out_ref, table_ref, tail_ref):
    per_source = faces_ref.shape[1] // 256

    @pl.when(pl.program_id(0) == 0)
    def _():
        fill_face_table(table_ref, tail_ref, (faces_ref,), faces)

    def columns(k, carry):
        here = pl.ds(pl.multiple_of(pl.program_id(0) * 1024 + 256 * k, 256), 256)
        lanes = pl.ds(pl.multiple_of(256 * k, 256), 256)
        for at, f in enumerate(faces):
            link = link_ref[f : f + 1, here]
            picked, last = look_up(table_ref, at, per_source, link & 255, (link >> 8) - per_source)
            out_ref[25 * at : 25 * at + 24, lanes] = faces_ref[24 * f : 24 * f + 24, here] + picked
            out_ref[25 * at + 24 : 25 * at + 25, lanes] = faces_ref[144 + f : 145 + f, here] + last
        return carry

    lax.fori_loop(0, out_ref.shape[1] // 256, columns, 0)


def neighbour_kernel(link_ref, before_ref, after_ref, faces_ref, first_ref, out_ref, table_ref, tail_ref, unpacked_before, unpacked_after):
    per_source = unpacked_before.shape[1] // 256

    @pl.when(pl.program_id(0) == 0)
    def _():
        def tile(i, carry):
            for k in range(2):
                for packed, unpacked in ((before_ref, unpacked_before), (after_ref, unpacked_after)):
                    unpack_tile(FACE_ROWS, FACE_CHUNK, 150, packed, unpacked, 2 * i + k)
            return carry

        lax.fori_loop(0, unpacked_before.shape[1] // 256, tile, 0)
        fill_face_table(table_ref, tail_ref, (unpacked_before, unpacked_after), FIRST)
        fill_face_table(table_ref, tail_ref, (unpacked_before, faces_ref, unpacked_after), SECOND)

    def columns(k, carry):
        here = pl.ds(pl.multiple_of(pl.program_id(0) * 1024 + 256 * k, 256), 256)
        lanes = pl.ds(pl.multiple_of(256 * k, 256), 256)
        for f in range(6):
            link = link_ref[f : f + 1, here]
            high = link >> 8
            if f in FIRST:
                high = jnp.where(high < per_source, high, jnp.where(high < 2 * per_source, -1, high - per_source))
                picked, last = look_up(table_ref, f, 2 * per_source, link & 255, high)
                row = 25 * FIRST.index(f)
                added, added_last = first_ref[row : row + 24, lanes], first_ref[row + 24 : row + 25, lanes]
            else:
                picked, last = look_up(table_ref, f, 3 * per_source, link & 255, high)
                added, added_last = faces_ref[24 * f : 24 * f + 24, here], faces_ref[144 + f : 145 + f, here]
            out_ref[25 * f : 25 * f + 24, lanes] = added + picked
            out_ref[25 * f + 24 : 25 * f + 25, lanes] = added_last + last
        return carry

    lax.fori_loop(0, out_ref.shape[1] // 256, columns, 0)


def collect_own(faces, links, chosen, name):
    slots = faces.shape[1]
    tiles = slots // 256
    height = 25 * len(chosen)
    return pl.pallas_call(
        functools.partial(own_kernel, chosen),
        out_shape=jax.ShapeDtypeStruct((height, slots), F32),
        grid=(slots // 1024,),
        in_specs=[whole(links), whole(faces)],
        out_specs=pl.BlockSpec((height, 1024), lambda i: (0, i)),
        scratch_shapes=[pltpu.VMEM((len(chosen), 25 * tiles, 512), BF16), pltpu.VMEM((tiles, 256), F32)],
        compiler_params=pltpu.CompilerParams(vmem_limit_bytes=VMEM),
        cost_estimate=pl.CostEstimate(flops=0, bytes_accessed=1024, transcendentals=0),
        name=name,
    )(links, faces)


def collect_neighbours(first, faces, before, after, links):
    slots = first.shape[1]
    tiles = 3 * slots // 256
    block = pl.BlockSpec((first.shape[0], 1024), lambda i: (0, i))
    return pl.pallas_call(
        neighbour_kernel,
        out_shape=jax.ShapeDtypeStruct((150, slots), F32),
        grid=(slots // 1024,),
        in_specs=[whole(links), whole(before), whole(after), whole(faces), block],
        out_specs=pl.BlockSpec((150, 1024), lambda i: (0, i)),
        scratch_shapes=[
            pltpu.VMEM((6, 25 * tiles, 512), BF16),
            pltpu.VMEM((tiles, 256), F32),
            pltpu.VMEM((150, slots), F32),
            pltpu.VMEM((150, slots), F32),
        ],
        compiler_params=pltpu.CompilerParams(vmem_limit_bytes=VMEM),
        cost_estimate=pl.CostEstimate(flops=10**12, bytes_accessed=10**9, transcendentals=0),
        name="collect_neighbours",
    )(links, before, after, faces, first)


def exchanged(rows, devices, tile):
    blocks = rows.reshape(devices, rows.shape[0] // devices // tile, tile, 128)
    return lax.all_to_all(blocks, ("seg", "rank"), split_axis=0, concat_axis=0, tiled=True).reshape(rows.shape)


def body(parent_nodes, marks, child_owner, face_link):
    devices = lax.axis_size("seg") * lax.axis_size("rank")
    kids = child_owner.shape[0]
    capacity = max(2, 2 * kids // devices)
    slots = devices * capacity
    faces, masses = make_outgoing(parent_nodes.T, marks, child_owner.reshape(kids // 128, 128), devices, capacity)
    arrived = exchanged(faces, devices, 1)
    arrived, masses = lax.optimization_barrier((arrived, masses))
    before = shifted(arrived, "rank", 1)
    after = shifted(arrived, "rank", -1)
    faces = unpack(arrived, slots, FACE_ROWS, FACE_CHUNK, 150, "unpack_faces")
    links = face_link.T
    first = collect_own(faces, links, FIRST, "collect_first")
    masses, first = lax.optimization_barrier((masses, first))
    masses = exchanged(masses, devices, 8)
    first, before, after = lax.optimization_barrier((first, before, after))
    face_mass = collect_neighbours(first, faces, before, after, links)
    masses, face_mass = lax.optimization_barrier((masses, face_mass))
    return (unpack(masses, slots, MASS_ROWS, MASS_ROWS, 125, "unpack_masses"), face_mass)


def solution(mesh):
    return jax.shard_map(
        body,
        mesh=mesh,
        in_specs=(P(("seg", "rank"), None),) * 4,
        out_specs=(P(None, ("seg", "rank")), P(None, ("seg", "rank"))),
        check_vma=False,
    )
```

```python
import functools
import math

import jax
import jax.numpy as jnp
import numpy as np
from jax import lax
from jax.experimental import pallas as pl
from jax.experimental.pallas import tpu as pltpu
from jax.sharding import PartitionSpec as P

F32 = jnp.float32
BF16 = jnp.bfloat16
FIRST, SECOND = (0, 1, 2), (3, 4, 5)
PARTS = 2
VMEM = 60 << 20
GROUPS = 8
FACE_ROWS = 19
FACES = GROUPS * FACE_ROWS
FACE_CHUNK = 19
MASS_ROWS = 16
MASS = GROUPS * MASS_ROWS


def shifted(array, axis, by):
    count = lax.axis_size(axis)
    pairs = [(i, i + by) for i in range(count) if 0 <= i + by < count]
    return lax.ppermute(array, axis, pairs)


def gll_tables():
    points = np.array([-1.0, -math.sqrt(3.0 / 7.0), 0.0, math.sqrt(3.0 / 7.0), 1.0])
    weights = np.array([0.1, 49.0 / 90.0, 32.0 / 45.0, 49.0 / 90.0, 0.1])
    barycentric = np.array(
        [1.0 / np.prod([points[j] - points[m] for m in range(5) if m != j]) for j in range(5)]
    )
    slopes = np.zeros((5, 5))
    for i in range(5):
        for j in range(5):
            if i != j:
                slopes[i, j] = barycentric[j] / barycentric[i] / (points[i] - points[j])
        slopes[i, i] = -np.sum(slopes[i])

    def lagrange_at(where):
        table = np.ones((5, 5))
        for a in range(5):
            for j in range(5):
                for m in range(5):
                    if m != j:
                        table[a, j] *= (where[a] - points[m]) / (points[j] - points[m])
        return table

    def blend(value, side):
        return (1.0 - value) / 2.0 if side == 0 else (1.0 + value) / 2.0

    def flat(i, j, k):
        return i * 25 + j * 5 + k

    ends = (0, 4)
    gordon = np.zeros((125, 125))
    for i in range(5):
        for j in range(5):
            for k in range(5):
                r, s, t = (points[i], points[j], points[k])
                target = flat(i, j, k)
                for a in range(2):
                    gordon[target, flat(ends[a], j, k)] += blend(r, a)
                    gordon[target, flat(i, ends[a], k)] += blend(s, a)
                    gordon[target, flat(i, j, ends[a])] += blend(t, a)
                    for b in range(2):
                        gordon[target, flat(ends[a], ends[b], k)] -= blend(r, a) * blend(s, b)
                        gordon[target, flat(ends[a], j, ends[b])] -= blend(r, a) * blend(t, b)
                        gordon[target, flat(i, ends[a], ends[b])] -= blend(s, a) * blend(t, b)
                        for c in range(2):
                            gordon[target, flat(ends[a], ends[b], ends[c])] += (
                                blend(r, a) * blend(s, b) * blend(t, c)
                            )
    children = np.zeros((8, 125, 125))
    for octant in range(8):
        shifts = [2 * (octant >> 2 & 1) - 1, 2 * (octant >> 1 & 1) - 1, 2 * (octant & 1) - 1]
        tables = [lagrange_at((points + shifts[q]) / 2.0) for q in range(3)]
        children[octant] = np.kron(np.kron(tables[0], tables[1]), tables[2]) @ gordon
    identity = np.eye(5)
    derivs = [
        np.kron(np.kron(slopes, identity), identity),
        np.kron(np.kron(identity, slopes), identity),
        np.kron(np.kron(identity, identity), slopes),
    ]
    deriv_table = np.concatenate([derivs[q].T for q in range(3)], axis=1)
    mass_weights = np.kron(np.kron(weights, weights), weights)
    face_weights = np.kron(weights, weights)
    tangents = [(1, 2), (1, 2), (0, 2), (0, 2), (0, 1), (0, 1)]
    boundary = [
        flat(i, j, k)
        for i in range(5)
        for j in range(5)
        for k in range(5)
        if i in ends or j in ends or k in ends
    ]
    children_map = children.transpose(2, 0, 1).reshape(125, 1000)
    return (children_map, deriv_table, mass_weights, face_weights, tangents, np.array(boundary))


def split(value, parts):
    pieces = []
    for _ in range(parts):
        piece = value.astype(BF16)
        pieces.append(piece)
        value = value - piece.astype(F32)
    return pieces


def flipped(blocks):
    lanes = lax.broadcasted_iota(jnp.int32, blocks[0].shape, 1) // (128 // GROUPS)
    blocks = list(blocks)
    for bit in (1, 2, 4):
        low = (lanes & bit) == 0
        step = bit * (128 // GROUPS)
        for i in range(GROUPS):
            if i & bit == 0:
                a, c = blocks[i], blocks[i | bit]
                blocks[i] = jnp.where(low, a, pltpu.roll(c, step, 1))
                blocks[i | bit] = jnp.where(low, pltpu.roll(a, 128 - step, 1), c)
    return blocks


def face_order():
    return [25 * f + p for f in range(6) for p in range(24)] + [25 * f + 24 for f in range(6)]


def constants():
    children_map, deriv_table, mass_weights, face_weights, tangents, _ = gll_tables()
    child = np.zeros((8, 128, 128))
    child[:, :125, :125] = children_map.reshape(125, 8, 125).transpose(1, 2, 0)
    derivs = deriv_table.reshape(125, 3, 125).transpose(1, 2, 0)
    grid = np.arange(125).reshape(5, 5, 5)
    face_rows = np.zeros((2 * FACES, 128))
    for face in range(6):
        nodes = np.take(grid, 0 if face % 2 == 0 else 4, axis=face // 2).reshape(-1)
        for p in range(25):
            n = 24 * face + p if p < 24 else 144 + face
            face_rows[n, :125] = face_weights[p] * derivs[tangents[face][0]][nodes[p]]
            face_rows[FACES + n, :125] = derivs[tangents[face][1]][nodes[p]]
    mass_rows = np.zeros((3 * MASS, 128))
    for d in range(3):
        weights = mass_weights[:, None] if d == 0 else 1.0
        mass_rows[d * MASS : d * MASS + 125, :125] = weights * derivs[d]
    child = child.reshape(1024, 128)
    return [jnp.asarray(np.concatenate([child, rows]), F32) for rows in (face_rows, mass_rows)]


def face_values(deriv_ref, row, marked):
    u = [deriv_ref[row : row + 8, c * marked : (c + 1) * marked] for c in range(3)]
    v = [deriv_ref[FACES + row : FACES + row + 8, c * marked : (c + 1) * marked] for c in range(3)]
    nx = u[1] * v[2] - u[2] * v[1]
    ny = u[2] * v[0] - u[0] * v[2]
    nz = u[0] * v[1] - u[1] * v[0]
    return jnp.sqrt(nx * nx + ny * ny + nz * nz)


def mass_values(deriv_ref, row, marked):
    j = [
        [deriv_ref[d * MASS + row : d * MASS + row + 8, c * marked : (c + 1) * marked] for d in range(3)]
        for c in range(3)
    ]
    return (
        j[0][0] * (j[1][1] * j[2][2] - j[1][2] * j[2][1])
        - j[0][1] * (j[1][0] * j[2][2] - j[1][2] * j[2][0])
        + j[0][2] * (j[1][0] * j[2][1] - j[1][1] * j[2][0])
    )


def child_kernel(
    values, rows, chunk, capacity, nodes_hbm, marks_hbm, owner_hbm, table_hbm, out_ref,
    nodes_ref, marks_ref, owner_ref, table_ref, sems, pick_ref, x_ref, cc_ref, dd_ref, deriv_a, deriv_b,
    vals_ref, natural_ref, target_ref, *buffers,
):
    elements = nodes_ref.shape[1]
    marked = marks_ref.shape[1]
    kids = 8 * marked
    height = GROUPS * rows
    onehots, ys = buffers[: len(buffers) // 2], buffers[len(buffers) // 2 :]
    columns = onehots[0].shape[1]
    destinations = columns // capacity
    devices = out_ref.shape[0] // chunk * pl.num_programs(0)

    @pl.when(pl.program_id(0) == 0)
    def _():
        copies = [
            pltpu.make_async_copy(source, kept, sems.at[i])
            for i, (source, kept) in enumerate(
                ((owner_hbm, owner_ref), (marks_hbm, marks_ref), (table_hbm, table_ref))
            )
        ]
        chunks = [
            pltpu.make_async_copy(
                nodes_hbm.at[:, pl.ds(at, 512)], nodes_ref.at[:, pl.ds(at, 512)], sems.at[3 + at // 512]
            )
            for at in range(0, elements, 512)
        ]
        for copy in copies[:2] + chunks + copies[2:]:
            copy.start()

        owner_rows = lax.broadcasted_iota(jnp.int32, (devices, 128), 0)
        earlier = lax.broadcasted_iota(jnp.int32, (128, 128), 0) < lax.broadcasted_iota(jnp.int32, (128, 128), 1)
        earlier = jnp.where(earlier, 1.0, 0.0).astype(BF16)
        ones = jnp.ones((128, 128), BF16)
        copies[0].wait()
        seen = jnp.zeros((devices, 128), F32)
        for b in range(kids // 128):
            owner = owner_ref[b : b + 1, :]
            same = owner_rows == owner
            same_b = jnp.where(same, 1.0, 0.0).astype(BF16)
            before = jnp.dot(same_b, earlier, preferred_element_type=F32) + seen
            position = jnp.sum(jnp.where(same, before, 0.0), axis=0, keepdims=True)
            target = owner.astype(F32) * capacity + position
            natural_ref[128 * b : 128 * b + 128, :] = jnp.broadcast_to(target, (128, 128)).T.astype(jnp.int32)
            seen = seen + jnp.dot(same_b, ones, preferred_element_type=F32)
        for o in range(8):
            target_ref[o * marked : (o + 1) * marked, :] = natural_ref[pl.ds(o, marked, stride=8), :]

        pick_ref[...] = jnp.zeros_like(pick_ref)
        copies[1].wait()
        marks = marks_ref[...]

        def pick(k, carry):
            start = pl.multiple_of(k * 256, 256)
            where = lax.broadcasted_iota(jnp.int32, (256, marked), 0) + start
            chosen = jnp.where(where == marks, 1.0, 0.0).astype(BF16)
            for piece in split(nodes_ref[:, pl.ds(start, 256)], 3):
                pick_ref[0:375, :] += jnp.dot(piece, chosen, preferred_element_type=F32)
            return carry

        for k, copy in enumerate(chunks):
            copy.wait()
            lax.fori_loop(2 * k, 2 * k + 2, pick, 0)
        copies[2].wait()
        for c in range(3):
            x = pick_ref[125 * c : 125 * c + 128, :]
            x = x - 0.5 * (x[0:1] + x[124:125])
            a1, a2, a3 = split(x, 3)
            for k, piece in enumerate((a1, a2, a1, a3, a2, a1)):
                x_ref[128 * k : 128 * k + 128, c * marked : (c + 1) * marked] = piece
        c1, c2, c3 = split(table_ref[0:1024, :], 3)
        for k, piece in enumerate((c1, c1, c2, c1, c2, c3)):
            cc_ref[:, 128 * k : 128 * k + 128] = piece
        d1, d2 = split(table_ref[1024:, :], 2)
        for k, piece in enumerate((d1, d1, d2, d2)):
            dd_ref[:, 128 * k : 128 * k + 128] = piece

        def octants(i, carry):
            for e, deriv_ref in enumerate((deriv_a, deriv_b)):
                o = 2 * i + e
                coords = jnp.dot(
                    cc_ref[pl.ds(pl.multiple_of(o * 128, 128), 128), :], x_ref[...], preferred_element_type=F32
                )
                y1, y2 = split(coords - coords[62:63], 2)
                deriv_ref[...] = jnp.dot(
                    dd_ref[...], jnp.concatenate([y1, y2, y1, y2], axis=0), preferred_element_type=F32
                )
                lanes = pl.ds(pl.multiple_of(o * marked, 128), marked)
                for row in range(0, height, 8):
                    v1, v2 = split(values(deriv_ref, row, marked), 2)
                    vals_ref[row : row + 8, lanes] = v1
                    vals_ref[height + row : height + row + 8, lanes] = v2
            return carry

        lax.fori_loop(0, 4, octants, 0)

    numbers = lax.broadcasted_iota(jnp.int32, (128, 128), 1)

    base = pl.program_id(0) * (out_ref.shape[0] // chunk * capacity)
    parts = list(enumerate(zip(onehots, ys)))
    for i, (onehot_ref, y_ref) in parts:
        for at in range(0, kids, 128):
            target = target_ref[at : at + 128, :] - (base + i * columns)
            for tile in range(columns // 128):
                onehot_ref[at : at + 128, 128 * tile : 128 * tile + 128] = jnp.where(
                    target == numbers + 128 * tile, 1.0, 0.0
                ).astype(BF16)
        moved = jnp.dot(vals_ref[...], onehot_ref[...], preferred_element_type=F32)
        y_ref[...] = moved[0:height] + moved[height:]
    for i, (_, y_ref) in parts:
        for tile in range(columns // 128):
            lanes = slice(128 * tile, 128 * tile + 128)
            blocks = flipped([y_ref[rows * g : rows * (g + 1), lanes] for g in range(GROUPS)])
            if chunk > rows:
                blocks = [jnp.concatenate([b, jnp.zeros((chunk - rows, 128), F32)], axis=0) for b in blocks]
            start = (i * destinations + tile * GROUPS) * chunk
            out_ref[start : start + GROUPS * chunk, :] = jnp.concatenate(blocks, axis=0)


def whole(a):
    return pl.BlockSpec(a.shape, lambda i: (0, 0))


def outgoing(values, rows, chunk, table, nodes, marks, owner, devices, capacity, name):
    marked = marks.shape[1]
    kids = 8 * marked
    operands = (nodes, marks, owner, table)
    steps = 4
    height = GROUPS * rows
    return pl.pallas_call(
        functools.partial(child_kernel, values, rows, chunk, capacity),
        out_shape=jax.ShapeDtypeStruct((devices * chunk, 128), F32),
        grid=(steps,),
        in_specs=[pl.BlockSpec(memory_space=pltpu.HBM)] * 4,
        out_specs=pl.BlockSpec((devices * chunk // steps, 128), lambda i: (i, 0)),
        scratch_shapes=[
            *(pltpu.VMEM(a.shape, a.dtype) for a in operands),
            pltpu.SemaphoreType.DMA((3 + nodes.shape[1] // 512,)),
            pltpu.VMEM((384, marked), F32),
            pltpu.VMEM((768, 3 * marked), BF16),
            pltpu.VMEM((1024, 768), BF16),
            pltpu.VMEM((table.shape[0] - 1024, 512), BF16),
            pltpu.VMEM((table.shape[0] - 1024, 3 * marked), F32),
            pltpu.VMEM((table.shape[0] - 1024, 3 * marked), F32),
            pltpu.VMEM((2 * height, kids), BF16),
            pltpu.VMEM((kids, 128), jnp.int32),
            pltpu.VMEM((kids, 128), jnp.int32),
            *(pltpu.VMEM((kids, 1024 // PARTS), BF16) for _ in range(PARTS)),
            *(pltpu.VMEM((height, 1024 // PARTS), F32) for _ in range(PARTS)),
        ],
        compiler_params=pltpu.CompilerParams(vmem_limit_bytes=VMEM),
        name=name,
    )(*operands)


def make_outgoing(nodes, marks, owner, devices, capacity):
    face_table, mass_table = constants()
    args = (nodes, marks, owner, devices, capacity)
    return (
        outgoing(face_values, FACE_ROWS, FACE_CHUNK, face_table, *args, "faces"),
        outgoing(mass_values, MASS_ROWS, MASS_ROWS, mass_table, *args, "masses"),
    )


def unpack_tile(rows, chunk, height, in_ref, out_ref, tile):
    start = pl.multiple_of(tile * (chunk * GROUPS), 8)
    lanes = pl.ds(pl.multiple_of(tile * 128, 128), 128)
    arrived = in_ref[pl.ds(start, chunk * GROUPS), :]
    blocks = flipped([arrived[chunk * j : chunk * j + rows] for j in range(GROUPS)])
    for g in range(GROUPS):
        count = min(rows, height - rows * g)
        out_ref[rows * g : rows * g + count, lanes] = blocks[g][0:count]


def unpack_kernel(rows, chunk, height, in_ref, out_ref):
    def tiles(i, carry):
        for k in range(4):
            unpack_tile(rows, chunk, height, in_ref, out_ref, 4 * i + k)
        return carry

    lax.fori_loop(0, out_ref.shape[1] // 512, tiles, 0)


def unpack(arrived, slots, rows, chunk, height, name):
    return pl.pallas_call(
        functools.partial(unpack_kernel, rows, chunk, height),
        out_shape=jax.ShapeDtypeStruct((height, slots), F32),
        grid=(slots // 1024,),
        in_specs=[pl.BlockSpec((8 * GROUPS * chunk, 128), lambda i: (i, 0))],
        out_specs=pl.BlockSpec((height, 1024), lambda i: (0, i)),
        compiler_params=pltpu.CompilerParams(vmem_limit_bytes=VMEM),
        name=name,
    )(arrived)


def fill_face_table(table_ref, tail_ref, sources, faces):
    per_source = sources[0].shape[1] // 256
    tiles = len(sources) * per_source
    body_rows = 24 * tiles
    for f in faces:
        at = f if table_ref.shape[0] == 6 else faces.index(f)
        other = f + 1 - 2 * (f % 2)
        for k, source in enumerate(sources):

            def pair(i, carry):
                lanes = [pl.ds(pl.multiple_of(512 * i + 256 * e, 256), 256) for e in range(2)]
                values = jnp.concatenate([source[24 * other : 24 * other + 24, l] for l in lanes], axis=0)
                row = pl.multiple_of(24 * per_source * k + 48 * i, 16)
                for part, piece in enumerate(split(values, 2)):
                    table_ref[at, pl.ds(row, 48), 256 * part : 256 * part + 256] = piece
                for e in range(2):
                    tail_ref[pl.ds(per_source * k + 2 * i + e, 1), :] = source[144 + other : 145 + other, lanes[e]]
                return carry

            lax.fori_loop(0, per_source // 2, pair, 0)
        for part, piece in enumerate(split(tail_ref[0:tiles, :], 2)):
            table_ref[at, body_rows : body_rows + tiles, 256 * part : 256 * part + 256] = piece


def look_up(table_ref, at, tiles, low, high):
    chosen = jnp.where(lax.broadcasted_iota(jnp.int32, (256, 256), 0) == low, 1.0, 0.0).astype(BF16)
    found = jnp.dot(table_ref[at, 0 : 25 * tiles], jnp.concatenate([chosen, chosen], axis=0), preferred_element_type=F32)
    high24 = jnp.broadcast_to(high, (24, 256))
    picked = jnp.zeros((24, 256), F32)
    for h in range(tiles):
        picked = jnp.where(high24 == h, found[24 * h : 24 * h + 24], picked)
    last = jnp.where(lax.broadcasted_iota(jnp.int32, (tiles, 256), 0) == high, found[24 * tiles :], 0.0)
    return picked, jnp.sum(last, axis=0, keepdims=True)


def own_kernel(faces, link_ref, faces_ref, out_ref, table_ref, tail_ref):
    per_source = faces_ref.shape[1] // 256

    @pl.when(pl.program_id(0) == 0)
    def _():
        fill_face_table(table_ref, tail_ref, (faces_ref,), faces)

    def columns(k, carry):
        here = pl.ds(pl.multiple_of(pl.program_id(0) * 1024 + 256 * k, 256), 256)
        lanes = pl.ds(pl.multiple_of(256 * k, 256), 256)
        for at, f in enumerate(faces):
            link = link_ref[f : f + 1, here]
            picked, last = look_up(table_ref, at, per_source, link & 255, (link >> 8) - per_source)
            out_ref[25 * at : 25 * at + 24, lanes] = faces_ref[24 * f : 24 * f + 24, here] + picked
            out_ref[25 * at + 24 : 25 * at + 25, lanes] = faces_ref[144 + f : 145 + f, here] + last
        return carry

    lax.fori_loop(0, out_ref.shape[1] // 256, columns, 0)


def neighbour_kernel(link_ref, before_ref, after_ref, faces_ref, first_ref, out_ref, table_ref, tail_ref, unpacked_before, unpacked_after):
    per_source = unpacked_before.shape[1] // 256

    @pl.when(pl.program_id(0) == 0)
    def _():
        def tile(i, carry):
            for k in range(2):
                for packed, unpacked in ((before_ref, unpacked_before), (after_ref, unpacked_after)):
                    unpack_tile(FACE_ROWS, FACE_CHUNK, 150, packed, unpacked, 2 * i + k)
            return carry

        lax.fori_loop(0, unpacked_before.shape[1] // 256, tile, 0)
        fill_face_table(table_ref, tail_ref, (unpacked_before, unpacked_after), FIRST)
        fill_face_table(table_ref, tail_ref, (unpacked_before, faces_ref, unpacked_after), SECOND)

    def columns(k, carry):
        here = pl.ds(pl.multiple_of(pl.program_id(0) * 1024 + 256 * k, 256), 256)
        lanes = pl.ds(pl.multiple_of(256 * k, 256), 256)
        for f in range(6):
            link = link_ref[f : f + 1, here]
            high = link >> 8
            if f in FIRST:
                high = jnp.where(high < per_source, high, jnp.where(high < 2 * per_source, -1, high - per_source))
                picked, last = look_up(table_ref, f, 2 * per_source, link & 255, high)
                row = 25 * FIRST.index(f)
                added, added_last = first_ref[row : row + 24, lanes], first_ref[row + 24 : row + 25, lanes]
            else:
                picked, last = look_up(table_ref, f, 3 * per_source, link & 255, high)
                added, added_last = faces_ref[24 * f : 24 * f + 24, here], faces_ref[144 + f : 145 + f, here]
            out_ref[25 * f : 25 * f + 24, lanes] = added + picked
            out_ref[25 * f + 24 : 25 * f + 25, lanes] = added_last + last
        return carry

    lax.fori_loop(0, out_ref.shape[1] // 256, columns, 0)


def collect_own(faces, links, chosen, name):
    slots = faces.shape[1]
    tiles = slots // 256
    height = 25 * len(chosen)
    return pl.pallas_call(
        functools.partial(own_kernel, chosen),
        out_shape=jax.ShapeDtypeStruct((height, slots), F32),
        grid=(slots // 1024,),
        in_specs=[whole(links), whole(faces)],
        out_specs=pl.BlockSpec((height, 1024), lambda i: (0, i)),
        scratch_shapes=[pltpu.VMEM((len(chosen), 25 * tiles, 512), BF16), pltpu.VMEM((tiles, 256), F32)],
        compiler_params=pltpu.CompilerParams(vmem_limit_bytes=VMEM),
        cost_estimate=pl.CostEstimate(flops=0, bytes_accessed=1024, transcendentals=0),
        name=name,
    )(links, faces)


def collect_neighbours(first, faces, before, after, links):
    slots = first.shape[1]
    tiles = 3 * slots // 256
    block = pl.BlockSpec((first.shape[0], 1024), lambda i: (0, i))
    return pl.pallas_call(
        neighbour_kernel,
        out_shape=jax.ShapeDtypeStruct((150, slots), F32),
        grid=(slots // 1024,),
        in_specs=[whole(links), whole(before), whole(after), whole(faces), block],
        out_specs=pl.BlockSpec((150, 1024), lambda i: (0, i)),
        scratch_shapes=[
            pltpu.VMEM((6, 25 * tiles, 512), BF16),
            pltpu.VMEM((tiles, 256), F32),
            pltpu.VMEM((150, slots), F32),
            pltpu.VMEM((150, slots), F32),
        ],
        compiler_params=pltpu.CompilerParams(vmem_limit_bytes=VMEM),
        cost_estimate=pl.CostEstimate(flops=10**12, bytes_accessed=10**9, transcendentals=0),
        name="collect_neighbours",
    )(links, before, after, faces, first)


def exchanged(rows, devices, tile):
    blocks = rows.reshape(devices, rows.shape[0] // devices // tile, tile, 128)
    return lax.all_to_all(blocks, ("seg", "rank"), split_axis=0, concat_axis=0, tiled=True).reshape(rows.shape)


def body(parent_nodes, marks, child_owner, face_link):
    devices = lax.axis_size("seg") * lax.axis_size("rank")
    kids = child_owner.shape[0]
    capacity = max(2, 2 * kids // devices)
    slots = devices * capacity
    faces, masses = make_outgoing(parent_nodes.T, marks, child_owner.reshape(kids // 128, 128), devices, capacity)
    arrived = exchanged(faces, devices, 1)
    arrived, masses = lax.optimization_barrier((arrived, masses))
    before = shifted(arrived, "rank", 1)
    after = shifted(arrived, "rank", -1)
    faces = unpack(arrived, slots, FACE_ROWS, FACE_CHUNK, 150, "unpack_faces")
    links = face_link.T
    first = collect_own(faces, links, FIRST, "collect_first")
    masses, first = lax.optimization_barrier((masses, first))
    masses = exchanged(masses, devices, 8)
    first, before, after = lax.optimization_barrier((first, before, after))
    face_mass = collect_neighbours(first, faces, before, after, links)
    masses, face_mass = lax.optimization_barrier((masses, face_mass))
    return (unpack(masses, slots, MASS_ROWS, MASS_ROWS, 125, "unpack_masses"), face_mass)


def solution(mesh):
    return jax.shard_map(
        body,
        mesh=mesh,
        in_specs=(P(("seg", "rank"), None),) * 4,
        out_specs=(P(None, ("seg", "rank")), P(None, ("seg", "rank"))),
        check_vma=False,
    )
```
